32 devices in a mesh: batch: 16 (over z, y, x), stream: 2 (over core).
Axes of the slice: x: 2, y: 2, z: 4, core: 2. Of those that a mesh axis runs over, the one named last changes fastest.
Arguments:
- tokens: bfloat16 [128, 198, 768], P(('batch', 'stream')), may hold values from -6 to 6
- prompts: float32 [50, 768], replicated, may hold values from -6 to 6
- keep_mask: int32 [128, 196], P(('batch', 'stream')), may hold values from 0 to 1, as said below
- counts: int32 [128], P(('batch', 'stream')), may hold values from 79 to 196, as said below
- ln1_gain: float32 [768], replicated, may hold values from 0.5 to 1.5
- ln1_bias: float32 [768], replicated, may hold values from -0.6 to 0.6
- w_qkv: bfloat16 [768, 2304], replicated, may hold values from -0.21875 to 0.21875
- q_bias: float32 [768], replicated, may hold values from -0.6 to 0.6
- v_bias: float32 [768], replicated, may hold values from -0.6 to 0.6
- w_out: bfloat16 [768, 768], replicated, may hold values from -2.5 to 2.5
- out_bias: float32 [768], replicated, may hold values from -0.6 to 0.6
- ln2_gain: float32 [768], replicated, may hold values from 0.5 to 1.5
- ln2_bias: float32 [768], replicated, may hold values from -0.6 to 0.6
- w_fc1: bfloat16 [768, 3072], replicated, may hold values from -0.21875 to 0.21875
- fc1_bias: float32 [3072], replicated, may hold values from -0.6 to 0.6
- w_fc2: bfloat16 [3072, 768], replicated, may hold values from -0.109375 to 0.109375
- fc2_bias: float32 [768], replicated, may hold values from -0.6 to 0.6
- cot_seq: bfloat16 [128, 198, 768], P(('batch', 'stream')), may hold values from -6 to 6
- cot_prompt: bfloat16 [128, 50, 768], P(('batch', 'stream')), may hold values from -6 to 6
Outputs:
- layer_out: bfloat16 [128, 198, 768], P(('batch', 'stream'))
- prompt_out: bfloat16 [128, 50, 768], P(('batch', 'stream'))
- input_grad: float32 [128, 198, 768], P(('batch', 'stream'))
- prompt_grad: float32 [50, 768], replicated
- penalty: float32 [], replicated
The draws below stay inside these ranges and needn't reach their ends.
Inputs may be any that keep to these rules, and one draw needn't show every extreme that they name: `keep_mask`: 1 keeps a patch; row i has exactly counts[i] ones. counts[i] is the number of ones in row i of keep_mask.
All inputs are finite; a program needn't handle non-finite values.
Results may differ from the reference program's by a relative error of at most 0.01.
Values sent between devices are 32-bit elements; how exact they have to be, the bound alone decides.
A program may use at most 128 MiB of HBM per device.

```python
import math
import jax
import jax.numpy as jnp
from jax import lax

D = 768
HEADS = 12
HEAD_DIM = 64
FF = 3072
PROMPTS = 50
PATCHES = 196
IMAGES = 128
SEQ = 198


def keep_levels(key):
    base_key = jax.random.fold_in(key, 7)
    position = jnp.arange(IMAGES, dtype=jnp.int32)
    least_kept = (2 * PATCHES + 4) // 5
    spread = PATCHES - least_kept
    rising = least_kept + spread * position // max(IMAGES - 1, 1)
    offset = jax.random.randint(jax.random.fold_in(base_key, 1), (), -(spread // 4), spread // 4 + 1)
    jitter = jax.random.randint(jax.random.fold_in(base_key, 2), (IMAGES,), -(spread // 8), spread // 8 + 1)
    levels = jnp.clip(rising + offset + jitter, least_kept, PATCHES)
    levels = jnp.where(position == 0, least_kept, levels)
    levels = jnp.where(position == IMAGES - 1, PATCHES, levels)
    return levels.astype(jnp.int32)


def draw_counts(key, part):
    return keep_levels(key)


def draw_keep_mask(key, part):
    levels = keep_levels(key)
    order_keys = jax.random.split(jax.random.fold_in(key, 11), IMAGES)
    ranks = jax.vmap(lambda row_key: jax.random.permutation(row_key, PATCHES))(order_keys)
    return (ranks < levels[:, None]).astype(jnp.int32)


def steps_of(key, extent, cuts, smallest, high):
    def one(axis_at, blocks):
        heights = jax.random.uniform(jax.random.fold_in(jax.random.fold_in(key, 6), axis_at), (blocks,), jnp.float32, smallest / len(cuts), high / len(cuts))
        return jnp.repeat(jnp.exp(heights), extent[axis_at] // blocks).reshape((-1,) + (1,) * (len(extent) - axis_at - 1))

    loudness = one(*cuts[0])
    for cut in cuts[1:]:
        loudness = loudness * one(*cut)
    return loudness


def centred(rng, dims, width, reach, cuts=(), kind=jnp.bfloat16):
    entries = width * jax.random.normal(rng, dims, jnp.float32)
    if cuts:
        entries = entries * steps_of(rng, dims, cuts, -0.22, 0.18)
    return jnp.clip(entries, -reach, reach).astype(kind)


def setup_inputs(seed: int = 0) -> dict:
    arg_keys = jax.random.split(jax.random.key(seed), 20)
    tokens = centred(arg_keys[0], (IMAGES, SEQ, D), 1.0, 6.0, ((0, 32),))
    prompts = centred(arg_keys[1], (PROMPTS, D), 1.0, 6.0, (), jnp.float32)
    keep_mask = draw_keep_mask(jax.random.fold_in(arg_keys[19], 71), 0)
    counts = draw_counts(jax.random.fold_in(arg_keys[19], 71), 0)
    ln1_gain = jnp.clip(1.0 + 0.1 * jax.random.normal(arg_keys[4], (D,), jnp.float32), 0.5, 1.5)
    ln1_bias = centred(arg_keys[5], (D,), 0.1, 0.6, (), jnp.float32)
    w_qkv = centred(arg_keys[6], (D, 3 * D), D ** -0.5, 0.21875)
    q_bias = centred(arg_keys[7], (D,), 0.1, 0.6, (), jnp.float32)
    v_bias = centred(arg_keys[8], (D,), 0.1, 0.6, (), jnp.float32)
    w_out = centred(arg_keys[9], (D, D), (max(D // 128, 1)) ** -0.5, 2.5)
    out_bias = centred(arg_keys[10], (D,), 0.1, 0.6, (), jnp.float32)
    ln2_gain = jnp.clip(1.0 + 0.1 * jax.random.normal(arg_keys[11], (D,), jnp.float32), 0.5, 1.5)
    ln2_bias = centred(arg_keys[12], (D,), 0.1, 0.6, (), jnp.float32)
    w_fc1 = centred(arg_keys[13], (D, FF), D ** -0.5, 0.21875)
    fc1_bias = centred(arg_keys[14], (FF,), 0.1, 0.6, (), jnp.float32)
    w_fc2 = centred(arg_keys[15], (FF, D), FF ** -0.5, 0.109375)
    fc2_bias = centred(arg_keys[16], (D,), 0.1, 0.6, (), jnp.float32)
    cot_seq = centred(arg_keys[17], (IMAGES, SEQ, D), 1.0, 6.0, ((0, 32),))
    cot_prompt = centred(arg_keys[18], (IMAGES, PROMPTS, D), 1.0, 6.0, ((0, 32),))
    return {"tokens": tokens, "prompts": prompts, "keep_mask": keep_mask, "counts": counts, "ln1_gain": ln1_gain, "ln1_bias": ln1_bias, "w_qkv": w_qkv, "q_bias": q_bias, "v_bias": v_bias, "w_out": w_out, "out_bias": out_bias, "ln2_gain": ln2_gain, "ln2_bias": ln2_bias, "w_fc1": w_fc1, "fc1_bias": fc1_bias, "w_fc2": w_fc2, "fc2_bias": fc2_bias, "cot_seq": cot_seq, "cot_prompt": cot_prompt}


EPSILON = 1e-06
HIGHEST_PRECISION = lax.Precision.HIGHEST

@jax.custom_vjp
def low(v):
    return lax.optimization_barrier(v.astype(jnp.bfloat16)).astype(jnp.float32)

@jax.custom_vjp
def low_back(v):
    return v

def low_keep(v):
    return (low(v), None)

def low_pass(kept, grad):
    return (grad,)

def back_keep(v):
    return (v, None)

def back_low(kept, grad):
    return (low(grad),)
low.defvjp(low_keep, low_pass)
low_back.defvjp(back_keep, back_low)

def layer_norm(values_in, norm_gain, norm_shift):
    row_mean = lax.optimization_barrier(jnp.mean(values_in, axis=-1, keepdims=True))
    centered = values_in - row_mean
    variance = lax.optimization_barrier(jnp.mean(centered * centered, axis=-1, keepdims=True))
    return centered * lax.rsqrt(variance + EPSILON) * norm_gain + norm_shift

def split_heads(tensor):
    return tensor.reshape(tensor.shape[0], tensor.shape[1], HEADS, HEAD_DIM)

def image_block(inputs, prompts, keep_rows, params):
    ln1_gain, ln1_bias, w_qkv, q_bias, v_bias, w_out, out_bias, ln2_gain, ln2_bias, w_fc1, fc1_bias, w_fc2, fc2_bias = params
    group_size = inputs.shape[0]
    prompt_count = prompts.shape[0]
    model_width = inputs.shape[2]
    full_rows = jnp.concatenate([jnp.broadcast_to(prompts[None], (group_size, prompt_count, model_width)), inputs], axis=1)
    normed = low(layer_norm(full_rows, ln1_gain, ln1_bias))
    projected = jnp.einsum('gld,de->gle', normed, w_qkv, precision=HIGHEST_PRECISION)
    queries = low(low_back(projected[..., :model_width] + q_bias))
    key_all = projected[..., model_width:2 * model_width]
    value_all = projected[..., 2 * model_width:] + v_bias
    key_part = low(jnp.concatenate([key_all[:, :prompt_count], low_back(key_all[:, prompt_count:])], axis=1))
    value_part = low(jnp.concatenate([value_all[:, :prompt_count], low_back(value_all[:, prompt_count:])], axis=1))
    raw_scores = jnp.einsum('gqhd,gkhd->ghqk', split_heads(queries), split_heads(key_part), precision=HIGHEST_PRECISION)
    scores = low_back(raw_scores * HEAD_DIM ** (-0.5))
    live_keys = jnp.concatenate([jnp.ones((group_size, prompt_count), jnp.int32), keep_rows], axis=1) > 0
    masked = jnp.where(live_keys[:, None, None, :], scores, -1e+30)
    soft_low = low(jax.nn.softmax(masked, axis=-1))
    context = jnp.einsum('ghqk,gkhd->gqhd', soft_low, split_heads(value_part), precision=HIGHEST_PRECISION)
    context = low(low_back(context.reshape(group_size, -1, model_width)))
    attention = low_back(jnp.einsum('gld,de->gle', context, w_out, precision=HIGHEST_PRECISION) + out_bias)
    middle = full_rows + attention
    second_norm = low(layer_norm(middle, ln2_gain, ln2_bias))
    hidden = low_back(jnp.einsum('gld,df->glf', second_norm, w_fc1, precision=HIGHEST_PRECISION) + fc1_bias)
    activated = low(jax.nn.gelu(hidden, approximate=False))
    result = middle + jnp.einsum('glf,fd->gld', activated, w_fc2, precision=HIGHEST_PRECISION) + fc2_bias
    prompt_rows = result[:, :prompt_count]
    kept_rows = keep_rows[:, :, None] > 0
    token_rows = jnp.where(kept_rows, result[:, prompt_count:], inputs)
    return (token_rows, prompt_rows)

def forward(tokens_in, prompts, keep_rows, params):
    images = tokens_in.shape[0]
    group_size = math.gcd(images, 16)
    blocks = images // group_size
    block_fn = jax.checkpoint(lambda block_tokens, block_keep: image_block(block_tokens, prompts, block_keep, params))

    def scan_step(carried, block_pair):
        return (carried, block_fn(block_pair[0], block_pair[1]))
    scanned = (tokens_in.reshape(blocks, group_size, tokens_in.shape[1], tokens_in.shape[2]), keep_rows.reshape(blocks, group_size, keep_rows.shape[1]))
    _, (token_rows, prompt_rows) = lax.scan(scan_step, jnp.zeros((), jnp.float32), scanned)
    return (token_rows.reshape(tokens_in.shape), prompt_rows.reshape(images, prompts.shape[0], tokens_in.shape[2]))

def reference(tokens, prompts, keep_mask, counts, ln1_gain, ln1_bias, w_qkv, q_bias, v_bias, w_out, out_bias, ln2_gain, ln2_bias, w_fc1, fc1_bias, w_fc2, fc2_bias, cot_seq, cot_prompt):
    params = tuple((member.astype(jnp.float32) for member in (ln1_gain, ln1_bias, w_qkv, q_bias, v_bias, w_out, out_bias, ln2_gain, ln2_bias, w_fc1, fc1_bias, w_fc2, fc2_bias)))
    tokens_in = tokens.astype(jnp.float32)
    prompts_in = prompts.astype(jnp.float32)
    keep_rows = jnp.concatenate([jnp.ones((tokens.shape[0], SEQ - PATCHES), jnp.int32), keep_mask.astype(jnp.int32)], axis=1)
    penalty_weight = jnp.sum(counts.astype(jnp.float32)) / (PATCHES * math.sqrt(IMAGES))

    def objective(token_arg, prompt_arg):
        token_rows, prompt_rows = forward(token_arg, prompt_arg, keep_rows, params)
        return (token_rows, prompt_rows, penalty_weight * jnp.sum(prompt_arg * prompt_arg))
    (token_rows, prompt_rows, regular), pullback = jax.vjp(objective, tokens_in, prompts_in)
    input_grad, prompt_grad = pullback((cot_seq.astype(jnp.float32), cot_prompt.astype(jnp.float32), jnp.ones((), jnp.float32)))
    penalty = regular / (PROMPTS * D)
    return (token_rows.astype(jnp.bfloat16), prompt_rows.astype(jnp.bfloat16), input_grad, prompt_grad, penalty)
```

```python
import functools
import math

import jax
import jax.numpy as jnp
from jax import lax
from jax.experimental import pallas as pl
from jax.experimental.pallas import tpu as pltpu
from jax.sharding import PartitionSpec as P

HEADS = 12
EPSILON = 1e-06
F32 = jnp.float32
BF16 = jnp.bfloat16
MESH = pl.DeviceIdType.MESH
DEAD = -1e30

NN = (((1,), (0,)), ((), ()))
NT = (((1,), (1,)), ((), ()))


def dot(a, b, dims=NN):
    return lax.dot_general(a, b, dims, preferred_element_type=F32)


def round_up(value, step):
    return -(-value // step) * step


def norm_stats(rows_in):
    mean = jnp.mean(rows_in, axis=-1, keepdims=True)
    centered = rows_in - mean
    variance = jnp.mean(centered * centered, axis=-1, keepdims=True)
    scale = lax.rsqrt(variance + EPSILON)
    return centered * scale, scale


def norm_back(grad, gain, unit, scale):
    scaled = grad * gain
    mean = jnp.mean(scaled, axis=-1, keepdims=True)
    along = jnp.mean(scaled * unit, axis=-1, keepdims=True)
    return scale * (scaled - mean - unit * along)


def layer_kernel(
    tokens_ref,
    prompts_ref,
    keep_ref,
    counts_ref,
    ln1_gain_ref,
    ln1_bias_ref,
    q_bias_ref,
    v_bias_ref,
    out_bias_ref,
    ln2_gain_ref,
    ln2_bias_ref,
    fc1_bias_ref,
    fc2_bias_ref,
    cot_seq_ref,
    cot_prompt_ref,
    w_qkv_hbm,
    w_out_hbm,
    w_fc1_hbm,
    w_fc2_hbm,
    layer_out_ref,
    prompt_out_ref,
    input_grad_ref,
    prompt_local_ref,
    w_qkv,
    w_out,
    w_fc1,
    w_fc2,
    rows_s,
    cot_s,
    normed_s,
    q_s,
    k_s,
    v_s,
    kt_s,
    vt_s,
    qm_s,
    gm_s,
    soft_s,
    ctx_s,
    act_s,
    gh_s,
    mid_s,
    gmid_s,
    dqkv_s,
    sum_s,
    gmid_sum_s,
    sems,
):
    image = pl.program_id(0)
    images = pl.num_programs(0)
    seq, width = tokens_ref.shape[1], tokens_ref.shape[2]
    prompt_count = prompts_ref.shape[0]
    patches = keep_ref.shape[1]
    lead = seq - patches
    head_dim = width // HEADS
    hidden = w_fc1.shape[1]
    total = rows_s.shape[0]
    first = round_up(seq, 8)
    score_scale = head_dim ** (-0.5)
    step_rows = 64

    copies = [
        pltpu.make_async_copy(src, dst, sems.at[at])
        for at, (src, dst) in enumerate(
            ((w_qkv_hbm, w_qkv), (w_out_hbm, w_out), (w_fc1_hbm, w_fc1), (w_fc2_hbm, w_fc2))
        )
    ]

    @pl.when(image == 0)
    def _():
        for copy in copies:
            copy.start()
        rows_s[...] = jnp.zeros_like(rows_s)
        cot_s[...] = jnp.zeros_like(cot_s)
        sum_s[...] = jnp.zeros_like(sum_s)
        gmid_sum_s[...] = jnp.zeros_like(gmid_sum_s)
        rows_s[first : first + prompt_count, :] = prompts_ref[...]

    at_row = lax.broadcasted_iota(jnp.int32, (total, patches), 0)
    at_col = lax.broadcasted_iota(jnp.int32, (total, patches), 1)
    keep_row = keep_ref[pl.ds(image, 1), :].astype(F32)
    patch_kept = jnp.sum(
        jnp.where(at_row == at_col + lead, keep_row, 0.0), axis=1, keepdims=True
    )
    row_at = lax.broadcasted_iota(jnp.int32, (total, 1), 0)
    is_prompt = (row_at >= first) & (row_at < first + prompt_count)
    live = (row_at < lead) | is_prompt | (patch_kept > 0.0)
    dead_add = jnp.where(live, 0.0, DEAD)
    token_kept = live[:seq]

    rows_s[:seq, :] = tokens_ref[0].astype(F32)
    cot_s[:seq, :] = jnp.where(token_kept, cot_seq_ref[0].astype(F32), 0.0)
    cot_s[first : first + prompt_count, :] = cot_prompt_ref[0].astype(F32)

    gain1 = ln1_gain_ref[...]
    bias1 = ln1_bias_ref[...]
    for at in range(0, total, step_rows):
        unit, _ = norm_stats(rows_s[at : at + step_rows, :])
        normed_s[at : at + step_rows, :] = (unit * gain1 + bias1).astype(BF16)

    @pl.when(image == 0)
    def _():
        copies[0].wait()

    normed = normed_s[...]
    q_s[...] = (
        (dot(normed, w_qkv[:, :width]) + q_bias_ref[...]).astype(BF16) * jnp.asarray(score_scale, BF16)
    )
    k_s[...] = dot(normed, w_qkv[:, width : 2 * width]).astype(BF16)
    v_s[...] = (dot(normed, w_qkv[:, 2 * width :]) + v_bias_ref[...]).astype(BF16)
    kt_s[...] = k_s[...].T
    vt_s[...] = v_s[...].T

    lane = lax.broadcasted_iota(jnp.int32, (total, 2 * head_dim), 1)
    low_half = lane < head_dim
    for pair in range(HEADS // 2):
        cols = slice(pair * 2 * head_dim, (pair + 1) * 2 * head_dim)
        q_pair = q_s[:, cols]
        for half in range(2):
            head = 2 * pair + half
            picked = low_half if half == 0 else ~low_half
            qm = jnp.where(picked, q_pair, jnp.zeros_like(q_pair))
            qm_s[head] = qm
            scores = dot(k_s[:, cols], qm, NT) + dead_add
            top = jnp.max(scores, axis=0, keepdims=True)
            weight = jnp.exp(scores - top)
            soft = weight * (1.0 / jnp.sum(weight, axis=0, keepdims=True))
            soft_low = soft.astype(BF16)
            soft_s[head] = soft_low
            ctx_s[head * head_dim : (head + 1) * head_dim, :] = dot(
                vt_s[head * head_dim : (head + 1) * head_dim, :], soft_low
            ).astype(BF16)

    @pl.when(image == 0)
    def _():
        copies[1].wait()

    context = ctx_s[...].T
    mid_s[...] = dot(context, w_out[...]) + out_bias_ref[...] + rows_s[...]
    gain2 = ln2_gain_ref[...]
    bias2 = ln2_bias_ref[...]
    for at in range(0, total, step_rows):
        unit, _ = norm_stats(mid_s[at : at + step_rows, :])
        normed_s[at : at + step_rows, :] = (unit * gain2 + bias2).astype(BF16)

    @pl.when(image == 0)
    def _():
        copies[2].wait()
        copies[3].wait()

    second = normed_s[...]
    grad_result = cot_s[...].astype(BF16)
    chunk = 2 * 128
    for at in range(0, hidden, chunk):
        cols = slice(at, at + chunk)
        pre = dot(second, w_fc1[:, cols]) + fc1_bias_ref[:, cols]
        share = 0.5 + 0.5 * lax.erf(pre * (0.5**0.5))
        density = jnp.exp(pre * pre * -0.5) * ((2.0 * math.pi) ** -0.5)
        act_s[:, cols] = (pre * share).astype(BF16)
        grad_act = dot(grad_result, w_fc2[cols, :], NT)
        gh_s[:, cols] = (grad_act * (share + pre * density)).astype(BF16)

    result = dot(act_s[...], w_fc2[...]) + fc2_bias_ref[...] + mid_s[...]
    layer_out_ref[0] = jnp.where(token_kept, result[:seq], rows_s[:seq, :]).astype(BF16)
    prompt_out_ref[0] = result[first : first + prompt_count].astype(BF16)

    gmid_s[...] = dot(gh_s[...], w_fc1[...], NT)
    for at in range(0, total, step_rows):
        part = slice(at, at + step_rows)
        unit, scale = norm_stats(mid_s[part, :])
        gmid = cot_s[part, :] + norm_back(gmid_s[part, :], gain2, unit, scale)
        gmid_s[part, :] = gmid
        normed_s[part, :] = gmid.astype(BF16)
    gctx = dot(normed_s[...], w_out[...], NT).astype(BF16)

    for pair in range(HEADS // 2):
        cols = slice(pair * 2 * head_dim, (pair + 1) * 2 * head_dim)
        key_grad = None
        value_grad = None
        for half in range(2):
            head = 2 * pair + half
            picked = low_half if half == 0 else ~low_half
            gctx_pair = gctx[:, cols]
            gm = jnp.where(picked, gctx_pair, jnp.zeros_like(gctx_pair))
            soft_low = soft_s[head]
            soft = soft_low.astype(F32)
            grad_soft = soft * dot(v_s[:, cols], gm, NT)
            row_dot = jnp.sum(grad_soft, axis=0, keepdims=True)
            grad_scores = (grad_soft - soft * row_dot).astype(BF16)
            gv = dot(soft_low, gm)
            gk = dot(grad_scores, qm_s[head])
            value_grad = gv if half == 0 else value_grad + gv
            key_grad = gk if half == 0 else key_grad + gk
            ctx_s[head * head_dim : (head + 1) * head_dim, :] = (
                dot(kt_s[head * head_dim : (head + 1) * head_dim, :], grad_scores) * score_scale
            ).astype(BF16)
        kcols = slice(width + cols.start, width + cols.stop)
        vcols = slice(2 * width + cols.start, 2 * width + cols.stop)
        dqkv_s[:, kcols] = key_grad.astype(BF16)
        dqkv_s[:, vcols] = value_grad.astype(BF16)
        sum_s[:, kcols] += key_grad[first:]
        sum_s[:, vcols] += value_grad[first:]
    dqkv_s[:, :width] = ctx_s[...].T
    sum_s[:, :width] += dqkv_s[first:, :width].astype(F32)
    gmid_sum_s[...] += gmid_s[first:, :]

    mid_s[...] = dot(dqkv_s[...], w_qkv[...], NT)
    for at in range(0, total, step_rows):
        part = slice(at, at + step_rows)
        unit, scale = norm_stats(rows_s[part, :])
        mid_s[part, :] = gmid_s[part, :] + norm_back(mid_s[part, :], gain1, unit, scale)
    input_grad_ref[0] = jnp.where(token_kept, mid_s[:seq, :], cot_seq_ref[0].astype(F32))

    @pl.when(image == images - 1)
    def _():
        pairs = sum_s[...]
        high = pairs.astype(BF16)
        rest = pairs - high.astype(F32)
        middle = rest.astype(BF16)
        low = (rest - middle.astype(F32)).astype(BF16)
        grad = dot(high, w_qkv[...], NT) + (
            dot(middle, w_qkv[...], NT) + dot(low, w_qkv[...], NT)
        )
        unit, scale = norm_stats(rows_s[first:, :])
        local = gmid_sum_s[...] + norm_back(grad, gain1, unit, scale)
        kept = jnp.sum(counts_ref[...].astype(F32))
        at_row = lax.broadcasted_iota(jnp.int32, local.shape, 0)
        prompt_local_ref[...] = jnp.where(at_row < prompt_count, local, kept)


def run_layer(
    tokens,
    prompts,
    keep_mask,
    counts,
    ln1_gain,
    ln1_bias,
    w_qkv,
    q_bias,
    v_bias,
    w_out,
    out_bias,
    ln2_gain,
    ln2_bias,
    w_fc1,
    fc1_bias,
    w_fc2,
    fc2_bias,
    cot_seq,
    cot_prompt,
):
    images, seq, width = tokens.shape
    prompt_count = prompts.shape[0]
    hidden = w_fc1.shape[1]
    first = round_up(seq, 8)
    total = round_up(first + prompt_count, 128)
    tail = total - first
    head_dim = width // HEADS
    row = lambda vector: vector.reshape(1, -1)
    whole = pl.BlockSpec(memory_space=pltpu.VMEM)
    anywhere = pl.BlockSpec(memory_space=pl.ANY)
    per_image = lambda shape: pl.BlockSpec((1,) + shape, lambda i: (i, 0, 0))
    return pl.pallas_call(
        layer_kernel,
        grid=(images,),
        out_shape=(
            jax.ShapeDtypeStruct((images, seq, width), BF16),
            jax.ShapeDtypeStruct((images, prompt_count, width), BF16),
            jax.ShapeDtypeStruct((images, seq, width), F32),
            jax.ShapeDtypeStruct((tail, width), F32),
        ),
        in_specs=[per_image((seq, width))]
        + [whole] * 12
        + [per_image((seq, width)), per_image((prompt_count, width))]
        + [anywhere] * 4,
        out_specs=(
            per_image((seq, width)),
            per_image((prompt_count, width)),
            per_image((seq, width)),
            whole,
        ),
        scratch_shapes=[
            pltpu.VMEM(w_qkv.shape, BF16),
            pltpu.VMEM(w_out.shape, BF16),
            pltpu.VMEM(w_fc1.shape, BF16),
            pltpu.VMEM(w_fc2.shape, BF16),
            pltpu.VMEM((total, width), F32),
            pltpu.VMEM((total, width), F32),
            pltpu.VMEM((total, width), BF16),
            pltpu.VMEM((total, width), BF16),
            pltpu.VMEM((total, width), BF16),
            pltpu.VMEM((total, width), BF16),
            pltpu.VMEM((width, total), BF16),
            pltpu.VMEM((width, total), BF16),
            pltpu.VMEM((HEADS, total, 2 * head_dim), BF16),
            pltpu.VMEM((HEADS, total, 2 * head_dim), BF16),
            pltpu.VMEM((HEADS, total, total), BF16),
            pltpu.VMEM((width, total), BF16),
            pltpu.VMEM((total, hidden), BF16),
            pltpu.VMEM((total, hidden), BF16),
            pltpu.VMEM((total, width), F32),
            pltpu.VMEM((total, width), F32),
            pltpu.VMEM((total, 3 * width), BF16),
            pltpu.VMEM((tail, 3 * width), F32),
            pltpu.VMEM((tail, width), F32),
            pltpu.SemaphoreType.DMA((4,)),
        ],
        compiler_params=pltpu.CompilerParams(vmem_limit_bytes=62 << 20),
    )(
        tokens,
        prompts,
        keep_mask,
        row(counts),
        row(ln1_gain),
        row(ln1_bias),
        row(q_bias),
        row(v_bias),
        row(out_bias),
        row(ln2_gain),
        row(ln2_bias),
        row(fc1_bias),
        row(fc2_bias),
        cot_seq,
        cot_prompt,
        w_qkv,
        w_out,
        w_fc1,
        w_fc2,
    )


def sum_kernel(
    plane, line, streams, local_ref, total_ref, sums, came, line_sums, done, send_sems, recv_sems
):
    group = plane * streams
    batch = lax.axis_index("batch")
    stream = lax.axis_index("stream")
    level = batch // plane
    spot = lax.rem(batch, plane) * streams + stream
    share = came.shape[1]
    filled = local_ref.shape[0]

    def in_plane(other):
        return (level * plane + other // streams, lax.rem(other, streams))

    def in_line(other):
        return (other * plane + lax.rem(batch, plane), stream)

    plane_peers = [lax.rem(spot + step, group) for step in range(1, group)]
    line_peers = [lax.rem(level + step, line) for step in range(1, line)]

    barrier = pltpu.get_barrier_semaphore()
    for other in plane_peers:
        pl.semaphore_signal(barrier, inc=1, device_id=in_plane(other), device_id_type=MESH)
    for other in line_peers:
        pl.semaphore_signal(barrier, inc=1, device_id=in_line(other), device_id_type=MESH)

    for at in range(group):
        low = min(at * share, filled)
        high = min((at + 1) * share, filled)
        if high > low:
            sums[at, : high - low, :] = local_ref[low:high, :]
        if high - low < share:
            sums[at, high - low :, :] = jnp.zeros((share - (high - low), sums.shape[2]), F32)
    pl.semaphore_wait(barrier, len(plane_peers) + len(line_peers))

    first_copies = []
    for step, other in enumerate(plane_peers):
        copy = pltpu.make_async_remote_copy(
            src_ref=sums.at[other],
            dst_ref=came.at[spot],
            send_sem=send_sems.at[0, step],
            recv_sem=recv_sems.at[0, spot],
            device_id=in_plane(other),
            device_id_type=MESH,
        )
        copy.start()
        first_copies.append(copy)
    came[spot] = sums[spot]
    for other in plane_peers:
        pltpu.make_async_remote_copy(
            src_ref=sums.at[other],
            dst_ref=came.at[other],
            send_sem=send_sems.at[0, 0],
            recv_sem=recv_sems.at[0, other],
            device_id=in_plane(other),
            device_id_type=MESH,
        ).wait_recv()
    part = came[0]
    for at in range(1, group):
        part = part + came[at]
    line_sums[level] = part

    second_copies = []
    for step, other in enumerate(line_peers):
        copy = pltpu.make_async_remote_copy(
            src_ref=line_sums.at[level],
            dst_ref=line_sums.at[level],
            send_sem=send_sems.at[1, step],
            recv_sem=recv_sems.at[1, level],
            device_id=in_line(other),
            device_id_type=MESH,
        )
        copy.start()
        second_copies.append(copy)
    for other in line_peers:
        pltpu.make_async_remote_copy(
            src_ref=line_sums.at[level],
            dst_ref=line_sums.at[other],
            send_sem=send_sems.at[1, 0],
            recv_sem=recv_sems.at[1, other],
            device_id=in_line(other),
            device_id_type=MESH,
        ).wait_recv()
    whole = line_sums[0]
    for at in range(1, line):
        whole = whole + line_sums[at]
    done[spot] = whole

    third_copies = []
    for step, other in enumerate(plane_peers):
        copy = pltpu.make_async_remote_copy(
            src_ref=done.at[spot],
            dst_ref=done.at[spot],
            send_sem=send_sems.at[2, step],
            recv_sem=recv_sems.at[2, spot],
            device_id=in_plane(other),
            device_id_type=MESH,
        )
        copy.start()
        third_copies.append(copy)
    for other in plane_peers:
        pltpu.make_async_remote_copy(
            src_ref=done.at[spot],
            dst_ref=done.at[other],
            send_sem=send_sems.at[2, 0],
            recv_sem=recv_sems.at[2, other],
            device_id=in_plane(other),
            device_id_type=MESH,
        ).wait_recv()
    for at in range(group):
        low = min(at * share, filled)
        high = min((at + 1) * share, filled)
        if high > low:
            total_ref[low:high, :] = done[at, : high - low, :]
    for copy in first_copies + second_copies + third_copies:
        copy.wait_send()


def sum_over_devices(local):
    devices = lax.axis_size("batch")
    streams = lax.axis_size("stream")
    plane = 2 ** math.ceil(math.log2(devices) / 2)
    line = devices // plane
    group = plane * streams
    filled, width = local.shape
    share = -(-filled // group)
    if share > 4:
        share = round_up(share, 8)
    whole = pl.BlockSpec(memory_space=pltpu.VMEM)
    return pl.pallas_call(
        functools.partial(sum_kernel, plane, line, streams),
        out_shape=jax.ShapeDtypeStruct((filled, width), F32),
        in_specs=[whole],
        out_specs=whole,
        scratch_shapes=[
            pltpu.VMEM((group, share, width), F32),
            pltpu.VMEM((group, share, width), F32),
            pltpu.VMEM((line, share, width), F32),
            pltpu.VMEM((group, share, width), F32),
            pltpu.SemaphoreType.DMA((3, max(group, line))),
            pltpu.SemaphoreType.DMA((3, max(group, line))),
        ],
        compiler_params=pltpu.CompilerParams(collective_id=0, has_side_effects=True),
    )(local)


def body(
    tokens,
    prompts,
    keep_mask,
    counts,
    ln1_gain,
    ln1_bias,
    w_qkv,
    q_bias,
    v_bias,
    w_out,
    out_bias,
    ln2_gain,
    ln2_bias,
    w_fc1,
    fc1_bias,
    w_fc2,
    fc2_bias,
    cot_seq,
    cot_prompt,
):
    images = tokens.shape[0]
    prompt_count, width = prompts.shape
    total_images = images * lax.axis_size("batch") * lax.axis_size("stream")
    layer_out, prompt_out, input_grad, prompt_local = run_layer(
        tokens,
        prompts,
        keep_mask,
        counts,
        ln1_gain,
        ln1_bias,
        w_qkv,
        q_bias,
        v_bias,
        w_out,
        out_bias,
        ln2_gain,
        ln2_bias,
        w_fc1,
        fc1_bias,
        w_fc2,
        fc2_bias,
        cot_seq,
        cot_prompt,
    )
    summed = sum_over_devices(prompt_local)
    penalty_weight = summed[prompt_count, 0] / (keep_mask.shape[1] * math.sqrt(total_images))
    prompt_grad = summed[:prompt_count] + 2.0 * penalty_weight * prompts
    penalty = penalty_weight * jnp.sum(prompts * prompts) / (prompt_count * width)
    return (layer_out, prompt_out, input_grad, prompt_grad, penalty)


def solution(mesh):
    rows = P(("batch", "stream"), None, None)
    in_specs = (
        (rows, P(), P(("batch", "stream"), None), P(("batch", "stream")))
        + (P(),) * 13
        + (rows, rows)
    )
    return jax.shard_map(
        body,
        mesh=mesh,
        in_specs=in_specs,
        out_specs=(rows, rows, rows, P(), P()),
        check_vma=False,
    )
```

```python
import functools
import math

import jax
import jax.numpy as jnp
from jax import lax
from jax.experimental import pallas as pl
from jax.experimental.pallas import tpu as pltpu
from jax.sharding import PartitionSpec as P

HEADS = 12
EPSILON = 1e-06
F32 = jnp.float32
BF16 = jnp.bfloat16
MESH = pl.DeviceIdType.MESH
DEAD = -1e30

NN = (((1,), (0,)), ((), ()))
NT = (((1,), (1,)), ((), ()))


def dot(a, b, dims=NN):
    return lax.dot_general(a, b, dims, preferred_element_type=F32)


def round_up(value, step):
    return -(-value // step) * step


def norm_stats(rows_in):
    mean = jnp.mean(rows_in, axis=-1, keepdims=True)
    centered = rows_in - mean
    variance = jnp.mean(centered * centered, axis=-1, keepdims=True)
    scale = lax.rsqrt(variance + EPSILON)
    return centered * scale, scale


def norm_back(grad, gain, unit, scale):
    scaled = grad * gain
    mean = jnp.mean(scaled, axis=-1, keepdims=True)
    along = jnp.mean(scaled * unit, axis=-1, keepdims=True)
    return scale * (scaled - mean - unit * along)


def layer_kernel(
    prompts_ref,
    keep_ref,
    counts_ref,
    ln1_gain_ref,
    ln1_bias_ref,
    q_bias_ref,
    v_bias_ref,
    out_bias_ref,
    ln2_gain_ref,
    ln2_bias_ref,
    fc1_bias_ref,
    fc2_bias_ref,
    tokens_hbm,
    cot_seq_hbm,
    cot_prompt_hbm,
    w_qkv_hbm,
    w_out_hbm,
    w_fc1_hbm,
    w_fc2_hbm,
    layer_out_ref,
    prompt_out_ref,
    input_grad_ref,
    prompt_local_ref,
    w_qkv,
    w_out,
    w_fc1,
    w_fc2,
    tokens_in,
    cot_seq_in,
    cot_prompt_in,
    tokens_s,
    cot_seq_s,
    cot_prompt_s,
    layer_s,
    prompt_s,
    rows_s,
    cot_s,
    normed_s,
    q_s,
    k_s,
    v_s,
    kt_s,
    vt_s,
    qm_s,
    gm_s,
    soft_s,
    ctx_s,
    act_s,
    gh_s,
    mid_s,
    gmid_s,
    dqkv_s,
    sum_s,
    gmid_sum_s,
    sems,
):
    image = pl.program_id(0)
    images = pl.num_programs(0)
    seq, width = tokens_s.shape[0], tokens_s.shape[2]
    prompt_count = prompts_ref.shape[0]
    patches = keep_ref.shape[1]
    lead = seq - patches
    head_dim = width // HEADS
    hidden = w_fc1.shape[1]
    total = rows_s.shape[0]
    first = round_up(seq, 8)
    score_scale = head_dim ** (-0.5)
    step_rows = 64

    copies = [
        pltpu.make_async_copy(src, dst, sems.at[at])
        for at, (src, dst) in enumerate(
            (
                (tokens_hbm, tokens_in),
                (w_qkv_hbm, w_qkv),
                (cot_seq_hbm, cot_seq_in),
                (cot_prompt_hbm, cot_prompt_in),
                (w_out_hbm, w_out),
                (w_fc1_hbm, w_fc1),
                (w_fc2_hbm, w_fc2),
            )
        )
    ]

    @pl.when(image == 0)
    def _():
        for copy in copies:
            copy.start()
        rows_s[...] = jnp.zeros_like(rows_s)
        cot_s[...] = jnp.zeros_like(cot_s)
        sum_s[...] = jnp.zeros_like(sum_s)
        gmid_sum_s[...] = jnp.zeros_like(gmid_sum_s)
        rows_s[first : first + prompt_count, :] = prompts_ref[...]
        copies[0].wait()
        tokens_s[...] = tokens_in[...].astype(F32)

    at_row = lax.broadcasted_iota(jnp.int32, (total, patches), 0)
    at_col = lax.broadcasted_iota(jnp.int32, (total, patches), 1)
    keep_row = keep_ref[pl.ds(image, 1), :].astype(F32)
    patch_kept = jnp.sum(
        jnp.where(at_row == at_col + lead, keep_row, 0.0), axis=1, keepdims=True
    )
    row_at = lax.broadcasted_iota(jnp.int32, (total, 1), 0)
    is_prompt = (row_at >= first) & (row_at < first + prompt_count)
    live = (row_at < lead) | is_prompt | (patch_kept > 0.0)
    dead_add = jnp.where(live, 0.0, DEAD)
    token_kept = live[:seq]

    rows_s[:seq, :] = tokens_s[:, image, :]

    gain1 = ln1_gain_ref[...][None, :]
    bias1 = ln1_bias_ref[...][None, :]
    for at in range(0, total, step_rows):
        unit, _ = norm_stats(rows_s[at : at + step_rows, :])
        normed_s[at : at + step_rows, :] = (unit * gain1 + bias1).astype(BF16)

    @pl.when(image == 0)
    def _():
        copies[1].wait()

    normed = normed_s[...]
    q_s[...] = (
        (dot(normed, w_qkv[:, :width]) + q_bias_ref[...][None, :]).astype(BF16) * jnp.asarray(score_scale, BF16)
    )
    k_s[...] = dot(normed, w_qkv[:, width : 2 * width]).astype(BF16)
    v_s[...] = (dot(normed, w_qkv[:, 2 * width :]) + v_bias_ref[...][None, :]).astype(BF16)
    kt_s[...] = k_s[...].T
    vt_s[...] = v_s[...].T

    lane = lax.broadcasted_iota(jnp.int32, (total, 2 * head_dim), 1)
    low_half = lane < head_dim
    for pair in range(HEADS // 2):
        cols = slice(pair * 2 * head_dim, (pair + 1) * 2 * head_dim)
        q_pair = q_s[:, cols]
        for half in range(2):
            head = 2 * pair + half
            picked = low_half if half == 0 else ~low_half
            qm = jnp.where(picked, q_pair, jnp.zeros_like(q_pair))
            qm_s[head] = qm
            scores = dot(k_s[:, cols], qm, NT) + dead_add
            top = jnp.max(scores, axis=0, keepdims=True)
            weight = jnp.exp(scores - top)
            soft = weight * (1.0 / jnp.sum(weight, axis=0, keepdims=True))
            soft_low = soft.astype(BF16)
            soft_s[head] = soft_low
            ctx_s[head * head_dim : (head + 1) * head_dim, :] = dot(
                vt_s[head * head_dim : (head + 1) * head_dim, :], soft_low
            ).astype(BF16)

    @pl.when(image == 0)
    def _():
        for copy in copies[2:]:
            copy.wait()
        cot_seq_s[...] = cot_seq_in[...].astype(F32)
        cot_prompt_s[...] = cot_prompt_in[...].astype(F32)

    cot_s[:seq, :] = jnp.where(token_kept, cot_seq_s[:, image, :], 0.0)
    cot_s[first : first + prompt_count, :] = cot_prompt_s[:, image, :]
    context = ctx_s[...].T
    mid_s[...] = dot(context, w_out[...]) + out_bias_ref[...][None, :] + rows_s[...]
    gain2 = ln2_gain_ref[...][None, :]
    bias2 = ln2_bias_ref[...][None, :]
    for at in range(0, total, step_rows):
        unit, _ = norm_stats(mid_s[at : at + step_rows, :])
        normed_s[at : at + step_rows, :] = (unit * gain2 + bias2).astype(BF16)

    second = normed_s[...]
    grad_result = cot_s[...].astype(BF16)
    chunk = 2 * 128
    for at in range(0, hidden, chunk):
        cols = slice(at, at + chunk)
        pre = dot(second, w_fc1[:, cols]) + fc1_bias_ref[cols][None, :]
        share = 0.5 + 0.5 * lax.erf(pre * (0.5**0.5))
        density = jnp.exp(pre * pre * -0.5) * ((2.0 * math.pi) ** -0.5)
        act_s[:, cols] = (pre * share).astype(BF16)
        grad_act = dot(grad_result, w_fc2[cols, :], NT)
        gh_s[:, cols] = (grad_act * (share + pre * density)).astype(BF16)

    result = dot(act_s[...], w_fc2[...]) + fc2_bias_ref[...][None, :] + mid_s[...]
    layer_s[:, image, :] = jnp.where(token_kept, result[:seq], rows_s[:seq, :])
    prompt_s[:, image, :] = result[first : first + prompt_count]

    gmid_s[...] = dot(gh_s[...], w_fc1[...], NT)
    for at in range(0, total, step_rows):
        part = slice(at, at + step_rows)
        unit, scale = norm_stats(mid_s[part, :])
        gmid = cot_s[part, :] + norm_back(gmid_s[part, :], gain2, unit, scale)
        gmid_s[part, :] = gmid
        normed_s[part, :] = gmid.astype(BF16)
    gctx = dot(normed_s[...], w_out[...], NT).astype(BF16)

    for pair in range(HEADS // 2):
        cols = slice(pair * 2 * head_dim, (pair + 1) * 2 * head_dim)
        key_grad = None
        value_grad = None
        for half in range(2):
            head = 2 * pair + half
            picked = low_half if half == 0 else ~low_half
            gctx_pair = gctx[:, cols]
            gm = jnp.where(picked, gctx_pair, jnp.zeros_like(gctx_pair))
            soft_low = soft_s[head]
            soft = soft_low.astype(F32)
            grad_soft = soft * dot(v_s[:, cols], gm, NT)
            row_dot = jnp.sum(grad_soft, axis=0, keepdims=True)
            grad_scores = (grad_soft - soft * row_dot).astype(BF16)
            gv = dot(soft_low, gm)
            gk = dot(grad_scores, qm_s[head])
            value_grad = gv if half == 0 else value_grad + gv
            key_grad = gk if half == 0 else key_grad + gk
            ctx_s[head * head_dim : (head + 1) * head_dim, :] = (
                dot(kt_s[head * head_dim : (head + 1) * head_dim, :], grad_scores) * score_scale
            ).astype(BF16)
        kcols = slice(width + cols.start, width + cols.stop)
        vcols = slice(2 * width + cols.start, 2 * width + cols.stop)
        dqkv_s[:, kcols] = key_grad.astype(BF16)
        dqkv_s[:, vcols] = value_grad.astype(BF16)
        sum_s[:, kcols] += key_grad[first:]
        sum_s[:, vcols] += value_grad[first:]
    dqkv_s[:, :width] = ctx_s[...].T
    sum_s[:, :width] += dqkv_s[first:, :width].astype(F32)
    gmid_sum_s[...] += gmid_s[first:, :]

    mid_s[...] = dot(dqkv_s[...], w_qkv[...], NT)
    for at in range(0, total, step_rows):
        part = slice(at, at + step_rows)
        unit, scale = norm_stats(rows_s[part, :])
        mid_s[part, :] = gmid_s[part, :] + norm_back(mid_s[part, :], gain1, unit, scale)
    input_grad_ref[:, image, :] = jnp.where(token_kept, mid_s[:seq, :], cot_seq_s[:, image, :])

    @pl.when(image == images - 1)
    def _():
        layer_out_ref[...] = layer_s[...].astype(BF16)
        prompt_out_ref[...] = prompt_s[...].astype(BF16)
        pairs = sum_s[...]
        high = pairs.astype(BF16)
        rest = pairs - high.astype(F32)
        middle = rest.astype(BF16)
        low = (rest - middle.astype(F32)).astype(BF16)
        grad = dot(high, w_qkv[...], NT) + (
            dot(middle, w_qkv[...], NT) + dot(low, w_qkv[...], NT)
        )
        unit, scale = norm_stats(rows_s[first:, :])
        local = gmid_sum_s[...] + norm_back(grad, gain1, unit, scale)
        kept = jnp.sum(counts_ref[...][None, :].astype(F32))
        at_row = lax.broadcasted_iota(jnp.int32, local.shape, 0)
        prompt_local_ref[...] = jnp.where(at_row < prompt_count, local, kept)


def run_layer(
    tokens,
    prompts,
    keep_mask,
    counts,
    ln1_gain,
    ln1_bias,
    w_qkv,
    q_bias,
    v_bias,
    w_out,
    out_bias,
    ln2_gain,
    ln2_bias,
    w_fc1,
    fc1_bias,
    w_fc2,
    fc2_bias,
    cot_seq,
    cot_prompt,
):
    images, seq, width = tokens.shape
    prompt_count = prompts.shape[0]
    hidden = w_fc1.shape[1]
    first = round_up(seq, 8)
    total = round_up(first + prompt_count, 128)
    tail = total - first
    head_dim = width // HEADS
    turn = lambda array: jnp.transpose(array, (1, 0, 2))
    whole = pl.BlockSpec(memory_space=pltpu.VMEM)
    anywhere = pl.BlockSpec(memory_space=pl.ANY)
    layer_out, prompt_out, input_grad, prompt_local = pl.pallas_call(
        layer_kernel,
        grid=(images,),
        out_shape=(
            jax.ShapeDtypeStruct((seq, images, width), BF16),
            jax.ShapeDtypeStruct((prompt_count, images, width), BF16),
            jax.ShapeDtypeStruct((seq, images, width), F32),
            jax.ShapeDtypeStruct((tail, width), F32),
        ),
        in_specs=[whole] * 12 + [anywhere] * 7,
        out_specs=(whole,) * 4,
        scratch_shapes=[
            pltpu.VMEM(w_qkv.shape, BF16),
            pltpu.VMEM(w_out.shape, BF16),
            pltpu.VMEM(w_fc1.shape, BF16),
            pltpu.VMEM(w_fc2.shape, BF16),
            pltpu.VMEM((seq, images, width), BF16),
            pltpu.VMEM((seq, images, width), BF16),
            pltpu.VMEM((prompt_count, images, width), BF16),
            pltpu.VMEM((seq, images, width), F32),
            pltpu.VMEM((seq, images, width), F32),
            pltpu.VMEM((prompt_count, images, width), F32),
            pltpu.VMEM((seq, images, width), F32),
            pltpu.VMEM((prompt_count, images, width), F32),
            pltpu.VMEM((total, width), F32),
            pltpu.VMEM((total, width), F32),
            pltpu.VMEM((total, width), BF16),
            pltpu.VMEM((total, width), BF16),
            pltpu.VMEM((total, width), BF16),
            pltpu.VMEM((total, width), BF16),
            pltpu.VMEM((width, total), BF16),
            pltpu.VMEM((width, total), BF16),
            pltpu.VMEM((HEADS, total, 2 * head_dim), BF16),
            pltpu.VMEM((HEADS, total, 2 * head_dim), BF16),
            pltpu.VMEM((HEADS, total, total), BF16),
            pltpu.VMEM((width, total), BF16),
            pltpu.VMEM((total, hidden), BF16),
            pltpu.VMEM((total, hidden), BF16),
            pltpu.VMEM((total, width), F32),
            pltpu.VMEM((total, width), F32),
            pltpu.VMEM((total, 3 * width), BF16),
            pltpu.VMEM((tail, 3 * width), F32),
            pltpu.VMEM((tail, width), F32),
            pltpu.SemaphoreType.DMA((7,)),
        ],
        compiler_params=pltpu.CompilerParams(vmem_limit_bytes=62 << 20),
    )(
        prompts,
        keep_mask,
        counts,
        ln1_gain,
        ln1_bias,
        q_bias,
        v_bias,
        out_bias,
        ln2_gain,
        ln2_bias,
        fc1_bias,
        fc2_bias,
        turn(tokens),
        turn(cot_seq),
        turn(cot_prompt),
        w_qkv,
        w_out,
        w_fc1,
        w_fc2,
    )
    return turn(layer_out), turn(prompt_out), turn(input_grad), prompt_local


def sum_kernel(
    plane,
    line,
    streams,
    patches,
    images,
    local_ref,
    prompts_ref,
    grad_ref,
    penalty_ref,
    sums,
    came,
    line_sums,
    done,
    send_sems,
    recv_sems,
):
    group = plane * streams
    batch = lax.axis_index("batch")
    stream = lax.axis_index("stream")
    level = batch // plane
    spot = lax.rem(batch, plane) * streams + stream
    share = came.shape[1]
    filled = local_ref.shape[0]

    def in_plane(other):
        return (level * plane + other // streams, lax.rem(other, streams))

    def in_line(other):
        return (other * plane + lax.rem(batch, plane), stream)

    plane_peers = [lax.rem(spot + step, group) for step in range(1, group)]
    line_peers = [lax.rem(level + step, line) for step in range(1, line)]

    barrier = pltpu.get_barrier_semaphore()
    for other in plane_peers:
        pl.semaphore_signal(barrier, inc=1, device_id=in_plane(other), device_id_type=MESH)
    for other in line_peers:
        pl.semaphore_signal(barrier, inc=1, device_id=in_line(other), device_id_type=MESH)

    for at in range(group):
        low = min(at * share, filled)
        high = min((at + 1) * share, filled)
        if high > low:
            sums[at, : high - low, :] = local_ref[low:high, :]
        if high - low < share:
            sums[at, high - low :, :] = jnp.zeros((share - (high - low), sums.shape[2]), F32)
    squares = jnp.sum(prompts_ref[...] * prompts_ref[...])
    pl.semaphore_wait(barrier, len(plane_peers) + len(line_peers))

    first_copies = []
    for step, other in enumerate(plane_peers):
        copy = pltpu.make_async_remote_copy(
            src_ref=sums.at[other],
            dst_ref=came.at[spot],
            send_sem=send_sems.at[0, step],
            recv_sem=recv_sems.at[0, spot],
            device_id=in_plane(other),
            device_id_type=MESH,
        )
        copy.start()
        first_copies.append(copy)
    came[spot] = sums[spot]
    for other in plane_peers:
        pltpu.make_async_remote_copy(
            src_ref=sums.at[other],
            dst_ref=came.at[other],
            send_sem=send_sems.at[0, 0],
            recv_sem=recv_sems.at[0, other],
            device_id=in_plane(other),
            device_id_type=MESH,
        ).wait_recv()
    part = came[0]
    for at in range(1, group):
        part = part + came[at]
    line_sums[level] = part

    second_copies = []
    for step, other in enumerate(line_peers):
        copy = pltpu.make_async_remote_copy(
            src_ref=line_sums.at[level],
            dst_ref=line_sums.at[level],
            send_sem=send_sems.at[1, step],
            recv_sem=recv_sems.at[1, level],
            device_id=in_line(other),
            device_id_type=MESH,
        )
        copy.start()
        second_copies.append(copy)
    for other in line_peers:
        pltpu.make_async_remote_copy(
            src_ref=line_sums.at[level],
            dst_ref=line_sums.at[other],
            send_sem=send_sems.at[1, 0],
            recv_sem=recv_sems.at[1, other],
            device_id=in_line(other),
            device_id_type=MESH,
        ).wait_recv()
    whole = line_sums[0]
    for at in range(1, line):
        whole = whole + line_sums[at]
    done[spot] = whole

    third_copies = []
    for step, other in enumerate(plane_peers):
        copy = pltpu.make_async_remote_copy(
            src_ref=done.at[spot],
            dst_ref=done.at[spot],
            send_sem=send_sems.at[2, step],
            recv_sem=recv_sems.at[2, spot],
            device_id=in_plane(other),
            device_id_type=MESH,
        )
        copy.start()
        third_copies.append(copy)
    for other in plane_peers:
        pltpu.make_async_remote_copy(
            src_ref=done.at[spot],
            dst_ref=done.at[other],
            send_sem=send_sems.at[2, 0],
            recv_sem=recv_sems.at[2, other],
            device_id=in_plane(other),
            device_id_type=MESH,
        ).wait_recv()
    prompt_count, width = prompts_ref.shape
    kept = done[prompt_count // share, prompt_count % share : prompt_count % share + 1, :]
    weight = kept * (1.0 / (patches * math.sqrt(images)))
    for at in range(group):
        low = min(at * share, prompt_count)
        high = min((at + 1) * share, prompt_count)
        if high > low:
            grad_ref[low:high, :] = (
                done[at, : high - low, :] + 2.0 * weight * prompts_ref[low:high, :]
            )
    penalty_ref[...] = weight[:, :1] * (squares * (1.0 / (prompt_count * width)))
    for copy in first_copies + second_copies + third_copies:
        copy.wait_send()


def sum_over_devices(local, prompts, patches, images):
    devices = lax.axis_size("batch")
    streams = lax.axis_size("stream")
    plane = 2 ** math.ceil(math.log2(devices) / 2)
    line = devices // plane
    group = plane * streams
    filled, width = local.shape
    share = -(-filled // group)
    if share > 4:
        share = round_up(share, 8)
    whole = pl.BlockSpec(memory_space=pltpu.VMEM)
    return pl.pallas_call(
        functools.partial(sum_kernel, plane, line, streams, patches, images * devices * streams),
        out_shape=(
            jax.ShapeDtypeStruct(prompts.shape, F32),
            jax.ShapeDtypeStruct((1, 1), F32),
        ),
        in_specs=[whole] * 2,
        out_specs=(whole,) * 2,
        scratch_shapes=[
            pltpu.VMEM((group, share, width), F32),
            pltpu.VMEM((group, share, width), F32),
            pltpu.VMEM((line, share, width), F32),
            pltpu.VMEM((group, share, width), F32),
            pltpu.SemaphoreType.DMA((3, max(group, line))),
            pltpu.SemaphoreType.DMA((3, max(group, line))),
        ],
        compiler_params=pltpu.CompilerParams(collective_id=0, has_side_effects=True),
    )(local, prompts)


def body(
    tokens,
    prompts,
    keep_mask,
    counts,
    ln1_gain,
    ln1_bias,
    w_qkv,
    q_bias,
    v_bias,
    w_out,
    out_bias,
    ln2_gain,
    ln2_bias,
    w_fc1,
    fc1_bias,
    w_fc2,
    fc2_bias,
    cot_seq,
    cot_prompt,
):
    layer_out, prompt_out, input_grad, prompt_local = run_layer(
        tokens,
        prompts,
        keep_mask,
        counts,
        ln1_gain,
        ln1_bias,
        w_qkv,
        q_bias,
        v_bias,
        w_out,
        out_bias,
        ln2_gain,
        ln2_bias,
        w_fc1,
        fc1_bias,
        w_fc2,
        fc2_bias,
        cot_seq,
        cot_prompt,
    )
    prompt_grad, penalty = sum_over_devices(
        prompt_local, prompts, keep_mask.shape[1], tokens.shape[0]
    )
    return (layer_out, prompt_out, input_grad, prompt_grad, penalty.reshape(()))


def solution(mesh):
    rows = P(("batch", "stream"), None, None)
    in_specs = (
        (rows, P(), P(("batch", "stream"), None), P(("batch", "stream")))
        + (P(),) * 13
        + (rows, rows)
    )
    return jax.shard_map(
        body,
        mesh=mesh,
        in_specs=in_specs,
        out_specs=(rows, rows, rows, P(), P()),
        check_vma=False,
    )
```

```python
import functools
import math

import jax
import jax.numpy as jnp
from jax import lax
from jax.experimental import pallas as pl
from jax.experimental.pallas import tpu as pltpu
from jax.sharding import PartitionSpec as P

HEADS = 12
EPSILON = 1e-06
F32 = jnp.float32
BF16 = jnp.bfloat16
MESH = pl.DeviceIdType.MESH
DEAD = -1e30

NN = (((1,), (0,)), ((), ()))
NT = (((1,), (1,)), ((), ()))


def dot(a, b, dims=NN):
    return lax.dot_general(a, b, dims, preferred_element_type=F32)


def round_up(value, step):
    return -(-value // step) * step


def norm_stats(rows_in):
    mean = jnp.mean(rows_in, axis=-1, keepdims=True)
    centered = rows_in - mean
    variance = jnp.mean(centered * centered, axis=-1, keepdims=True)
    scale = lax.rsqrt(variance + EPSILON)
    return centered * scale, scale


def norm_back(grad, gain, unit, scale):
    scaled = grad * gain
    mean = jnp.mean(scaled, axis=-1, keepdims=True)
    along = jnp.mean(scaled * unit, axis=-1, keepdims=True)
    return scale * (scaled - mean - unit * along)


class DeviceSum:
    def __init__(self, plane, line, streams, sums, came, line_sums, done, send_sems, recv_sems):
        self.group = plane * streams
        self.line = line
        batch = lax.axis_index("batch")
        stream = lax.axis_index("stream")
        self.level = batch // plane
        self.spot = lax.rem(batch, plane) * streams + stream
        self.sums, self.came, self.line_sums, self.done = sums, came, line_sums, done
        self.send_sems, self.recv_sems = send_sems, recv_sems
        self.in_plane = lambda other: (
            self.level * plane + other // streams,
            lax.rem(other, streams),
        )
        self.in_line = lambda other: (other * plane + lax.rem(batch, plane), stream)
        self.plane_peers = [lax.rem(self.spot + step, self.group) for step in range(1, self.group)]
        self.line_peers = [lax.rem(self.level + step, line) for step in range(1, line)]
        self.started = []

    def greet(self):
        barrier = pltpu.get_barrier_semaphore()
        for other in self.plane_peers:
            pl.semaphore_signal(
                barrier, inc=1, device_id=self.in_plane(other), device_id_type=MESH
            )
        for other in self.line_peers:
            pl.semaphore_signal(barrier, inc=1, device_id=self.in_line(other), device_id_type=MESH)

    def gather(self):
        pl.semaphore_wait(
            pltpu.get_barrier_semaphore(), len(self.plane_peers) + len(self.line_peers)
        )

    def copies(self, phase, peers, where, me, source, target):
        return [
            pltpu.make_async_remote_copy(
                src_ref=source(other),
                dst_ref=target(me),
                send_sem=self.send_sems.at[phase, step],
                recv_sem=self.recv_sems.at[phase, me],
                device_id=where(other),
                device_id_type=MESH,
            )
            for step, other in enumerate(peers)
        ]

    def send(self, phase, peers, where, me, source, target):
        started = self.copies(phase, peers, where, me, source, target)
        for copy in started:
            copy.start()
        self.started += started

    def receive(self, phase, peers, where, source, target):
        for step, other in enumerate(peers):
            pltpu.make_async_remote_copy(
                src_ref=source(other),
                dst_ref=target(other),
                send_sem=self.send_sems.at[phase, step],
                recv_sem=self.recv_sems.at[phase, other],
                device_id=where(other),
                device_id_type=MESH,
            ).wait_recv()

    def first(self):
        self.send(
            0,
            self.plane_peers,
            self.in_plane,
            self.spot,
            lambda other: self.sums.at[other],
            lambda me: self.came.at[me],
        )
        self.came[self.spot] = self.sums[self.spot]

    def second(self):
        self.receive(
            0,
            self.plane_peers,
            self.in_plane,
            lambda other: self.sums.at[other],
            lambda other: self.came.at[other],
        )
        part = self.came[0]
        for at in range(1, self.group):
            part = part + self.came[at]
        self.line_sums[self.level] = part
        self.send(
            1,
            self.line_peers,
            self.in_line,
            self.level,
            lambda other: self.line_sums.at[self.level],
            lambda me: self.line_sums.at[me],
        )

    def third(self):
        self.receive(
            1,
            self.line_peers,
            self.in_line,
            lambda other: self.line_sums.at[self.level],
            lambda other: self.line_sums.at[other],
        )
        whole = self.line_sums[0]
        for at in range(1, self.line):
            whole = whole + self.line_sums[at]
        self.done[self.spot] = whole
        self.send(
            2,
            self.plane_peers,
            self.in_plane,
            self.spot,
            lambda other: self.done.at[self.spot],
            lambda me: self.done.at[me],
        )

    def finish(self):
        self.receive(
            2,
            self.plane_peers,
            self.in_plane,
            lambda other: self.done.at[self.spot],
            lambda other: self.done.at[other],
        )
        for copy in self.started:
            copy.wait_send()


def layer_kernel(
    plane,
    line,
    streams,
    all_images,
    prompts_ref,
    keep_ref,
    counts_ref,
    ln1_gain_ref,
    ln1_bias_ref,
    q_bias_ref,
    v_bias_ref,
    out_bias_ref,
    ln2_gain_ref,
    ln2_bias_ref,
    fc1_bias_ref,
    fc2_bias_ref,
    tokens_hbm,
    cot_seq_hbm,
    cot_prompt_hbm,
    w_qkv_hbm,
    w_out_hbm,
    w_fc1_hbm,
    w_fc2_hbm,
    layer_out_hbm,
    prompt_out_hbm,
    input_grad_hbm,
    prompt_grad_ref,
    penalty_ref,
    w_qkv,
    w_out,
    w_fc1,
    w_fc2,
    seq_low,
    cot_low,
    prompt_low,
    seq_turn,
    cot_turn,
    prompt_turn,
    rows_s,
    cot_s,
    mask_s,
    live_s,
    unit1_s,
    scale1_s,
    unit2_s,
    scale2_s,
    normed_s,
    second_s,
    q_s,
    k_s,
    v_s,
    v_next,
    kt_s,
    kt_next,
    vt_s,
    qm_s,
    gm_s,
    soft_s,
    ds_s,
    ctx_s,
    gq_s,
    recip_s,
    act_s,
    gh_s,
    mid_s,
    gmid_s,
    gsec_s,
    gctx_s,
    dqkv_s,
    gnorm_s,
    igrad_s,
    igrad_rest,
    sum_s,
    gmid_sum_s,
    local_sums,
    came_sums,
    line_sums,
    done_sums,
    load_sems,
    out_sems,
    igrad_sems,
    send_sems,
    recv_sems,
):
    image = pl.program_id(0)
    images = seq_low.shape[1]
    seq, width = seq_low.shape[0], seq_low.shape[2]
    whole_rows = seq // 8 * 8
    prompt_count = prompts_ref.shape[0]
    patches = keep_ref.shape[1]
    lead = seq - patches
    head_dim = width // HEADS
    pair_dim = 2 * head_dim
    pairs = HEADS // 2
    hidden = w_fc1.shape[1]
    total = rows_s.shape[1]
    first = round_up(seq, 8)
    tail = slice(first, total)
    tail_rows = total - first
    score_scale = head_dim ** (-0.5)
    block = 32
    blocks = [slice(at, at + block) for at in range(0, total, block)]
    wide = 256
    tiles = [slice(at, at + wide) for at in range(0, width, wide)]
    past = jnp.maximum(image - 1, 0)
    coming = jnp.minimum(image + 1, images - 1)
    now2 = lax.rem(image, 2)
    other2 = 1 - now2

    gain1 = ln1_gain_ref[...][None, :]
    bias1 = ln1_bias_ref[...][None, :]
    gain2 = ln2_gain_ref[...][None, :]
    bias2 = ln2_bias_ref[...][None, :]

    lane = lax.broadcasted_iota(jnp.int32, (total, pair_dim), 1)
    low_half = lane < head_dim
    one_column = jnp.where(lane == 0, 1.0, 0.0).astype(BF16)

    loads = [
        pltpu.make_async_copy(src, dst, load_sems.at[at])
        for at, (src, dst) in enumerate(
            (
                (tokens_hbm, seq_low),
                (w_qkv_hbm, w_qkv),
                (cot_seq_hbm, cot_low),
                (cot_prompt_hbm, prompt_low),
                (w_out_hbm, w_out),
                (w_fc1_hbm, w_fc1),
                (w_fc2_hbm, w_fc2),
            )
        )
    ]
    def igrad_copies(at, slot):
        return (
            pltpu.make_async_copy(
                igrad_s.at[slot, pl.ds(0, whole_rows), :],
                input_grad_hbm.at[pl.ds(0, whole_rows), at, :],
                igrad_sems.at[0, slot],
            ),
            pltpu.make_async_copy(
                igrad_rest.at[slot],
                input_grad_hbm.at[pl.ds(whole_rows, seq - whole_rows), at, :],
                igrad_sems.at[1, slot],
            ),
        )

    def first_norm(at, slot, part):
        if part.stop <= whole_rows:
            rows = seq_turn[part, at, :]
            rows_s[slot, part, :] = rows
        else:
            if part.start < seq:
                rows_s[slot, part.start : seq, :] = seq_turn[part.start : seq, at, :]
            rows = rows_s[slot, part, :]
        unit, scale = norm_stats(rows)
        unit1_s[slot, part, :] = unit
        scale1_s[slot, part, :] = scale
        normed_s[part, :] = (unit * gain1 + bias1).astype(BF16)

    def project_query():
        q_s[...] = (dot(normed_s[...], w_qkv[:, :width]) + q_bias_ref[...][None, :]).astype(
            BF16
        ) * jnp.asarray(score_scale, BF16)

    def project_key():
        k_s[...] = dot(normed_s[...], w_qkv[:, width : 2 * width]).astype(BF16)
        kt_next[...] = k_s[...].T

    def project_value():
        value = (dot(normed_s[...], w_qkv[:, 2 * width :]) + v_bias_ref[...][None, :]).astype(BF16)
        v_next[...] = value
        for head in range(HEADS):
            vt_s[head, :head_dim, :] = value[:, head * head_dim : (head + 1) * head_dim].T

    def grad_normed(tile):
        gnorm_s[:, tile] = dot(dqkv_s[...], w_qkv[tile, :], NT)

    def first_norm_back(at, slot, part):
        grad = gmid_s[part, :] + norm_back(
            gnorm_s[part, :], gain1, unit1_s[slot, part, :], scale1_s[slot, part, :]
        )
        grad = jnp.where(live_s[at, part, :] > 0.0, grad, cot_s[slot, part, :])
        igrad_s[slot, part, :] = grad
        if part.start <= whole_rows < part.stop and seq > whole_rows:
            igrad_rest[slot] = grad[whole_rows - part.start : seq - part.start]

    over_devices = DeviceSum(
        plane, line, streams, local_sums, came_sums, line_sums, done_sums, send_sems, recv_sems
    )

    @pl.when(image == 0)
    def _():
        over_devices.greet()
        for copy in loads:
            copy.start()
        sum_s[...] = jnp.zeros_like(sum_s)
        gmid_sum_s[...] = jnp.zeros_like(gmid_sum_s)
        dqkv_s[...] = jnp.zeros_like(dqkv_s)
        gmid_s[...] = jnp.zeros_like(gmid_s)
        unit1_s[...] = jnp.zeros_like(unit1_s)
        scale1_s[...] = jnp.zeros_like(scale1_s)
        recip_s[...] = jnp.zeros_like(recip_s)
        for at in range(2):
            rows_s[at, whole_rows:, :] = jnp.zeros((total - whole_rows, width), F32)
            rows_s[at, first : first + prompt_count, :] = prompts_ref[...]
            cot_s[at, whole_rows:, :] = jnp.zeros((total - whole_rows, width), F32)
        for head in range(HEADS):
            vt_s[head, head_dim:, :] = jnp.ones((vt_s.shape[1] - head_dim, total), BF16)
        loads[0].wait()
        seq_turn[...] = seq_low[...].astype(F32)

        at_row = lax.broadcasted_iota(jnp.int32, (total, patches), 0)
        at_col = lax.broadcasted_iota(jnp.int32, (total, patches), 1)
        row_at = lax.broadcasted_iota(jnp.int32, (total, 1), 0)
        always = (row_at < lead) | ((row_at >= first) & (row_at < first + prompt_count))
        for at in range(images):
            keep_row = keep_ref[at : at + 1, :].astype(F32)
            patch_kept = jnp.sum(
                jnp.where(at_row == at_col + lead, keep_row, 0.0), axis=1, keepdims=True
            )
            live = always | (patch_kept > 0.0)
            live_s[at] = jnp.where(live, 1.0, 0.0)
            mask_s[at] = jnp.where((lane == 0) & jnp.logical_not(live), DEAD, 0.0).astype(BF16)

        for part in blocks:
            first_norm(0, 0, part)
        loads[1].wait()
        project_query()
        project_key()
        project_value()
        loads[2].wait()
        cot_turn[...] = cot_low[...].astype(F32)
        loads[3].wait()
        prompt_turn[...] = prompt_low[...].astype(F32)
        for copy in loads[4:]:
            copy.wait()

    @pl.when(image > 1)
    def _():
        for copy in igrad_copies(image - 2, now2):
            copy.start()

    v_s[...] = v_next[...]
    kt_s[...] = kt_next[...]
    mask = mask_s[image]

    def make_queries(pair):
        q_pair = q_s[:, pair * pair_dim : (pair + 1) * pair_dim]
        qm_s[pair, :total, :] = jnp.where(low_half, q_pair, jnp.zeros_like(q_pair))
        qm_s[pair, total:, :] = jnp.where(low_half, jnp.zeros_like(q_pair), q_pair)

    def head_scores(head):
        pair, half = divmod(head, 2)
        if half == 0:
            make_queries(pair)
        keys = jnp.concatenate([k_s[:, pair * pair_dim : (pair + 1) * pair_dim], mask], axis=1)
        queries = jnp.concatenate(
            [qm_s[pair, half * total : (half + 1) * total, :], one_column], axis=1
        )
        return dot(keys, queries, NT)

    scores = head_scores(0)
    for head in range(HEADS):
        pair, half = divmod(head, 2)
        current = scores
        if head + 1 < HEADS:
            scores = head_scores(head + 1)
        for at in range(0, total, 128):
            part = current[:, at : at + 128]
            top = jnp.max(part, axis=0, keepdims=True)
            soft_s[pair, :, half * total + at : half * total + at + 128] = jnp.exp(
                part - top
            ).astype(BF16)
        mixed = dot(vt_s[head], soft_s[pair, :, half * total : (half + 1) * total])
        recip = 1.0 / mixed[head_dim : head_dim + 8]
        recip_s[head : head + 1, :] = recip[:1]
        ctx_s[head * head_dim : (head + 1) * head_dim, :] = (
            mixed[:head_dim].reshape(head_dim // 8, 8, total) * recip[None]
        ).reshape(head_dim, total).astype(BF16)
        if head % 4 == 1:
            grad_normed(tiles[head // 4])

    mid_s[...] = dot(ctx_s[...].T, w_out[...]) + out_bias_ref[...][None, :] + rows_s[now2]
    for part in blocks:
        unit, scale = norm_stats(mid_s[part, :])
        unit2_s[part, :] = unit
        scale2_s[part, :] = scale
        second_s[part, :] = (unit * (0.5 * gain2) + 0.5 * bias2).astype(BF16)

    live = live_s[image]
    for part in blocks:
        if part.stop <= whole_rows:
            cot_s[now2, part, :] = cot_turn[part, image, :]
        elif part.start < seq:
            cot_s[now2, part.start : seq, :] = cot_turn[part.start : seq, image, :]
    cot_s[now2, first : first + prompt_count, :] = prompt_turn[:, image, :]
    grad_half = (jnp.where(live > 0.0, cot_s[now2], 0.0) * 0.5).astype(BF16)
    second = second_s[...]
    root2 = 2.0**0.5
    for count, at in enumerate(range(0, hidden, wide)):
        cols = slice(at, at + wide)
        half_pre = dot(second, w_fc1[:, cols]) + 0.5 * fc1_bias_ref[cols][None, :]
        grad_act = dot(grad_half, w_fc2[cols, :], NT)
        scaled = half_pre * root2
        twice = 1.0 + lax.erf(scaled)
        act_s[:, cols] = (half_pre * twice).astype(BF16)
        bell = jnp.exp2(scaled * scaled * (-math.log2(math.e)))
        gh_s[:, cols] = (grad_act * (twice + scaled * bell * (2.0 / math.pi**0.5))).astype(BF16)
        if count < len(blocks):
            first_norm_back(past, other2, blocks[count])

    per_tile = -(-len(blocks) // len(tiles))
    for count, tile in enumerate(tiles):
        gsec_s[:, tile] = dot(gh_s[...], w_fc1[tile, :], NT)
        for part in blocks[count * per_tile : (count + 1) * per_tile]:
            first_norm(coming, other2, part)
    for count, tile in enumerate(tiles):
        result = dot(act_s[...], w_fc2[:, tile]) + fc2_bias_ref[tile][None, :] + mid_s[:, tile]
        result = jnp.where(live > 0.0, result, rows_s[now2, :, tile])
        seq_turn[:, image, tile] = result[:seq]
        prompt_turn[:, image, tile] = result[first : first + prompt_count]
        for part in blocks[count * per_tile : (count + 1) * per_tile]:
            grad = jnp.where(live[part] > 0.0, cot_s[now2, part, :], 0.0)
            gmid = grad + norm_back(gsec_s[part, :], gain2, unit2_s[part, :], scale2_s[part, :])
            gmid_s[part, :] = gmid
            second_s[part, :] = gmid.astype(BF16)
    gmid_sum_s[...] += gmid_s[tail, :]

    gctx_s[...] = dot(second_s[...], w_out[...], NT)
    project_query()
    gctx_t = gctx_s[...].astype(BF16).T
    recip_t = recip_s[...].T
    for pair in range(pairs):
        cols = slice(pair * pair_dim, (pair + 1) * pair_dim)
        by_total = jnp.where(
            low_half, recip_t[:, 2 * pair : 2 * pair + 1], recip_t[:, 2 * pair + 1 : 2 * pair + 2]
        )
        scaled = (gctx_s[:, cols] * by_total).astype(BF16)
        gm_s[pair, :total, :] = jnp.where(low_half, scaled, jnp.zeros_like(scaled))
        gm_s[pair, total:, :] = jnp.where(low_half, jnp.zeros_like(scaled), scaled)
    project_key()
    project_value()

    def head_grads(head):
        pair, half = divmod(head, 2)
        return dot(
            v_s[:, pair * pair_dim : (pair + 1) * pair_dim],
            gm_s[pair, half * total : (half + 1) * total, :],
            NT,
        )

    grads = head_grads(0)
    for head in range(HEADS):
        pair, half = divmod(head, 2)
        current = grads
        if head + 1 < HEADS:
            grads = head_grads(head + 1)
        rows = slice(head * head_dim, (head + 1) * head_dim)
        row_dot = jnp.sum(
            gctx_t[rows].astype(F32) * ctx_s[rows, :].astype(F32), axis=0, keepdims=True
        ) * recip_s[head : head + 1, :]
        for at in range(0, total, 128):
            cols = slice(half * total + at, half * total + at + 128)
            ds_s[pair, :, cols] = soft_s[pair, :, cols] * (
                current[:, at : at + 128] - row_dot[:, at : at + 128]
            ).astype(BF16)
        gq_s[rows, :] = (
            dot(kt_s[rows, :], ds_s[pair, :, half * total : (half + 1) * total]) * score_scale
        ).astype(BF16)
        if half == 1:
            cols = slice(pair * pair_dim, (pair + 1) * pair_dim)
            kcols = slice(width + cols.start, width + cols.stop)
            vcols = slice(2 * width + cols.start, 2 * width + cols.stop)
            value_grad = dot(soft_s[pair], gm_s[pair])
            dqkv_s[:, vcols] = value_grad.astype(BF16)
            sum_s[:, vcols] += value_grad[first:]
            key_grad = dot(ds_s[pair], qm_s[pair])
            dqkv_s[:, kcols] = key_grad.astype(BF16)
            sum_s[:, kcols] += key_grad[first:]
    query_grad = gq_s[...].T
    dqkv_s[:, :width] = query_grad
    sum_s[:, :width] += query_grad.astype(F32)[first:]

    @pl.when(image > 1)
    def _():
        for copy in igrad_copies(image - 2, now2):
            copy.wait()

    @pl.when(image == images - 1)
    def _():
        last = images - 1
        for copy in igrad_copies(last - 1, (last - 1) % 2):
            copy.start()
        sums = sum_s[...]
        high = sums.astype(BF16)
        rest = sums - high.astype(F32)
        middle = rest.astype(BF16)
        low = (rest - middle.astype(F32)).astype(BF16)
        size = sums.shape[0]
        stacked = dot(jnp.concatenate([high, middle, low], axis=0), w_qkv[...], NT)
        grad = stacked[:size] + (stacked[size : 2 * size] + stacked[2 * size :])
        slot = last % 2
        local = gmid_sum_s[...] + norm_back(
            grad, gain1, unit1_s[slot, tail, :], scale1_s[slot, tail, :]
        )
        kept = jnp.sum(counts_ref[...][None, :].astype(F32))
        at_row = lax.broadcasted_iota(jnp.int32, local.shape, 0)
        local = jnp.where(at_row < prompt_count, local, kept)
        share = local_sums.shape[1]
        for at in range(local_sums.shape[0]):
            low_row, high_row = min(at * share, tail_rows), min((at + 1) * share, tail_rows)
            if high_row > low_row:
                local_sums[at, : high_row - low_row, :] = local[low_row:high_row]
            if high_row - low_row < share:
                local_sums[at, high_row - low_row :, :] = jnp.zeros(
                    (share - (high_row - low_row), width), F32
                )
        over_devices.gather()
        over_devices.first()
        seq_low[...] = seq_turn[...].astype(BF16)
        prompt_low[...] = prompt_turn[...].astype(BF16)
        outs = [
            pltpu.make_async_copy(seq_low, layer_out_hbm, out_sems.at[0]),
            pltpu.make_async_copy(prompt_low, prompt_out_hbm, out_sems.at[1]),
        ]
        for copy in outs:
            copy.start()
        for tile in tiles:
            grad_normed(tile)
        over_devices.second()
        for part in blocks:
            first_norm_back(last, slot, part)
        ends = igrad_copies(last, slot)
        for copy in ends:
            copy.start()
        squares = jnp.sum(prompts_ref[...] * prompts_ref[...])
        over_devices.third()
        for copy in igrad_copies(last - 1, (last - 1) % 2) + ends:
            copy.wait()
        for copy in outs:
            copy.wait()
        over_devices.finish()
        kept_row = done_sums[
            prompt_count // share, prompt_count % share : prompt_count % share + 1, :
        ]
        weight = kept_row * (1.0 / (patches * math.sqrt(all_images)))
        for at in range(done_sums.shape[0]):
            low_row, high_row = min(at * share, prompt_count), min((at + 1) * share, prompt_count)
            if high_row > low_row:
                prompt_grad_ref[low_row:high_row, :] = (
                    done_sums[at, : high_row - low_row, :]
                    + 2.0 * weight * prompts_ref[low_row:high_row, :]
                )
        penalty_ref[...] = weight[:, :1] * (squares * (1.0 / (prompt_count * width)))


def run_layer(
    tokens,
    prompts,
    keep_mask,
    counts,
    ln1_gain,
    ln1_bias,
    w_qkv,
    q_bias,
    v_bias,
    w_out,
    out_bias,
    ln2_gain,
    ln2_bias,
    w_fc1,
    fc1_bias,
    w_fc2,
    fc2_bias,
    cot_seq,
    cot_prompt,
):
    images, seq, width = tokens.shape
    prompt_count = prompts.shape[0]
    hidden = w_fc1.shape[1]
    first = round_up(seq, 8)
    total = round_up(first + prompt_count, 128)
    tail = total - first
    head_dim = width // HEADS
    pairs = HEADS // 2
    turn = lambda array: jnp.transpose(array, (1, 0, 2))
    whole = pl.BlockSpec(memory_space=pltpu.VMEM)
    anywhere = pl.BlockSpec(memory_space=pl.ANY)
    low = lambda *shape: pltpu.VMEM(shape, BF16)
    full = lambda *shape: pltpu.VMEM(shape, F32)
    devices = lax.axis_size("batch")
    streams = lax.axis_size("stream")
    plane = 2 ** math.ceil(math.log2(devices) / 2)
    line = devices // plane
    group = plane * streams
    share = -(-tail // group)
    if share > 4:
        share = round_up(share, 8)
    layer_out, prompt_out, input_grad, prompt_grad, penalty = pl.pallas_call(
        functools.partial(layer_kernel, plane, line, streams, images * devices * streams),
        grid=(images,),
        out_shape=(
            jax.ShapeDtypeStruct((seq, images, width), BF16),
            jax.ShapeDtypeStruct((prompt_count, images, width), BF16),
            jax.ShapeDtypeStruct((seq, images, width), F32),
            jax.ShapeDtypeStruct((prompt_count, width), F32),
            jax.ShapeDtypeStruct((1, 1), F32),
        ),
        in_specs=[whole] * 12 + [anywhere] * 7,
        out_specs=(anywhere,) * 3 + (whole,) * 2,
        scratch_shapes=[
            low(*w_qkv.shape),
            low(*w_out.shape),
            low(*w_fc1.shape),
            low(*w_fc2.shape),
            low(seq, images, width),
            low(seq, images, width),
            low(prompt_count, images, width),
            full(seq, images, width),
            full(seq, images, width),
            full(prompt_count, images, width),
            full(2, total, width),
            full(2, total, width),
            low(images, total, 2 * head_dim),
            full(images, total, 1),
            full(2, total, width),
            full(2, total, 1),
            full(total, width),
            full(total, 1),
            low(total, width),
            low(total, width),
            low(total, width),
            low(total, width),
            low(total, width),
            low(total, width),
            low(width, total),
            low(width, total),
            low(HEADS, head_dim + 16, total),
            low(pairs, 2 * total, 2 * head_dim),
            low(pairs, 2 * total, 2 * head_dim),
            low(pairs, total, 2 * total),
            low(pairs, total, 2 * total),
            low(width, total),
            low(width, total),
            full(16, total),
            low(total, hidden),
            low(total, hidden),
            full(total, width),
            full(total, width),
            full(total, width),
            full(total, width),
            low(total, 3 * width),
            full(total, width),
            full(2, total, width),
            full(2, max(seq % 8, 1), width),
            full(tail, 3 * width),
            full(tail, width),
            full(group, share, width),
            full(group, share, width),
            full(line, share, width),
            full(group, share, width),
            pltpu.SemaphoreType.DMA((7,)),
            pltpu.SemaphoreType.DMA((2,)),
            pltpu.SemaphoreType.DMA((2, 2)),
            pltpu.SemaphoreType.DMA((3, max(group, line))),
            pltpu.SemaphoreType.DMA((3, max(group, line))),
        ],
        compiler_params=pltpu.CompilerParams(
            vmem_limit_bytes=63 << 20, collective_id=0, has_side_effects=True
        ),
    )(
        prompts,
        keep_mask,
        counts,
        ln1_gain,
        ln1_bias,
        q_bias,
        v_bias,
        out_bias,
        ln2_gain,
        ln2_bias,
        fc1_bias,
        fc2_bias,
        turn(tokens),
        turn(cot_seq),
        turn(cot_prompt),
        w_qkv,
        w_out,
        w_fc1,
        w_fc2,
    )
    return (
        turn(layer_out),
        turn(prompt_out),
        turn(input_grad),
        prompt_grad,
        penalty.reshape(()),
    )


def solution(mesh):
    rows = P(("batch", "stream"), None, None)
    in_specs = (
        (rows, P(), P(("batch", "stream"), None), P(("batch", "stream")))
        + (P(),) * 13
        + (rows, rows)
    )
    return jax.shard_map(
        run_layer,
        mesh=mesh,
        in_specs=in_specs,
        out_specs=(rows, rows, rows, P(), P()),
        check_vma=False,
    )
```

```python
import functools
import math

import jax
import jax.numpy as jnp
from jax import lax
from jax.experimental import pallas as pl
from jax.experimental.pallas import tpu as pltpu
from jax.sharding import PartitionSpec as P

HEADS = 12
EPSILON = 1e-06
F32 = jnp.float32
BF16 = jnp.bfloat16
MESH = pl.DeviceIdType.MESH
DEAD = -1e30

NN = (((1,), (0,)), ((), ()))
NT = (((1,), (1,)), ((), ()))


def dot(a, b, dims=NN):
    return lax.dot_general(a, b, dims, preferred_element_type=F32)


def round_up(value, step):
    return -(-value // step) * step


def norm_stats(rows_in):
    mean = jnp.mean(rows_in, axis=-1, keepdims=True)
    centered = rows_in - mean
    variance = jnp.mean(centered * centered, axis=-1, keepdims=True)
    scale = lax.rsqrt(variance + EPSILON)
    return centered * scale, scale


def norm_back(grad, gain, unit, scale):
    scaled = grad * gain
    mean = jnp.mean(scaled, axis=-1, keepdims=True)
    along = jnp.mean(scaled * unit, axis=-1, keepdims=True)
    return scale * (scaled - mean - unit * along)


class DeviceSum:
    def __init__(self, plane, line, streams, sums, came, line_sums, done, send_sems, recv_sems):
        self.group = plane * streams
        self.line = line
        batch = lax.axis_index("batch")
        stream = lax.axis_index("stream")
        self.level = batch // plane
        self.spot = lax.rem(batch, plane) * streams + stream
        self.sums, self.came, self.line_sums, self.done = sums, came, line_sums, done
        self.send_sems, self.recv_sems = send_sems, recv_sems
        self.in_plane = lambda other: (
            self.level * plane + other // streams,
            lax.rem(other, streams),
        )
        self.in_line = lambda other: (other * plane + lax.rem(batch, plane), stream)
        self.plane_peers = [lax.rem(self.spot + step, self.group) for step in range(1, self.group)]
        self.line_peers = [lax.rem(self.level + step, line) for step in range(1, line)]
        self.started = []

    def greet(self):
        barrier = pltpu.get_barrier_semaphore()
        for other in self.plane_peers:
            pl.semaphore_signal(
                barrier, inc=1, device_id=self.in_plane(other), device_id_type=MESH
            )
        for other in self.line_peers:
            pl.semaphore_signal(barrier, inc=1, device_id=self.in_line(other), device_id_type=MESH)

    def gather(self):
        pl.semaphore_wait(
            pltpu.get_barrier_semaphore(), len(self.plane_peers) + len(self.line_peers)
        )

    def copies(self, phase, peers, where, me, source, target):
        return [
            pltpu.make_async_remote_copy(
                src_ref=source(other),
                dst_ref=target(me),
                send_sem=self.send_sems.at[phase, step],
                recv_sem=self.recv_sems.at[phase, me],
                device_id=where(other),
                device_id_type=MESH,
            )
            for step, other in enumerate(peers)
        ]

    def send(self, phase, peers, where, me, source, target):
        started = self.copies(phase, peers, where, me, source, target)
        for copy in started:
            copy.start()
        self.started += started

    def receive(self, phase, peers, where, source, target):
        for step, other in enumerate(peers):
            pltpu.make_async_remote_copy(
                src_ref=source(other),
                dst_ref=target(other),
                send_sem=self.send_sems.at[phase, step],
                recv_sem=self.recv_sems.at[phase, other],
                device_id=where(other),
                device_id_type=MESH,
            ).wait_recv()

    def first(self):
        self.send(
            0,
            self.plane_peers,
            self.in_plane,
            self.spot,
            lambda other: self.sums.at[other],
            lambda me: self.came.at[me],
        )
        self.came[self.spot] = self.sums[self.spot]

    def second(self):
        self.receive(
            0,
            self.plane_peers,
            self.in_plane,
            lambda other: self.sums.at[other],
            lambda other: self.came.at[other],
        )
        part = self.came[0]
        for at in range(1, self.group):
            part = part + self.came[at]
        self.line_sums[self.level] = part
        self.send(
            1,
            self.line_peers,
            self.in_line,
            self.level,
            lambda other: self.line_sums.at[self.level],
            lambda me: self.line_sums.at[me],
        )

    def third(self):
        self.receive(
            1,
            self.line_peers,
            self.in_line,
            lambda other: self.line_sums.at[self.level],
            lambda other: self.line_sums.at[other],
        )
        whole = self.line_sums[0]
        for at in range(1, self.line):
            whole = whole + self.line_sums[at]
        self.done[self.spot] = whole
        self.send(
            2,
            self.plane_peers,
            self.in_plane,
            self.spot,
            lambda other: self.done.at[self.spot],
            lambda me: self.done.at[me],
        )

    def finish(self):
        self.receive(
            2,
            self.plane_peers,
            self.in_plane,
            lambda other: self.done.at[self.spot],
            lambda other: self.done.at[other],
        )
        for copy in self.started:
            copy.wait_send()


def layer_kernel(
    plane,
    line,
    streams,
    all_images,
    prompts_ref,
    keep_ref,
    counts_ref,
    ln1_gain_ref,
    ln1_bias_ref,
    q_bias_ref,
    v_bias_ref,
    out_bias_ref,
    ln2_gain_ref,
    ln2_bias_ref,
    fc1_bias_ref,
    fc2_bias_ref,
    tokens_hbm,
    cot_seq_hbm,
    cot_prompt_hbm,
    w_qkv_hbm,
    w_out_hbm,
    w_fc1_hbm,
    w_fc2_hbm,
    layer_out_ref,
    prompt_out_ref,
    input_grad_ref,
    prompt_grad_ref,
    penalty_ref,
    w_qkv,
    w_out,
    w_fc1,
    w_fc2,
    cot_low,
    prompt_low,
    seq_turn,
    cot_turn,
    prompt_turn,
    rows_s,
    cot_s,
    mask_s,
    live_s,
    unit2_s,
    scale2_s,
    normed_s,
    second_s,
    q_s,
    k_s,
    v_s,
    v_next,
    kt_s,
    kt_next,
    vt_s,
    qm_s,
    gm_s,
    soft_s,
    ds_s,
    ctx_s,
    gctx_s,
    gq_s,
    recip_s,
    half_s,
    early_s,
    act_s,
    gh_s,
    mid_s,
    gmid_s,
    grad_s,
    dqkv_s,
    sum_s,
    gmid_sum_s,
    local_sums,
    came_sums,
    line_sums,
    done_sums,
    load_sems,
    send_sems,
    recv_sems,
):
    image = pl.program_id(0)
    seq, images, width = layer_out_ref.shape
    whole_rows = seq // 8 * 8
    prompt_count = prompts_ref.shape[0]
    patches = keep_ref.shape[1]
    lead = seq - patches
    head_dim = width // HEADS
    pair_dim = 2 * head_dim
    pairs = HEADS // 2
    hidden = w_fc1.shape[1]
    total = rows_s.shape[1]
    first = round_up(seq, 8)
    tail = slice(first, total)
    tail_rows = total - first
    score_scale = head_dim ** (-0.5)
    block = 32
    blocks = [slice(at, at + block) for at in range(0, total, block)]
    wide = 256
    tiles = [slice(at, at + wide) for at in range(0, width, wide)]
    coming = jnp.minimum(image + 1, images - 1)
    now2 = lax.rem(image, 2)
    other2 = 1 - now2

    gain1 = ln1_gain_ref[...][None, :]
    bias1 = ln1_bias_ref[...][None, :]
    gain2 = ln2_gain_ref[...][None, :]
    bias2 = ln2_bias_ref[...][None, :]

    lane = lax.broadcasted_iota(jnp.int32, (total, pair_dim), 1)
    low_half = lane < head_dim
    one_column = jnp.where(lane == 0, 1.0, 0.0).astype(BF16)

    loads = [
        pltpu.make_async_copy(src, dst, load_sems.at[at])
        for at, (src, dst) in enumerate(
            (
                (tokens_hbm, layer_out_ref),
                (w_qkv_hbm, w_qkv),
                (cot_seq_hbm, cot_low),
                (cot_prompt_hbm, prompt_low),
                (w_out_hbm, w_out),
                (w_fc1_hbm, w_fc1),
                (w_fc2_hbm, w_fc2),
            )
        )
    ]
    def token_rows(source, at, target, part):
        stop = min(part.stop, seq)
        if stop > part.start:
            target[part.start : stop, :] = source[part.start : stop, at, :]
        return target[part, :]

    def first_norm(at, slot, part):
        unit, _ = norm_stats(token_rows(seq_turn, at, rows_s.at[slot], part))
        normed_s[part, :] = (unit * gain1 + bias1).astype(BF16)

    def result_cotangent(at, slot, part):
        grad = token_rows(cot_turn, at, cot_s.at[slot], part)
        low_row, high_row = max(part.start, first), min(part.stop, first + prompt_count)
        if high_row > low_row:
            cot_s[slot, low_row:high_row, :] = prompt_turn[low_row - first : high_row - first, at, :]
            grad = cot_s[slot, part, :]
        grad = jnp.where(live_s[at, part, :] > 0.0, grad, 0.0)
        cot_s[slot, part, :] = grad
        half_s[part, :] = (grad * 0.5).astype(BF16)

    def project_query():
        q_s[...] = (dot(normed_s[...], w_qkv[:, :width]) + q_bias_ref[...][None, :]).astype(
            BF16
        ) * jnp.asarray(score_scale, BF16)

    def project_key():
        k_s[...] = dot(normed_s[...], w_qkv[:, width : 2 * width]).astype(BF16)
        kt_next[...] = k_s[...].T

    def project_value():
        value = (dot(normed_s[...], w_qkv[:, 2 * width :]) + v_bias_ref[...][None, :]).astype(BF16)
        v_next[...] = value
        for head in range(HEADS):
            vt_s[head, :head_dim, :] = value[:, head * head_dim : (head + 1) * head_dim].T

    over_devices = DeviceSum(
        plane, line, streams, local_sums, came_sums, line_sums, done_sums, send_sems, recv_sems
    )

    @pl.when(image == 0)
    def _():
        over_devices.greet()
        for copy in loads:
            copy.start()
        sum_s[...] = jnp.zeros_like(sum_s)
        gmid_sum_s[...] = jnp.zeros_like(gmid_sum_s)
        recip_s[...] = jnp.zeros_like(recip_s)
        for at in range(2):
            rows_s[at, whole_rows:, :] = jnp.zeros((total - whole_rows, width), F32)
            rows_s[at, first : first + prompt_count, :] = prompts_ref[...]
            cot_s[at, whole_rows:, :] = jnp.zeros((total - whole_rows, width), F32)
        for head in range(HEADS):
            vt_s[head, head_dim:, :] = jnp.ones((vt_s.shape[1] - head_dim, total), BF16)
        at_row = lax.broadcasted_iota(jnp.int32, (total, patches), 0)
        at_col = lax.broadcasted_iota(jnp.int32, (total, patches), 1)
        row_at = lax.broadcasted_iota(jnp.int32, (total, 1), 0)
        always = (row_at < lead) | ((row_at >= first) & (row_at < first + prompt_count))
        for at in range(images):
            keep_row = keep_ref[at : at + 1, :].astype(F32)
            patch_kept = jnp.sum(
                jnp.where(at_row == at_col + lead, keep_row, 0.0), axis=1, keepdims=True
            )
            live = always | (patch_kept > 0.0)
            live_s[at] = jnp.where(live, 1.0, 0.0)
            mask_s[at] = jnp.where((lane == 0) & jnp.logical_not(live), DEAD, 0.0).astype(BF16)
        loads[0].wait()
        seq_turn[...] = layer_out_ref[...].astype(F32)
        for part in blocks:
            first_norm(0, 0, part)
        loads[1].wait()
        project_query()
        project_key()
        project_value()
        loads[2].wait()
        cot_turn[...] = cot_low[...].astype(F32)
        loads[3].wait()
        prompt_turn[...] = prompt_low[...].astype(F32)
        for part in blocks:
            result_cotangent(0, 0, part)

    v_s[...] = v_next[...]
    kt_s[...] = kt_next[...]
    mask = mask_s[image]

    def make_queries(pair):
        q_pair = q_s[:, pair * pair_dim : (pair + 1) * pair_dim]
        qm_s[pair, :total, :] = jnp.where(low_half, q_pair, jnp.zeros_like(q_pair))
        qm_s[pair, total:, :] = jnp.where(low_half, jnp.zeros_like(q_pair), q_pair)

    def head_scores(head):
        pair, half = divmod(head, 2)
        if half == 0:
            make_queries(pair)
        keys = jnp.concatenate([k_s[:, pair * pair_dim : (pair + 1) * pair_dim], mask], axis=1)
        queries = jnp.concatenate(
            [qm_s[pair, half * total : (half + 1) * total, :], one_column], axis=1
        )
        return dot(keys, queries, NT)

    @pl.when(image == 0)
    def _():
        for copy in loads[4:]:
            copy.wait()

    heads_a_tile = wide // head_dim
    scores = head_scores(0)
    for head in range(HEADS):
        pair, half = divmod(head, 2)
        current = scores
        if head + 1 < HEADS:
            scores = head_scores(head + 1)
        for at in range(0, total, 128):
            part = current[:, at : at + 128]
            top = jnp.max(part, axis=0, keepdims=True)
            soft_s[pair, :, half * total + at : half * total + at + 128] = jnp.exp(
                part - top
            ).astype(BF16)
        mixed = dot(vt_s[head], soft_s[pair, :, half * total : (half + 1) * total])
        recip = 1.0 / mixed[head_dim : head_dim + 8]
        recip_s[head : head + 1, :] = recip[:1]
        ctx_s[head * head_dim : (head + 1) * head_dim, :] = (
            mixed[:head_dim].reshape(head_dim // 8, 8, total) * recip[None]
        ).reshape(head_dim, total).astype(BF16)
        if (head + 1) % heads_a_tile == 0:
            tile = tiles[head // heads_a_tile]
            before = mid_s[image] if tile.start else rows_s[now2] + out_bias_ref[...][None, :]
            mid_s[image] = before + dot(ctx_s[tile, :].T, w_out[tile, :])

    ahead = early_s.shape[0]
    for count in range(ahead):
        early_s[count] = dot(half_s[...], w_fc2[count * wide : (count + 1) * wide, :], NT)
    for part in blocks:
        unit, scale = norm_stats(mid_s[image, part, :])
        unit2_s[part, :] = unit
        scale2_s[part, :] = scale
        second_s[part, :] = (unit * (0.5 * gain2) + 0.5 * bias2).astype(BF16)

    second = second_s[...]
    root2 = 2.0**0.5
    for count, at in enumerate(range(0, hidden, wide)):
        cols = slice(at, at + wide)
        half_pre = dot(second, w_fc1[:, cols]) + 0.5 * fc1_bias_ref[cols][None, :]
        grad_act = early_s[count] if count < ahead else dot(half_s[...], w_fc2[cols, :], NT)
        scaled = half_pre * root2
        twice = 1.0 + lax.erf(scaled)
        act_s[image, :, cols] = (half_pre * twice).astype(BF16)
        bell = jnp.exp2(scaled * scaled * (-math.log2(math.e)))
        gh_s[:, cols] = (grad_act * (twice + scaled * bell * (2.0 / math.pi**0.5))).astype(BF16)

    per_tile = -(-len(blocks) // len(tiles))
    for count, tile in enumerate(tiles):
        grad_s[0, :, tile] = dot(gh_s[...], w_fc1[tile, :], NT)
        for part in blocks[count * per_tile : (count + 1) * per_tile]:
            first_norm(coming, other2, part)
            result_cotangent(coming, other2, part)
    for count, project in enumerate((project_query, project_key, project_value)):
        project()
        for part in blocks[count * per_tile : (count + 1) * per_tile]:
            gmid = cot_s[now2, part, :] + norm_back(
                grad_s[0, part, :], gain2, unit2_s[part, :], scale2_s[part, :]
            )
            gmid_s[image, part, :] = gmid
            second_s[part, :] = gmid.astype(BF16)
    gmid_sum_s[...] += gmid_s[image, tail, :]

    recip_t = recip_s[...].T

    def context_grads(tile):
        grad = dot(second_s[...], w_out[tile, :], NT)
        gctx_s[tile, :] = grad.astype(BF16).T
        for at in range(0, wide, pair_dim):
            pair = (tile.start + at) // pair_dim
            by_total = jnp.where(
                low_half,
                recip_t[:, 2 * pair : 2 * pair + 1],
                recip_t[:, 2 * pair + 1 : 2 * pair + 2],
            )
            scaled = (grad[:, at : at + pair_dim] * by_total).astype(BF16)
            gm_s[pair, :total, :] = jnp.where(low_half, scaled, jnp.zeros_like(scaled))
            gm_s[pair, total:, :] = jnp.where(low_half, jnp.zeros_like(scaled), scaled)

    def head_grads(head):
        pair, half = divmod(head, 2)
        return dot(
            v_s[:, pair * pair_dim : (pair + 1) * pair_dim],
            gm_s[pair, half * total : (half + 1) * total, :],
            NT,
        )

    context_grads(tiles[0])
    grads = head_grads(0)
    for head in range(HEADS):
        pair, half = divmod(head, 2)
        current = grads
        if head % heads_a_tile == 0 and head // heads_a_tile + 1 < len(tiles):
            context_grads(tiles[head // heads_a_tile + 1])
        if head + 1 < HEADS:
            grads = head_grads(head + 1)
        rows = slice(head * head_dim, (head + 1) * head_dim)
        row_dot = jnp.sum(
            gctx_s[rows, :].astype(F32) * ctx_s[rows, :].astype(F32), axis=0, keepdims=True
        ) * recip_s[head : head + 1, :]
        for at in range(0, total, 128):
            cols = slice(half * total + at, half * total + at + 128)
            ds_s[pair % 2, :, cols] = soft_s[pair, :, cols] * (
                current[:, at : at + 128] - row_dot[:, at : at + 128]
            ).astype(BF16)
        gq_s[rows, :] = (
            dot(kt_s[rows, :], ds_s[pair % 2, :, half * total : (half + 1) * total]) * score_scale
        ).astype(BF16)
        if half == 1:
            cols = slice(pair * pair_dim, (pair + 1) * pair_dim)
            kcols = slice(width + cols.start, width + cols.stop)
            vcols = slice(2 * width + cols.start, 2 * width + cols.stop)
            value_grad = dot(soft_s[pair], gm_s[pair])
            dqkv_s[image, :, vcols] = value_grad.astype(BF16)
            sum_s[:, vcols] += value_grad[first:]
            key_grad = dot(ds_s[pair % 2], qm_s[pair])
            dqkv_s[image, :, kcols] = key_grad.astype(BF16)
            sum_s[:, kcols] += key_grad[first:]
    query_grad = gq_s[...].T
    dqkv_s[image, :, :width] = query_grad
    sum_s[:, :width] += query_grad.astype(F32)[first:]

    @pl.when(image == images - 1)
    def _():
        last = images - 1
        sums = sum_s[...]
        high = sums.astype(BF16)
        rest = sums - high.astype(F32)
        middle = rest.astype(BF16)
        low = (rest - middle.astype(F32)).astype(BF16)
        size = sums.shape[0]
        stacked = dot(jnp.concatenate([high, middle, low], axis=0), w_qkv[...], NT)
        grad = stacked[:size] + (stacked[size : 2 * size] + stacked[2 * size :])
        unit, scale = norm_stats(rows_s[0, tail, :])
        local = gmid_sum_s[...] + norm_back(grad, gain1, unit, scale)
        kept = jnp.sum(counts_ref[...][None, :].astype(F32))
        at_row = lax.broadcasted_iota(jnp.int32, local.shape, 0)
        local = jnp.where(at_row < prompt_count, local, kept)
        share = local_sums.shape[1]
        for at in range(local_sums.shape[0]):
            low_row, high_row = min(at * share, tail_rows), min((at + 1) * share, tail_rows)
            if high_row > low_row:
                local_sums[at, : high_row - low_row, :] = local[low_row:high_row]
            if high_row - low_row < share:
                local_sums[at, high_row - low_row :, :] = jnp.zeros(
                    (share - (high_row - low_row), width), F32
                )
        over_devices.gather()
        over_devices.first()

        some_rows = round_up(seq, 16)
        token_blocks = [slice(at, min(at + block, seq)) for at in range(0, seq, block)]

        def forward_out(at, tile):
            result = dot(act_s[at], w_fc2[:, tile]) + fc2_bias_ref[tile][None, :]
            result = result + mid_s[at, :, tile]
            seq_turn[:, at, tile] = jnp.where(
                live_s[at, :seq, :] > 0.0, result[:seq], seq_turn[:, at, tile]
            )
            prompt_turn[:, at, tile] = result[first : first + prompt_count]

        def normed_grads(at):
            for tile in tiles:
                grad_s[at % 2, :some_rows, tile] = dot(
                    dqkv_s[at, :some_rows, :], w_qkv[tile, :], NT
                )

        def first_norm_back(at, part):
            unit, scale = norm_stats(seq_turn[part, at, :])
            grad = gmid_s[at, part, :] + norm_back(grad_s[at % 2, part, :], gain1, unit, scale)
            input_grad_ref[part, at, :] = jnp.where(
                live_s[at, part, :] > 0.0, grad, cot_turn[part, at, :]
            )

        squares = jnp.sum(prompts_ref[...] * prompts_ref[...])
        passes = {(images + 1) * 2 // 5: over_devices.second, (images + 1) * 3 // 5: over_devices.third}
        for at in range(images + 1):
            if at in passes:
                passes[at]()
            if at < images:
                normed_grads(at)
            for count, tile in enumerate(tiles):
                if at > 0:
                    forward_out(at - 1, tile)
                if at < images:
                    each = -(-len(token_blocks) // len(tiles))
                    for part in token_blocks[count * each : (count + 1) * each]:
                        first_norm_back(at, part)
        layer_out_ref[...] = seq_turn[...].astype(BF16)
        prompt_out_ref[...] = prompt_turn[...].astype(BF16)
        over_devices.finish()
        kept_row = done_sums[
            prompt_count // share, prompt_count % share : prompt_count % share + 1, :
        ]
        weight = kept_row * (1.0 / (patches * math.sqrt(all_images)))
        for at in range(done_sums.shape[0]):
            low_row, high_row = min(at * share, prompt_count), min((at + 1) * share, prompt_count)
            if high_row > low_row:
                prompt_grad_ref[low_row:high_row, :] = (
                    done_sums[at, : high_row - low_row, :]
                    + 2.0 * weight * prompts_ref[low_row:high_row, :]
                )
        penalty_ref[...] = weight[:, :1] * (squares * (1.0 / (prompt_count * width)))


def run_layer(
    tokens,
    prompts,
    keep_mask,
    counts,
    ln1_gain,
    ln1_bias,
    w_qkv,
    q_bias,
    v_bias,
    w_out,
    out_bias,
    ln2_gain,
    ln2_bias,
    w_fc1,
    fc1_bias,
    w_fc2,
    fc2_bias,
    cot_seq,
    cot_prompt,
):
    images, seq, width = tokens.shape
    prompt_count = prompts.shape[0]
    hidden = w_fc1.shape[1]
    first = round_up(seq, 8)
    total = round_up(first + prompt_count, 128)
    tail = total - first
    head_dim = width // HEADS
    pairs = HEADS // 2
    turn = lambda array: jnp.transpose(array, (1, 0, 2))
    whole = pl.BlockSpec(memory_space=pltpu.VMEM)
    anywhere = pl.BlockSpec(memory_space=pl.ANY)
    low = lambda *shape: pltpu.VMEM(shape, BF16)
    full = lambda *shape: pltpu.VMEM(shape, F32)
    devices = lax.axis_size("batch")
    streams = lax.axis_size("stream")
    plane = 2 ** math.ceil(math.log2(devices) / 2)
    line = devices // plane
    group = plane * streams
    share = -(-tail // group)
    if share > 4:
        share = round_up(share, 8)
    layer_out, prompt_out, input_grad, prompt_grad, penalty = pl.pallas_call(
        functools.partial(layer_kernel, plane, line, streams, images * devices * streams),
        grid=(images,),
        out_shape=(
            low(seq, images, width),
            low(prompt_count, images, width),
            full(seq, images, width),
            full(prompt_count, width),
            jax.ShapeDtypeStruct((1, 1), F32),
        ),
        in_specs=[whole] * 12 + [anywhere] * 7,
        out_specs=(whole,) * 5,
        scratch_shapes=[
            low(*w_qkv.shape),
            low(*w_out.shape),
            low(*w_fc1.shape),
            low(*w_fc2.shape),
            low(seq, images, width),
            low(prompt_count, images, width),
            full(seq, images, width),
            full(seq, images, width),
            full(prompt_count, images, width),
            full(2, total, width),
            full(2, total, width),
            low(images, total, 2 * head_dim),
            full(images, total, 1),
            full(total, width),
            full(total, 1),
            low(total, width),
            low(total, width),
            low(total, width),
            low(total, width),
            low(total, width),
            low(total, width),
            low(width, total),
            low(width, total),
            low(HEADS, head_dim + 16, total),
            low(pairs, 2 * total, 2 * head_dim),
            low(pairs, 2 * total, 2 * head_dim),
            low(pairs, total, 2 * total),
            low(2, total, 2 * total),
            low(width, total),
            low(width, total),
            low(width, total),
            full(16, total),
            low(total, width),
            full(4, total, 256),
            low(images, total, hidden),
            low(total, hidden),
            full(images, total, width),
            full(images, total, width),
            full(2, total, width),
            low(images, total, 3 * width),
            full(tail, 3 * width),
            full(tail, width),
            full(group, share, width),
            full(group, share, width),
            full(line, share, width),
            full(group, share, width),
            pltpu.SemaphoreType.DMA((7,)),
            pltpu.SemaphoreType.DMA((3, max(group, line))),
            pltpu.SemaphoreType.DMA((3, max(group, line))),
        ],
        compiler_params=pltpu.CompilerParams(
            vmem_limit_bytes=59 << 20, collective_id=0, has_side_effects=True
        ),
    )(
        prompts,
        keep_mask,
        counts,
        ln1_gain,
        ln1_bias,
        q_bias,
        v_bias,
        out_bias,
        ln2_gain,
        ln2_bias,
        fc1_bias,
        fc2_bias,
        turn(tokens),
        turn(cot_seq),
        turn(cot_prompt),
        w_qkv,
        w_out,
        w_fc1,
        w_fc2,
    )
    return (
        turn(layer_out),
        turn(prompt_out),
        turn(input_grad),
        prompt_grad,
        penalty.reshape(()),
    )


def solution(mesh):
    rows = P(("batch", "stream"), None, None)
    in_specs = (
        (rows, P(), P(("batch", "stream"), None), P(("batch", "stream")))
        + (P(),) * 13
        + (rows, rows)
    )
    return jax.shard_map(
        run_layer,
        mesh=mesh,
        in_specs=in_specs,
        out_specs=(rows, rows, rows, P(), P()),
        check_vma=False,
    )
```

```python
import functools
import math

import jax
import jax.numpy as jnp
from jax import lax
from jax.experimental import pallas as pl
from jax.experimental.pallas import tpu as pltpu
from jax.sharding import PartitionSpec as P

HEADS = 12
EPSILON = 1e-06
F32 = jnp.float32
BF16 = jnp.bfloat16
MESH = pl.DeviceIdType.MESH
DEAD = -1e30

NN = (((1,), (0,)), ((), ()))
NT = (((1,), (1,)), ((), ()))


def dot(a, b, dims=NN):
    return lax.dot_general(a, b, dims, preferred_element_type=F32)


def round_up(value, step):
    return -(-value // step) * step


def norm_stats(rows_in):
    mean = jnp.mean(rows_in, axis=-1, keepdims=True)
    centered = rows_in - mean
    variance = jnp.mean(centered * centered, axis=-1, keepdims=True)
    scale = lax.rsqrt(variance + EPSILON)
    return centered * scale, scale


def norm_back(grad, gain, unit, scale):
    scaled = grad * gain
    mean = jnp.mean(scaled, axis=-1, keepdims=True)
    along = jnp.mean(scaled * unit, axis=-1, keepdims=True)
    return scale * (scaled - mean - unit * along)


class DeviceSum:
    def __init__(self, plane, line, streams, sums, came, line_sums, done, send_sems, recv_sems):
        self.group = plane * streams
        self.line = line
        batch = lax.axis_index("batch")
        stream = lax.axis_index("stream")
        self.level = batch // plane
        self.spot = lax.rem(batch, plane) * streams + stream
        self.sums, self.came, self.line_sums, self.done = sums, came, line_sums, done
        self.send_sems, self.recv_sems = send_sems, recv_sems
        self.in_plane = lambda other: (
            self.level * plane + other // streams,
            lax.rem(other, streams),
        )
        self.in_line = lambda other: (other * plane + lax.rem(batch, plane), stream)
        self.plane_peers = [lax.rem(self.spot + step, self.group) for step in range(1, self.group)]
        self.line_peers = [lax.rem(self.level + step, line) for step in range(1, line)]
        self.started = []

    def greet(self):
        barrier = pltpu.get_barrier_semaphore()
        for other in self.plane_peers:
            pl.semaphore_signal(
                barrier, inc=1, device_id=self.in_plane(other), device_id_type=MESH
            )
        for other in self.line_peers:
            pl.semaphore_signal(barrier, inc=1, device_id=self.in_line(other), device_id_type=MESH)

    def gather(self):
        pl.semaphore_wait(
            pltpu.get_barrier_semaphore(), len(self.plane_peers) + len(self.line_peers)
        )

    def copies(self, phase, peers, where, me, source, target):
        return [
            pltpu.make_async_remote_copy(
                src_ref=source(other),
                dst_ref=target(me),
                send_sem=self.send_sems.at[phase, step],
                recv_sem=self.recv_sems.at[phase, me],
                device_id=where(other),
                device_id_type=MESH,
            )
            for step, other in enumerate(peers)
        ]

    def send(self, phase, peers, where, me, source, target):
        started = self.copies(phase, peers, where, me, source, target)
        for copy in started:
            copy.start()
        self.started += started

    def receive(self, phase, peers, where, source, target):
        for step, other in enumerate(peers):
            pltpu.make_async_remote_copy(
                src_ref=source(other),
                dst_ref=target(other),
                send_sem=self.send_sems.at[phase, step],
                recv_sem=self.recv_sems.at[phase, other],
                device_id=where(other),
                device_id_type=MESH,
            ).wait_recv()

    def first(self):
        self.send(
            0,
            self.plane_peers,
            self.in_plane,
            self.spot,
            lambda other: self.sums.at[other],
            lambda me: self.came.at[me],
        )
        self.came[self.spot] = self.sums[self.spot]

    def second(self):
        self.receive(
            0,
            self.plane_peers,
            self.in_plane,
            lambda other: self.sums.at[other],
            lambda other: self.came.at[other],
        )
        part = self.came[0]
        for at in range(1, self.group):
            part = part + self.came[at]
        self.line_sums[self.level] = part
        self.send(
            1,
            self.line_peers,
            self.in_line,
            self.level,
            lambda other: self.line_sums.at[self.level],
            lambda me: self.line_sums.at[me],
        )

    def third(self):
        self.receive(
            1,
            self.line_peers,
            self.in_line,
            lambda other: self.line_sums.at[self.level],
            lambda other: self.line_sums.at[other],
        )
        whole = self.line_sums[0]
        for at in range(1, self.line):
            whole = whole + self.line_sums[at]
        self.done[self.spot] = whole
        self.send(
            2,
            self.plane_peers,
            self.in_plane,
            self.spot,
            lambda other: self.done.at[self.spot],
            lambda me: self.done.at[me],
        )

    def finish(self):
        self.receive(
            2,
            self.plane_peers,
            self.in_plane,
            lambda other: self.done.at[self.spot],
            lambda other: self.done.at[other],
        )
        for copy in self.started:
            copy.wait_send()


def layer_kernel(
    plane,
    line,
    streams,
    all_images,
    prompts_hbm,
    keep_hbm,
    counts_hbm,
    ln1_gain_hbm,
    ln1_bias_hbm,
    q_bias_hbm,
    v_bias_hbm,
    out_bias_hbm,
    ln2_gain_hbm,
    ln2_bias_hbm,
    fc1_bias_hbm,
    fc2_bias_hbm,
    tokens_hbm,
    cot_seq_hbm,
    cot_prompt_hbm,
    w_qkv_hbm,
    w_out_hbm,
    w_fc1_hbm,
    w_fc2_hbm,
    layer_out_ref,
    prompt_out_ref,
    input_grad_ref,
    prompt_grad_ref,
    penalty_ref,
    prompts_ref,
    keep_ref,
    counts_ref,
    ln1_gain_ref,
    ln1_bias_ref,
    q_bias_ref,
    v_bias_ref,
    out_bias_ref,
    ln2_gain_ref,
    ln2_bias_ref,
    fc1_bias_ref,
    fc2_bias_ref,
    w_qkv,
    w_out,
    w_fc1,
    w_fc2,
    cot_low,
    prompt_low,
    seq_turn,
    cot_turn,
    prompt_turn,
    rows_s,
    cot_s,
    mask_s,
    live_s,
    unit2_s,
    scale2_s,
    normed_s,
    second_s,
    q_s,
    k_s,
    v_s,
    v_next,
    kt_s,
    kt_next,
    vt_s,
    qm_s,
    gm_s,
    soft_s,
    ds_s,
    ctx_s,
    gctx_s,
    gq_s,
    recip_s,
    half_s,
    early_s,
    act_s,
    gh_s,
    mid_s,
    gmid_s,
    grad_s,
    dqkv_s,
    sum_s,
    gmid_sum_s,
    local_sums,
    came_sums,
    line_sums,
    done_sums,
    load_sems,
    small_sems,
    send_sems,
    recv_sems,
):
    image = pl.program_id(0)
    seq, images, width = layer_out_ref.shape
    whole_rows = seq // 8 * 8
    prompt_count = prompts_ref.shape[0]
    patches = keep_ref.shape[1]
    lead = seq - patches
    head_dim = width // HEADS
    pair_dim = 2 * head_dim
    pairs = HEADS // 2
    hidden = w_fc1.shape[1]
    total = rows_s.shape[1]
    first = round_up(seq, 8)
    tail = slice(first, total)
    tail_rows = total - first
    score_scale = head_dim ** (-0.5)
    block = 32
    blocks = [slice(at, at + block) for at in range(0, total, block)]
    wide = 256
    tiles = [slice(at, at + wide) for at in range(0, width, wide)]
    coming = jnp.minimum(image + 1, images - 1)
    now2 = lax.rem(image, 2)
    other2 = 1 - now2

    lane = lax.broadcasted_iota(jnp.int32, (total, pair_dim), 1)
    low_half = lane < head_dim
    one_column = jnp.where(lane == 0, 1.0, 0.0).astype(BF16)

    loads = [
        pltpu.make_async_copy(src, dst, load_sems.at[at])
        for at, (src, dst) in enumerate(
            (
                (tokens_hbm, layer_out_ref),
                (w_qkv_hbm, w_qkv),
                (cot_seq_hbm, cot_low),
                (cot_prompt_hbm, prompt_low),
                (w_out_hbm, w_out),
                (w_fc1_hbm, w_fc1),
                (w_fc2_hbm, w_fc2),
            )
        )
    ]
    smalls = [
        pltpu.make_async_copy(src, dst, small_sems.at[at])
        for at, (src, dst) in enumerate(
            (
                (prompts_hbm, prompts_ref),
                (keep_hbm, keep_ref),
                (counts_hbm, counts_ref),
                (ln1_gain_hbm, ln1_gain_ref),
                (ln1_bias_hbm, ln1_bias_ref),
                (q_bias_hbm, q_bias_ref),
                (v_bias_hbm, v_bias_ref),
                (out_bias_hbm, out_bias_ref),
                (ln2_gain_hbm, ln2_gain_ref),
                (ln2_bias_hbm, ln2_bias_ref),
                (fc1_bias_hbm, fc1_bias_ref),
                (fc2_bias_hbm, fc2_bias_ref),
            )
        )
    ]
    def token_rows(source, at, target, part):
        stop = min(part.stop, seq)
        if stop > part.start:
            target[part.start : stop, :] = source[part.start : stop, at, :]
        return target[part, :]

    def first_norm(at, slot, part):
        unit, _ = norm_stats(token_rows(seq_turn, at, rows_s.at[slot], part))
        normed_s[part, :] = (unit * ln1_gain_ref[...][None, :] + ln1_bias_ref[...][None, :]).astype(BF16)

    def result_cotangent(at, slot, part):
        grad = token_rows(cot_turn, at, cot_s.at[slot], part)
        low_row, high_row = max(part.start, first), min(part.stop, first + prompt_count)
        if high_row > low_row:
            cot_s[slot, low_row:high_row, :] = prompt_turn[low_row - first : high_row - first, at, :]
            grad = cot_s[slot, part, :]
        grad = jnp.where(live_s[at, part, :] > 0.0, grad, 0.0)
        cot_s[slot, part, :] = grad
        half_s[part, :] = (grad * 0.5).astype(BF16)

    def project_query():
        q_s[...] = (dot(normed_s[...], w_qkv[:, :width]) + q_bias_ref[...][None, :]).astype(
            BF16
        ) * jnp.asarray(score_scale, BF16)

    def project_key():
        k_s[...] = dot(normed_s[...], w_qkv[:, width : 2 * width]).astype(BF16)
        kt_next[...] = k_s[...].T

    def project_value():
        value = (dot(normed_s[...], w_qkv[:, 2 * width :]) + v_bias_ref[...][None, :]).astype(BF16)
        v_next[...] = value
        for head in range(HEADS):
            vt_s[head, :head_dim, :] = value[:, head * head_dim : (head + 1) * head_dim].T

    over_devices = DeviceSum(
        plane, line, streams, local_sums, came_sums, line_sums, done_sums, send_sems, recv_sems
    )

    @pl.when(image == 0)
    def _():
        loads[0].start()
        for copy in smalls:
            copy.start()
        for copy in loads[1:]:
            copy.start()
        over_devices.greet()
        sum_s[...] = jnp.zeros_like(sum_s)
        gmid_sum_s[...] = jnp.zeros_like(gmid_sum_s)
        recip_s[...] = jnp.zeros_like(recip_s)
        for copy in smalls:
            copy.wait()
        for at in range(2):
            rows_s[at, whole_rows:, :] = jnp.zeros((total - whole_rows, width), F32)
            rows_s[at, first : first + prompt_count, :] = prompts_ref[...]
            cot_s[at, whole_rows:, :] = jnp.zeros((total - whole_rows, width), F32)
        for head in range(HEADS):
            vt_s[head, head_dim:, :] = jnp.ones((vt_s.shape[1] - head_dim, total), BF16)
        at_row = lax.broadcasted_iota(jnp.int32, (total, patches), 0)
        at_col = lax.broadcasted_iota(jnp.int32, (total, patches), 1)
        row_at = lax.broadcasted_iota(jnp.int32, (total, 1), 0)
        always = (row_at < lead) | ((row_at >= first) & (row_at < first + prompt_count))
        for at in range(images):
            keep_row = keep_ref[at : at + 1, :].astype(F32)
            patch_kept = jnp.sum(
                jnp.where(at_row == at_col + lead, keep_row, 0.0), axis=1, keepdims=True
            )
            live = always | (patch_kept > 0.0)
            live_s[at] = jnp.where(live, 1.0, 0.0)
            mask_s[at] = jnp.where((lane == 0) & jnp.logical_not(live), DEAD, 0.0).astype(BF16)
        loads[0].wait()
        seq_turn[...] = layer_out_ref[...].astype(F32)
        for part in blocks:
            first_norm(0, 0, part)
        for copy in loads[1:4]:
            copy.wait()
        project_query()
        cot_turn[...] = cot_low[...].astype(F32)
        prompt_turn[...] = prompt_low[...].astype(F32)
        project_key()
        for part in blocks:
            result_cotangent(0, 0, part)
        project_value()

    v_s[...] = v_next[...]
    kt_s[...] = kt_next[...]
    mask = mask_s[image]

    def make_queries(pair):
        q_pair = q_s[:, pair * pair_dim : (pair + 1) * pair_dim]
        qm_s[pair, :total, :] = jnp.where(low_half, q_pair, jnp.zeros_like(q_pair))
        qm_s[pair, total:, :] = jnp.where(low_half, jnp.zeros_like(q_pair), q_pair)

    def head_scores(head):
        pair, half = divmod(head, 2)
        if half == 0:
            make_queries(pair)
        keys = jnp.concatenate([k_s[:, pair * pair_dim : (pair + 1) * pair_dim], mask], axis=1)
        queries = jnp.concatenate(
            [qm_s[pair, half * total : (half + 1) * total, :], one_column], axis=1
        )
        return dot(keys, queries, NT)

    @pl.when(image == 0)
    def _():
        for copy in loads[4:]:
            copy.wait()

    heads_a_tile = wide // head_dim

    def soften(head, scores):
        pair, half = divmod(head, 2)
        for at in range(0, total, 128):
            part = scores[:, at : at + 128]
            top = jnp.max(part, axis=0, keepdims=True)
            soft_s[pair, :, half * total + at : half * total + at + 128] = jnp.exp(
                part - top
            ).astype(BF16)

    def mix(head):
        pair, half = divmod(head, 2)
        mixed = dot(vt_s[head], soft_s[pair, :, half * total : (half + 1) * total])
        recip = 1.0 / mixed[head_dim : head_dim + 8]
        recip_s[head : head + 1, :] = recip[:1]
        ctx_s[head * head_dim : (head + 1) * head_dim, :] = (
            mixed[:head_dim].reshape(head_dim // 8, 8, total) * recip[None]
        ).reshape(head_dim, total).astype(BF16)
        if (head + 1) % heads_a_tile == 0:
            tile = tiles[head // heads_a_tile]
            before = mid_s[image] if tile.start else rows_s[now2] + out_bias_ref[...][None, :]
            mid_s[image] = before + dot(ctx_s[tile, :].T, w_out[tile, :])

    before, after = 3, 3
    waiting = [head_scores(head) for head in range(before)]
    for head in range(HEADS + after):
        if head + before < HEADS:
            waiting.append(head_scores(head + before))
        if head < HEADS:
            soften(head, waiting.pop(0))
        if head >= after:
            mix(head - after)

    ahead = early_s.shape[0]
    for count in range(ahead):
        early_s[count] = dot(half_s[...], w_fc2[count * wide : (count + 1) * wide, :], NT)
    for part in blocks:
        unit, scale = norm_stats(mid_s[image, part, :])
        unit2_s[part, :] = unit
        scale2_s[part, :] = scale
        second_s[part, :] = (
            unit * (0.5 * ln2_gain_ref[...][None, :]) + 0.5 * ln2_bias_ref[...][None, :]
        ).astype(BF16)

    second = second_s[...]
    root2 = 2.0**0.5
    for count, at in enumerate(range(0, hidden, wide)):
        cols = slice(at, at + wide)
        half_pre = dot(second, w_fc1[:, cols]) + 0.5 * fc1_bias_ref[cols][None, :]
        grad_act = early_s[count] if count < ahead else dot(half_s[...], w_fc2[cols, :], NT)
        scaled = half_pre * root2
        twice = 1.0 + lax.erf(scaled)
        act_s[image, :, cols] = (half_pre * twice).astype(BF16)
        bell = jnp.exp2(scaled * scaled * (-math.log2(math.e)))
        gh_s[:, cols] = (grad_act * (twice + scaled * bell * (2.0 / math.pi**0.5))).astype(BF16)

    per_tile = -(-len(blocks) // len(tiles))
    for count, tile in enumerate(tiles):
        grad_s[0, :, tile] = dot(gh_s[...], w_fc1[tile, :], NT)
        for part in blocks[count * per_tile : (count + 1) * per_tile]:
            first_norm(coming, other2, part)
            result_cotangent(coming, other2, part)
    def second_norm_back(part):
        gmid = cot_s[now2, part, :] + norm_back(
            grad_s[0, part, :], ln2_gain_ref[...][None, :], unit2_s[part, :], scale2_s[part, :]
        )
        gmid_s[image, part, :] = gmid
        second_s[part, :] = gmid.astype(BF16)

    for count, project in enumerate((project_query, project_key, project_value)):
        project()
        for part in blocks[count * per_tile : (count + 1) * per_tile]:
            second_norm_back(part)
    gmid_sum_s[...] += gmid_s[image, tail, :]

    recip_t = recip_s[...].T

    def context_grads(tile):
        grad = dot(second_s[...], w_out[tile, :], NT)
        gctx_s[tile, :] = grad.astype(BF16).T
        for at in range(0, wide, pair_dim):
            pair = (tile.start + at) // pair_dim
            by_total = jnp.where(
                low_half,
                recip_t[:, 2 * pair : 2 * pair + 1],
                recip_t[:, 2 * pair + 1 : 2 * pair + 2],
            )
            scaled = (grad[:, at : at + pair_dim] * by_total).astype(BF16)
            gm_s[pair, :total, :] = jnp.where(low_half, scaled, jnp.zeros_like(scaled))
            gm_s[pair, total:, :] = jnp.where(low_half, jnp.zeros_like(scaled), scaled)

    def head_grads(head):
        pair, half = divmod(head, 2)
        return dot(
            v_s[:, pair * pair_dim : (pair + 1) * pair_dim],
            gm_s[pair, half * total : (half + 1) * total, :],
            NT,
        )

    def score_grads(head, grads):
        pair, half = divmod(head, 2)
        rows = slice(head * head_dim, (head + 1) * head_dim)
        row_dot = jnp.sum(
            gctx_s[rows, :].astype(F32) * ctx_s[rows, :].astype(F32), axis=0, keepdims=True
        ) * recip_s[head : head + 1, :]
        for at in range(0, total, 128):
            cols = slice(half * total + at, half * total + at + 128)
            ds_s[pair % 3, :, cols] = soft_s[pair, :, cols] * (
                grads[:, at : at + 128] - row_dot[:, at : at + 128]
            ).astype(BF16)

    def head_products(head):
        pair, half = divmod(head, 2)
        rows = slice(head * head_dim, (head + 1) * head_dim)
        gq_s[rows, :] = (
            dot(kt_s[rows, :], ds_s[pair % 3, :, half * total : (half + 1) * total]) * score_scale
        ).astype(BF16)
        if half == 1:
            cols = slice(pair * pair_dim, (pair + 1) * pair_dim)
            kcols = slice(width + cols.start, width + cols.stop)
            vcols = slice(2 * width + cols.start, 2 * width + cols.stop)
            value_grad = dot(soft_s[pair], gm_s[pair])
            dqkv_s[image, :, vcols] = value_grad.astype(BF16)
            sum_s[:, vcols] += value_grad[first:]
            key_grad = dot(ds_s[pair % 3], qm_s[pair])
            dqkv_s[image, :, kcols] = key_grad.astype(BF16)
            sum_s[:, kcols] += key_grad[first:]

    context_grads(tiles[0])
    before, after = 2, 3
    waiting = [head_grads(head) for head in range(before)]
    for head in range(HEADS + after):
        if head % heads_a_tile == 0 and head // heads_a_tile + 1 < len(tiles):
            context_grads(tiles[head // heads_a_tile + 1])
        if head + before < HEADS:
            waiting.append(head_grads(head + before))
        if head < HEADS:
            score_grads(head, waiting.pop(0))
        if head >= after:
            head_products(head - after)
    query_grad = gq_s[...].T
    dqkv_s[image, :, :width] = query_grad
    sum_s[:, :width] += query_grad.astype(F32)[first:]

    @pl.when(image == images - 1)
    def _():
        last = images - 1
        sums = sum_s[...]
        high = sums.astype(BF16)
        rest = sums - high.astype(F32)
        middle = rest.astype(BF16)
        low = (rest - middle.astype(F32)).astype(BF16)
        size = sums.shape[0]
        stacked = dot(jnp.concatenate([high, middle, low], axis=0), w_qkv[...], NT)
        grad = stacked[:size] + (stacked[size : 2 * size] + stacked[2 * size :])
        unit, scale = norm_stats(rows_s[0, tail, :])
        local = gmid_sum_s[...] + norm_back(grad, ln1_gain_ref[...][None, :], unit, scale)
        kept = jnp.sum(counts_ref[...][None, :].astype(F32))
        at_row = lax.broadcasted_iota(jnp.int32, local.shape, 0)
        local = jnp.where(at_row < prompt_count, local, kept)
        share = local_sums.shape[1]
        for at in range(local_sums.shape[0]):
            low_row, high_row = min(at * share, tail_rows), min((at + 1) * share, tail_rows)
            if high_row > low_row:
                local_sums[at, : high_row - low_row, :] = local[low_row:high_row]
            if high_row - low_row < share:
                local_sums[at, high_row - low_row :, :] = jnp.zeros(
                    (share - (high_row - low_row), width), F32
                )
        over_devices.gather()
        over_devices.first()

        some_rows = round_up(seq, 16)
        token_blocks = [slice(at, min(at + block, seq)) for at in range(0, seq, block)]

        def forward_out(at, tile):
            result = dot(act_s[at], w_fc2[:, tile]) + fc2_bias_ref[tile][None, :]
            result = result + mid_s[at, :, tile]
            seq_turn[:, at, tile] = jnp.where(
                live_s[at, :seq, :] > 0.0, result[:seq], seq_turn[:, at, tile]
            )
            prompt_turn[:, at, tile] = result[first : first + prompt_count]

        def normed_grads(at):
            for tile in tiles:
                grad_s[at % 2, :some_rows, tile] = dot(
                    dqkv_s[at, :some_rows, :], w_qkv[tile, :], NT
                )

        def first_norm_back(at, part):
            unit, scale = norm_stats(seq_turn[part, at, :])
            grad = gmid_s[at, part, :] + norm_back(grad_s[at % 2, part, :], ln1_gain_ref[...][None, :], unit, scale)
            input_grad_ref[part, at, :] = jnp.where(
                live_s[at, part, :] > 0.0, grad, cot_turn[part, at, :]
            )

        squares = jnp.sum(prompts_ref[...] * prompts_ref[...])
        passes = {(images + 1) * 2 // 5: over_devices.second, (images + 1) * 3 // 5: over_devices.third}
        for at in range(images + 1):
            if at in passes:
                passes[at]()
            if at < images:
                normed_grads(at)
            for count, tile in enumerate(tiles):
                if at > 0:
                    forward_out(at - 1, tile)
                if at < images:
                    each = -(-len(token_blocks) // len(tiles))
                    for part in token_blocks[count * each : (count + 1) * each]:
                        first_norm_back(at, part)
        layer_out_ref[...] = seq_turn[...].astype(BF16)
        prompt_out_ref[...] = prompt_turn[...].astype(BF16)
        over_devices.finish()
        kept_row = done_sums[
            prompt_count // share, prompt_count % share : prompt_count % share + 1, :
        ]
        weight = kept_row * (1.0 / (patches * math.sqrt(all_images)))
        for at in range(done_sums.shape[0]):
            low_row, high_row = min(at * share, prompt_count), min((at + 1) * share, prompt_count)
            if high_row > low_row:
                prompt_grad_ref[low_row:high_row, :] = (
                    done_sums[at, : high_row - low_row, :]
                    + 2.0 * weight * prompts_ref[low_row:high_row, :]
                )
        penalty_ref[...] = weight[:, :1] * (squares * (1.0 / (prompt_count * width)))


def write_kernel(*refs):
    sems = refs[-1]
    count = len(refs) // 2
    copies = [
        pltpu.make_async_copy(refs[at], refs[count + at], sems.at[at]) for at in range(count)
    ]
    for copy in copies:
        copy.start()
    for copy in copies:
        copy.wait()


def run_layer(
    tokens,
    prompts,
    keep_mask,
    counts,
    ln1_gain,
    ln1_bias,
    w_qkv,
    q_bias,
    v_bias,
    w_out,
    out_bias,
    ln2_gain,
    ln2_bias,
    w_fc1,
    fc1_bias,
    w_fc2,
    fc2_bias,
    cot_seq,
    cot_prompt,
):
    images, seq, width = tokens.shape
    prompt_count = prompts.shape[0]
    hidden = w_fc1.shape[1]
    first = round_up(seq, 8)
    total = round_up(first + prompt_count, 128)
    tail = total - first
    head_dim = width // HEADS
    pairs = HEADS // 2
    turn = lambda array: jnp.transpose(array, (1, 0, 2))
    whole = pl.BlockSpec(memory_space=pltpu.VMEM)
    anywhere = pl.BlockSpec(memory_space=pl.ANY)
    low = lambda *shape: pltpu.VMEM(shape, BF16)
    full = lambda *shape: pltpu.VMEM(shape, F32)
    devices = lax.axis_size("batch")
    streams = lax.axis_size("stream")
    plane = 2 ** math.ceil(math.log2(devices) / 2)
    line = devices // plane
    group = plane * streams
    share = -(-tail // group)
    if share > 4:
        share = round_up(share, 8)
    layer_out, prompt_out, input_grad, prompt_grad, penalty = pl.pallas_call(
        functools.partial(layer_kernel, plane, line, streams, images * devices * streams),
        grid=(images,),
        out_shape=(
            low(seq, images, width),
            low(prompt_count, images, width),
            full(seq, images, width),
            full(prompt_count, width),
            full(1, 1),
        ),
        in_specs=[anywhere] * 19,
        out_specs=(whole,) * 5,
        scratch_shapes=[
            full(*prompts.shape),
            pltpu.VMEM(keep_mask.shape, jnp.int32),
            pltpu.VMEM(counts.shape, jnp.int32),
        ]
        + [
            full(*vector.shape)
            for vector in (
                ln1_gain,
                ln1_bias,
                q_bias,
                v_bias,
                out_bias,
                ln2_gain,
                ln2_bias,
                fc1_bias,
                fc2_bias,
            )
        ]
        + [
            low(*w_qkv.shape),
            low(*w_out.shape),
            low(*w_fc1.shape),
            low(*w_fc2.shape),
            low(seq, images, width),
            low(prompt_count, images, width),
            full(seq, images, width),
            full(seq, images, width),
            full(prompt_count, images, width),
            full(2, total, width),
            full(2, total, width),
            low(images, total, 2 * head_dim),
            full(images, total, 1),
            full(total, width),
            full(total, 1),
            low(total, width),
            low(total, width),
            low(total, width),
            low(total, width),
            low(total, width),
            low(total, width),
            low(width, total),
            low(width, total),
            low(HEADS, head_dim + 16, total),
            low(pairs, 2 * total, 2 * head_dim),
            low(pairs, 2 * total, 2 * head_dim),
            low(pairs, total, 2 * total),
            low(3, total, 2 * total),
            low(width, total),
            low(width, total),
            low(width, total),
            full(16, total),
            low(total, width),
            full(4, total, 256),
            low(images, total, hidden),
            low(total, hidden),
            full(images, total, width),
            full(images, total, width),
            full(2, total, width),
            low(images, total, 3 * width),
            full(tail, 3 * width),
            full(tail, width),
            full(group, share, width),
            full(group, share, width),
            full(line, share, width),
            full(group, share, width),
            pltpu.SemaphoreType.DMA((7,)),
            pltpu.SemaphoreType.DMA((12,)),
            pltpu.SemaphoreType.DMA((3, max(group, line))),
            pltpu.SemaphoreType.DMA((3, max(group, line))),
        ],
        compiler_params=pltpu.CompilerParams(
            vmem_limit_bytes=59 << 20, collective_id=0, has_side_effects=True
        ),
    )(
        prompts,
        keep_mask,
        counts,
        ln1_gain,
        ln1_bias,
        q_bias,
        v_bias,
        out_bias,
        ln2_gain,
        ln2_bias,
        fc1_bias,
        fc2_bias,
        turn(tokens),
        turn(cot_seq),
        turn(cot_prompt),
        w_qkv,
        w_out,
        w_fc1,
        w_fc2,
    )
    results = tuple(
        pltpu.with_memory_space_constraint(item, pltpu.VMEM)
        for item in (layer_out, prompt_out, input_grad, prompt_grad, penalty)
    )
    layer_out, prompt_out, input_grad, prompt_grad, penalty = pl.pallas_call(
        write_kernel,
        out_shape=tuple(jax.ShapeDtypeStruct(item.shape, item.dtype) for item in results),
        in_specs=[whole] * len(results),
        out_specs=(anywhere,) * len(results),
        scratch_shapes=[pltpu.SemaphoreType.DMA((len(results),))],
        compiler_params=pltpu.CompilerParams(vmem_limit_bytes=1 << 20),
    )(*results)
    return (
        turn(layer_out),
        turn(prompt_out),
        turn(input_grad),
        prompt_grad,
        penalty.reshape(()),
    )


def solution(mesh):
    rows = P(("batch", "stream"), None, None)
    in_specs = (
        (rows, P(), P(("batch", "stream"), None), P(("batch", "stream")))
        + (P(),) * 13
        + (rows, rows)
    )
    return jax.shard_map(
        run_layer,
        mesh=mesh,
        in_specs=in_specs,
        out_specs=(rows, rows, rows, P(), P()),
        check_vma=False,
    )
```

```python
import functools
import math

import jax
import jax.numpy as jnp
from jax import lax
from jax.experimental import pallas as pl
from jax.experimental.pallas import tpu as pltpu
from jax.sharding import PartitionSpec as P

HEADS = 12
EPSILON = 1e-06
F32 = jnp.float32
BF16 = jnp.bfloat16
MESH = pl.DeviceIdType.MESH
DEAD = -1e30

NN = (((1,), (0,)), ((), ()))
NT = (((1,), (1,)), ((), ()))


def dot(a, b, dims=NN):
    return lax.dot_general(a, b, dims, preferred_element_type=F32)


def round_up(value, step):
    return -(-value // step) * step


def norm_stats(rows_in):
    mean = jnp.mean(rows_in, axis=-1, keepdims=True)
    centered = rows_in - mean
    variance = jnp.mean(centered * centered, axis=-1, keepdims=True)
    scale = lax.rsqrt(variance + EPSILON)
    return centered * scale, scale


def norm_back(grad, gain, unit, scale):
    scaled = grad * gain
    mean = jnp.mean(scaled, axis=-1, keepdims=True)
    along = jnp.mean(scaled * unit, axis=-1, keepdims=True)
    return scale * (scaled - mean - unit * along)


class DeviceSum:
    def __init__(self, plane, line, streams, sums, came, line_sums, done, send_sems, recv_sems):
        self.group = plane * streams
        self.line = line
        batch = lax.axis_index("batch")
        stream = lax.axis_index("stream")
        self.level = batch // plane
        self.spot = lax.rem(batch, plane) * streams + stream
        self.sums, self.came, self.line_sums, self.done = sums, came, line_sums, done
        self.send_sems, self.recv_sems = send_sems, recv_sems
        self.in_plane = lambda other: (
            self.level * plane + other // streams,
            lax.rem(other, streams),
        )
        self.in_line = lambda other: (other * plane + lax.rem(batch, plane), stream)
        self.plane_peers = [lax.rem(self.spot + step, self.group) for step in range(1, self.group)]
        self.line_peers = [lax.rem(self.level + step, line) for step in range(1, line)]
        self.started = []

    def greet(self):
        barrier = pltpu.get_barrier_semaphore()
        for other in self.plane_peers:
            pl.semaphore_signal(
                barrier, inc=1, device_id=self.in_plane(other), device_id_type=MESH
            )
        for other in self.line_peers:
            pl.semaphore_signal(barrier, inc=1, device_id=self.in_line(other), device_id_type=MESH)

    def gather(self):
        pl.semaphore_wait(
            pltpu.get_barrier_semaphore(), len(self.plane_peers) + len(self.line_peers)
        )

    def copies(self, phase, peers, where, me, source, target):
        return [
            pltpu.make_async_remote_copy(
                src_ref=source(other),
                dst_ref=target(me),
                send_sem=self.send_sems.at[phase, step],
                recv_sem=self.recv_sems.at[phase, me],
                device_id=where(other),
                device_id_type=MESH,
            )
            for step, other in enumerate(peers)
        ]

    def send(self, phase, peers, where, me, source, target):
        started = self.copies(phase, peers, where, me, source, target)
        for copy in started:
            copy.start()
        self.started += started

    def receive(self, phase, peers, where, source, target):
        for step, other in enumerate(peers):
            pltpu.make_async_remote_copy(
                src_ref=source(other),
                dst_ref=target(other),
                send_sem=self.send_sems.at[phase, step],
                recv_sem=self.recv_sems.at[phase, other],
                device_id=where(other),
                device_id_type=MESH,
            ).wait_recv()

    def first(self):
        self.send(
            0,
            self.plane_peers,
            self.in_plane,
            self.spot,
            lambda other: self.sums.at[other],
            lambda me: self.came.at[me],
        )
        self.came[self.spot] = self.sums[self.spot]

    def second(self):
        self.receive(
            0,
            self.plane_peers,
            self.in_plane,
            lambda other: self.sums.at[other],
            lambda other: self.came.at[other],
        )
        part = self.came[0]
        for at in range(1, self.group):
            part = part + self.came[at]
        self.line_sums[self.level] = part
        self.send(
            1,
            self.line_peers,
            self.in_line,
            self.level,
            lambda other: self.line_sums.at[self.level],
            lambda me: self.line_sums.at[me],
        )

    def third(self):
        self.receive(
            1,
            self.line_peers,
            self.in_line,
            lambda other: self.line_sums.at[self.level],
            lambda other: self.line_sums.at[other],
        )
        whole = self.line_sums[0]
        for at in range(1, self.line):
            whole = whole + self.line_sums[at]
        self.done[self.spot] = whole
        self.send(
            2,
            self.plane_peers,
            self.in_plane,
            self.spot,
            lambda other: self.done.at[self.spot],
            lambda me: self.done.at[me],
        )

    def finish(self):
        self.receive(
            2,
            self.plane_peers,
            self.in_plane,
            lambda other: self.done.at[self.spot],
            lambda other: self.done.at[other],
        )
        for copy in self.started:
            copy.wait_send()


def layer_kernel(
    plane,
    line,
    streams,
    all_images,
    prompts_hbm,
    keep_hbm,
    counts_hbm,
    ln1_gain_hbm,
    ln1_bias_hbm,
    q_bias_hbm,
    v_bias_hbm,
    out_bias_hbm,
    ln2_gain_hbm,
    ln2_bias_hbm,
    fc1_bias_hbm,
    fc2_bias_hbm,
    tokens_hbm,
    cot_seq_hbm,
    cot_prompt_hbm,
    w_qkv_hbm,
    w_out_hbm,
    w_fc1_hbm,
    w_fc2_hbm,
    layer_out_ref,
    prompt_out_ref,
    input_grad_ref,
    prompt_grad_ref,
    penalty_ref,
    prompts_ref,
    keep_ref,
    counts_ref,
    ln1_gain_ref,
    ln1_bias_ref,
    q_bias_ref,
    v_bias_ref,
    out_bias_ref,
    ln2_gain_ref,
    ln2_bias_ref,
    fc1_bias_ref,
    fc2_bias_ref,
    w_qkv,
    w_out,
    w_fc1,
    w_fc2,
    cot_low,
    prompt_low,
    seq_turn,
    cot_turn,
    prompt_turn,
    rows_s,
    cot_s,
    mask_s,
    live_s,
    unit2_s,
    scale2_s,
    normed_s,
    second_s,
    q_s,
    k_s,
    v_s,
    v_next,
    kt_s,
    kt_next,
    vt_s,
    qm_s,
    gm_s,
    soft_s,
    ds_s,
    ctx_s,
    gctx_s,
    gq_s,
    recip_s,
    half_s,
    early_s,
    act_s,
    gh_s,
    mid_s,
    gmid_s,
    grad_s,
    dqkv_s,
    sum_s,
    gmid_sum_s,
    local_sums,
    came_sums,
    line_sums,
    done_sums,
    load_sems,
    small_sems,
    send_sems,
    recv_sems,
):
    image = pl.program_id(0)
    seq, images, width = layer_out_ref.shape
    whole_rows = seq // 8 * 8
    prompt_count = prompts_ref.shape[0]
    patches = keep_ref.shape[1]
    lead = seq - patches
    head_dim = width // HEADS
    pair_dim = 2 * head_dim
    pairs = HEADS // 2
    hidden = w_fc1.shape[1]
    total = rows_s.shape[1]
    first = round_up(seq, 8)
    tail = slice(first, total)
    tail_rows = total - first
    score_scale = head_dim ** (-0.5)
    block = 32
    blocks = [slice(at, at + block) for at in range(0, total, block)]
    wide = 256
    tiles = [slice(at, at + wide) for at in range(0, width, wide)]
    coming = jnp.minimum(image + 1, images - 1)
    now2 = lax.rem(image, 2)
    other2 = 1 - now2

    lane = lax.broadcasted_iota(jnp.int32, (total, pair_dim), 1)
    low_half = lane < head_dim
    one_column = jnp.where(lane == 0, 1.0, 0.0).astype(BF16)

    loads = [
        pltpu.make_async_copy(src, dst, load_sems.at[at])
        for at, (src, dst) in enumerate(
            (
                (tokens_hbm, layer_out_ref),
                (w_qkv_hbm.at[:, pl.ds(0, width)], w_qkv.at[:, pl.ds(0, width)]),
                (w_qkv_hbm.at[:, pl.ds(width, width)], w_qkv.at[:, pl.ds(width, width)]),
                (w_qkv_hbm.at[:, pl.ds(2 * width, width)], w_qkv.at[:, pl.ds(2 * width, width)]),
                (cot_seq_hbm, cot_low),
                (cot_prompt_hbm, prompt_low),
                (w_out_hbm, w_out),
                (w_fc2_hbm, w_fc2),
                (w_fc1_hbm, w_fc1),
            )
        )
    ]
    smalls = [
        pltpu.make_async_copy(src, dst, small_sems.at[at])
        for at, (src, dst) in enumerate(
            (
                (prompts_hbm, prompts_ref),
                (keep_hbm, keep_ref),
                (counts_hbm, counts_ref),
                (ln1_gain_hbm, ln1_gain_ref),
                (ln1_bias_hbm, ln1_bias_ref),
                (q_bias_hbm, q_bias_ref),
                (v_bias_hbm, v_bias_ref),
                (out_bias_hbm, out_bias_ref),
                (ln2_gain_hbm, ln2_gain_ref),
                (ln2_bias_hbm, ln2_bias_ref),
                (fc1_bias_hbm, fc1_bias_ref),
                (fc2_bias_hbm, fc2_bias_ref),
            )
        )
    ]
    def token_rows(source, at, target, part):
        stop = min(part.stop, seq)
        if stop > part.start:
            target[part.start : stop, :] = source[part.start : stop, at, :]
        return target[part, :]

    def first_norm(at, slot, part):
        unit, _ = norm_stats(token_rows(seq_turn, at, rows_s.at[slot], part))
        normed_s[part, :] = (unit * ln1_gain_ref[...][None, :] + ln1_bias_ref[...][None, :]).astype(BF16)

    def result_cotangent(at, slot, part):
        grad = token_rows(cot_turn, at, cot_s.at[slot], part)
        low_row, high_row = max(part.start, first), min(part.stop, first + prompt_count)
        if high_row > low_row:
            cot_s[slot, low_row:high_row, :] = prompt_turn[low_row - first : high_row - first, at, :]
            grad = cot_s[slot, part, :]
        grad = jnp.where(live_s[at, part, :] > 0.0, grad, 0.0)
        cot_s[slot, part, :] = grad
        half_s[part, :] = (grad * 0.5).astype(BF16)

    some_rows = round_up(seq, 16)

    def project_query(stop):
        q_s[:stop, :] = (
            dot(normed_s[:stop, :], w_qkv[:, :width]) + q_bias_ref[...][None, :]
        ).astype(BF16) * jnp.asarray(score_scale, BF16)

    def project_key(stop):
        k_s[:stop, :] = dot(normed_s[:stop, :], w_qkv[:, width : 2 * width]).astype(BF16)
        kt_next[...] = k_s[...].T

    def project_value(stop):
        v_next[:stop, :] = (
            dot(normed_s[:stop, :], w_qkv[:, 2 * width :]) + v_bias_ref[...][None, :]
        ).astype(BF16)
        value = v_next[...]
        for head in range(HEADS):
            vt_s[head, :head_dim, :] = value[:, head * head_dim : (head + 1) * head_dim].T

    over_devices = DeviceSum(
        plane, line, streams, local_sums, came_sums, line_sums, done_sums, send_sems, recv_sems
    )

    @pl.when(image == 0)
    def _():
        loads[0].start()
        for copy in smalls:
            copy.start()
        for copy in loads[1:6]:
            copy.start()
        over_devices.greet()
        sum_s[...] = jnp.zeros_like(sum_s)
        gmid_sum_s[...] = jnp.zeros_like(gmid_sum_s)
        recip_s[...] = jnp.zeros_like(recip_s)
        for copy in smalls:
            copy.wait()
        for at in range(2):
            rows_s[at, whole_rows:, :] = jnp.zeros((total - whole_rows, width), F32)
            rows_s[at, first : first + prompt_count, :] = prompts_ref[...]
            cot_s[at, whole_rows:, :] = jnp.zeros((total - whole_rows, width), F32)
        for head in range(HEADS):
            vt_s[head, head_dim:, :] = jnp.ones((vt_s.shape[1] - head_dim, total), BF16)
        at_row = lax.broadcasted_iota(jnp.int32, (total, patches), 0)
        at_col = lax.broadcasted_iota(jnp.int32, (total, patches), 1)
        row_at = lax.broadcasted_iota(jnp.int32, (total, 1), 0)
        always = (row_at < lead) | ((row_at >= first) & (row_at < first + prompt_count))
        for at in range(images):
            keep_row = keep_ref[at : at + 1, :].astype(F32)
            patch_kept = jnp.sum(
                jnp.where(at_row == at_col + lead, keep_row, 0.0), axis=1, keepdims=True
            )
            live = always | (patch_kept > 0.0)
            live_s[at] = jnp.where(live, 1.0, 0.0)
            mask_s[at] = jnp.where((lane == 0) & jnp.logical_not(live), DEAD, 0.0).astype(BF16)
        loads[0].wait()
        for copy in loads[6:]:
            copy.start()
        seq_turn[...] = layer_out_ref[...].astype(F32)
        for part in blocks:
            first_norm(0, 0, part)
        loads[1].wait()
        project_query(total)
        loads[2].wait()
        project_key(total)
        loads[3].wait()
        for copy in loads[4:6]:
            copy.wait()
        cot_turn[...] = cot_low[...].astype(F32)
        prompt_turn[...] = prompt_low[...].astype(F32)
        project_value(total)
        for part in blocks:
            result_cotangent(0, 0, part)

    v_s[...] = v_next[...]
    kt_s[...] = kt_next[...]
    mask = mask_s[image]

    def make_queries(pair):
        q_pair = q_s[:, pair * pair_dim : (pair + 1) * pair_dim]
        qm_s[pair, :total, :] = jnp.where(low_half, q_pair, jnp.zeros_like(q_pair))
        qm_s[pair, total:, :] = jnp.where(low_half, jnp.zeros_like(q_pair), q_pair)

    def head_scores(head):
        pair, half = divmod(head, 2)
        if half == 0:
            make_queries(pair)
        keys = jnp.concatenate([k_s[:, pair * pair_dim : (pair + 1) * pair_dim], mask], axis=1)
        queries = jnp.concatenate(
            [qm_s[pair, half * total : (half + 1) * total, :], one_column], axis=1
        )
        return dot(keys, queries, NT)

    @pl.when(image == 0)
    def _():
        loads[6].wait()

    heads_a_tile = wide // head_dim

    def soften(head, scores):
        pair, half = divmod(head, 2)
        for at in range(0, total, 128):
            part = scores[:, at : at + 128]
            top = jnp.max(part, axis=0, keepdims=True)
            soft_s[pair, :, half * total + at : half * total + at + 128] = jnp.exp(
                part - top
            ).astype(BF16)

    def mix(head):
        pair, half = divmod(head, 2)
        mixed = dot(vt_s[head], soft_s[pair, :, half * total : (half + 1) * total])
        recip = 1.0 / mixed[head_dim : head_dim + 8]
        recip_s[head : head + 1, :] = recip[:1]
        ctx_s[head * head_dim : (head + 1) * head_dim, :] = (
            mixed[:head_dim].reshape(head_dim // 8, 8, total) * recip[None]
        ).reshape(head_dim, total).astype(BF16)
        if (head + 1) % heads_a_tile == 0:
            tile = tiles[head // heads_a_tile]
            before = mid_s[image] if tile.start else rows_s[now2] + out_bias_ref[...][None, :]
            mid_s[image] = before + dot(ctx_s[tile, :].T, w_out[tile, :])

    before, after = 3, 3
    waiting = [head_scores(head) for head in range(before)]
    for head in range(HEADS + after):
        if head + before < HEADS:
            waiting.append(head_scores(head + before))
        if head < HEADS:
            soften(head, waiting.pop(0))
        if head >= after:
            mix(head - after)

    @pl.when(image == 0)
    def _():
        for copy in loads[7:]:
            copy.wait()

    ahead = early_s.shape[0]
    for count in range(ahead):
        early_s[count] = dot(half_s[...], w_fc2[count * wide : (count + 1) * wide, :], NT)
        share_of = -(-len(blocks) // ahead)
        for part in blocks[count * share_of : (count + 1) * share_of]:
            unit, scale = norm_stats(mid_s[image, part, :])
            unit2_s[part, :] = unit
            scale2_s[part, :] = scale
            second_s[part, :] = (
                unit * (0.5 * ln2_gain_ref[...][None, :]) + 0.5 * ln2_bias_ref[...][None, :]
            ).astype(BF16)

    second = second_s[...]
    root2 = 2.0**0.5
    for count, at in enumerate(range(0, hidden, wide)):
        cols = slice(at, at + wide)
        half_pre = dot(second, w_fc1[:, cols]) + 0.5 * fc1_bias_ref[cols][None, :]
        grad_act = early_s[count] if count < ahead else dot(half_s[...], w_fc2[cols, :], NT)
        scaled = half_pre * root2
        twice = 1.0 + lax.erf(scaled)
        act_s[image, :, cols] = (half_pre * twice).astype(BF16)
        bell = jnp.exp2(scaled * scaled * (-math.log2(math.e)))
        gh_s[:, cols] = (grad_act * (twice + scaled * bell * (2.0 / math.pi**0.5))).astype(BF16)

    per_tile = -(-len(blocks) // len(tiles))
    for count, tile in enumerate(tiles):
        grad_s[0, :, tile] = dot(gh_s[...], w_fc1[tile, :], NT)
        for part in blocks[count * per_tile : (count + 1) * per_tile]:
            if part.start < some_rows:
                first_norm(coming, other2, part)
            result_cotangent(coming, other2, part)
    def second_norm_back(part):
        gmid = cot_s[now2, part, :] + norm_back(
            grad_s[0, part, :], ln2_gain_ref[...][None, :], unit2_s[part, :], scale2_s[part, :]
        )
        gmid_s[image, part, :] = gmid
        second_s[part, :] = gmid.astype(BF16)

    for count, project in enumerate((project_query, project_key, project_value)):
        project(some_rows)
        for part in blocks[count * per_tile : (count + 1) * per_tile]:
            second_norm_back(part)
    gmid_sum_s[...] += gmid_s[image, tail, :]

    recip_t = recip_s[...].T

    def context_grads(tile):
        grad = dot(second_s[...], w_out[tile, :], NT)
        gctx_s[tile, :] = grad.astype(BF16).T
        for at in range(0, wide, pair_dim):
            pair = (tile.start + at) // pair_dim
            by_total = jnp.where(
                low_half,
                recip_t[:, 2 * pair : 2 * pair + 1],
                recip_t[:, 2 * pair + 1 : 2 * pair + 2],
            )
            scaled = (grad[:, at : at + pair_dim] * by_total).astype(BF16)
            gm_s[pair, :total, :] = jnp.where(low_half, scaled, jnp.zeros_like(scaled))
            gm_s[pair, total:, :] = jnp.where(low_half, jnp.zeros_like(scaled), scaled)

    def head_grads(head):
        pair, half = divmod(head, 2)
        return dot(
            v_s[:, pair * pair_dim : (pair + 1) * pair_dim],
            gm_s[pair, half * total : (half + 1) * total, :],
            NT,
        )

    def score_grads(head, grads):
        pair, half = divmod(head, 2)
        rows = slice(head * head_dim, (head + 1) * head_dim)
        row_dot = jnp.sum(
            gctx_s[rows, :].astype(F32) * ctx_s[rows, :].astype(F32), axis=0, keepdims=True
        ) * recip_s[head : head + 1, :]
        for at in range(0, total, 128):
            cols = slice(half * total + at, half * total + at + 128)
            ds_s[pair % 3, :, cols] = soft_s[pair, :, cols] * (
                grads[:, at : at + 128] - row_dot[:, at : at + 128]
            ).astype(BF16)

    def head_products(head):
        pair, half = divmod(head, 2)
        rows = slice(head * head_dim, (head + 1) * head_dim)
        gq_s[rows, :] = (
            dot(kt_s[rows, :], ds_s[pair % 3, :, half * total : (half + 1) * total]) * score_scale
        ).astype(BF16)
        if half == 1:
            cols = slice(pair * pair_dim, (pair + 1) * pair_dim)
            kcols = slice(width + cols.start, width + cols.stop)
            vcols = slice(2 * width + cols.start, 2 * width + cols.stop)
            value_grad = dot(soft_s[pair], gm_s[pair])
            dqkv_s[image, :, vcols] = value_grad.astype(BF16)
            sum_s[:, vcols] += value_grad[first:]
            key_grad = dot(ds_s[pair % 3], qm_s[pair])
            dqkv_s[image, :, kcols] = key_grad.astype(BF16)
            sum_s[:, kcols] += key_grad[first:]

    context_grads(tiles[0])
    before, after = 2, 3
    waiting = [head_grads(head) for head in range(before)]
    for head in range(HEADS + after):
        if head % heads_a_tile == 0 and head // heads_a_tile + 1 < len(tiles):
            context_grads(tiles[head // heads_a_tile + 1])
        if head + before < HEADS:
            waiting.append(head_grads(head + before))
        if head < HEADS:
            score_grads(head, waiting.pop(0))
        if head >= after:
            head_products(head - after)
    query_grad = gq_s[...].T
    dqkv_s[image, :, :width] = query_grad
    sum_s[:, :width] += query_grad.astype(F32)[first:]

    @pl.when(image == images - 1)
    def _():
        last = images - 1
        sums = sum_s[...]
        high = sums.astype(BF16)
        rest = sums - high.astype(F32)
        middle = rest.astype(BF16)
        low = (rest - middle.astype(F32)).astype(BF16)
        size = sums.shape[0]
        stacked = dot(jnp.concatenate([high, middle, low], axis=0), w_qkv[...], NT)
        grad = stacked[:size] + (stacked[size : 2 * size] + stacked[2 * size :])
        unit, scale = norm_stats(rows_s[0, tail, :])
        local = gmid_sum_s[...] + norm_back(grad, ln1_gain_ref[...][None, :], unit, scale)
        kept = jnp.sum(counts_ref[...][None, :].astype(F32))
        at_row = lax.broadcasted_iota(jnp.int32, local.shape, 0)
        local = jnp.where(at_row < prompt_count, local, kept)
        share = local_sums.shape[1]
        for at in range(local_sums.shape[0]):
            low_row, high_row = min(at * share, tail_rows), min((at + 1) * share, tail_rows)
            if high_row > low_row:
                local_sums[at, : high_row - low_row, :] = local[low_row:high_row]
            if high_row - low_row < share:
                local_sums[at, high_row - low_row :, :] = jnp.zeros(
                    (share - (high_row - low_row), width), F32
                )
        over_devices.gather()
        over_devices.first()

        token_blocks = [slice(at, min(at + block, seq)) for at in range(0, seq, block)]

        def forward_out(group, tile):
            count = len(group)
            products = dot(
                act_s[group[0] : group[0] + count].reshape(count * total, hidden), w_fc2[:, tile]
            )
            for order, at in enumerate(group):
                result = products[order * total : (order + 1) * total]
                result = result + fc2_bias_ref[tile][None, :] + mid_s[at, :, tile]
                seq_turn[:, at, tile] = jnp.where(
                    live_s[at, :seq, :] > 0.0, result[:seq], seq_turn[:, at, tile]
                )
                prompt_turn[:, at, tile] = result[first : first + prompt_count]

        def normed_grads(group):
            count = len(group)
            grads = dqkv_s[group[0] : group[0] + count, :some_rows, :]
            for tile in tiles:
                grad_s[:count, :some_rows, tile] = dot(
                    grads.reshape(count * some_rows, 3 * width), w_qkv[tile, :], NT
                ).reshape(count, some_rows, wide)

        def first_norm_back(at, order, part):
            unit, scale = norm_stats(layer_out_ref[part, at, :].astype(F32))
            grad = gmid_s[at, part, :] + norm_back(
                grad_s[order, part, :], ln1_gain_ref[...][None, :], unit, scale
            )
            input_grad_ref[part, at, :] = jnp.where(
                live_s[at, part, :] > 0.0, grad, cot_turn[part, at, :]
            )

        squares = jnp.sum(prompts_ref[...] * prompts_ref[...])
        groups = [list(range(at, min(at + 2, images))) for at in range(0, images, 2)]
        spots = len(groups) * len(tiles)
        passes = {spots * 2 // 6: over_devices.second, spots * 4 // 6: over_devices.third}
        for turn_at, group in enumerate(groups):
            todo = [
                (at, order, part) for order, at in enumerate(group) for part in token_blocks
            ]
            each = -(-len(todo) // len(tiles))
            for count, tile in enumerate(tiles):
                if turn_at * len(tiles) + count in passes:
                    passes[turn_at * len(tiles) + count]()
                if count == 0:
                    normed_grads(group)
                forward_out(group, tile)
                for item in todo[count * each : (count + 1) * each]:
                    first_norm_back(*item)
        layer_out_ref[...] = seq_turn[...].astype(BF16)
        prompt_out_ref[...] = prompt_turn[...].astype(BF16)
        over_devices.finish()
        kept_row = done_sums[
            prompt_count // share, prompt_count % share : prompt_count % share + 1, :
        ]
        weight = kept_row * (1.0 / (patches * math.sqrt(all_images)))
        for at in range(done_sums.shape[0]):
            low_row, high_row = min(at * share, prompt_count), min((at + 1) * share, prompt_count)
            if high_row > low_row:
                prompt_grad_ref[low_row:high_row, :] = (
                    done_sums[at, : high_row - low_row, :]
                    + 2.0 * weight * prompts_ref[low_row:high_row, :]
                )
        penalty_ref[...] = weight[:, :1] * (squares * (1.0 / (prompt_count * width)))


def write_kernel(*refs):
    sems = refs[-1]
    count = len(refs) // 2
    copies = []
    for at in range(count):
        size = refs[at].shape[0]
        cuts = 4 if size > 100 else 1
        for cut in range(cuts):
            part = pl.ds(cut * size // cuts, (cut + 1) * size // cuts - cut * size // cuts)
            copies.append(
                pltpu.make_async_copy(
                    refs[at].at[part], refs[count + at].at[part], sems.at[at, cut]
                )
            )
    for copy in copies:
        copy.start()
    for copy in copies:
        copy.wait()


def run_layer(
    tokens,
    prompts,
    keep_mask,
    counts,
    ln1_gain,
    ln1_bias,
    w_qkv,
    q_bias,
    v_bias,
    w_out,
    out_bias,
    ln2_gain,
    ln2_bias,
    w_fc1,
    fc1_bias,
    w_fc2,
    fc2_bias,
    cot_seq,
    cot_prompt,
):
    images, seq, width = tokens.shape
    prompt_count = prompts.shape[0]
    hidden = w_fc1.shape[1]
    first = round_up(seq, 8)
    total = round_up(first + prompt_count, 128)
    tail = total - first
    head_dim = width // HEADS
    pairs = HEADS // 2
    turn = lambda array: jnp.transpose(array, (1, 0, 2))
    whole = pl.BlockSpec(memory_space=pltpu.VMEM)
    anywhere = pl.BlockSpec(memory_space=pl.ANY)
    low = lambda *shape: pltpu.VMEM(shape, BF16)
    full = lambda *shape: pltpu.VMEM(shape, F32)
    devices = lax.axis_size("batch")
    streams = lax.axis_size("stream")
    plane = 2 ** math.ceil(math.log2(devices) / 2)
    line = devices // plane
    group = plane * streams
    share = -(-tail // group)
    if share > 4:
        share = round_up(share, 8)
    layer_out, prompt_out, input_grad, prompt_grad, penalty = pl.pallas_call(
        functools.partial(layer_kernel, plane, line, streams, images * devices * streams),
        grid=(images,),
        out_shape=(
            low(seq, images, width),
            low(prompt_count, images, width),
            full(seq, images, width),
            full(prompt_count, width),
            full(1, 1),
        ),
        in_specs=[anywhere] * 19,
        out_specs=(whole,) * 5,
        scratch_shapes=[
            full(*prompts.shape),
            pltpu.VMEM(keep_mask.shape, jnp.int32),
            pltpu.VMEM(counts.shape, jnp.int32),
        ]
        + [
            full(*vector.shape)
            for vector in (
                ln1_gain,
                ln1_bias,
                q_bias,
                v_bias,
                out_bias,
                ln2_gain,
                ln2_bias,
                fc1_bias,
                fc2_bias,
            )
        ]
        + [
            low(*w_qkv.shape),
            low(*w_out.shape),
            low(*w_fc1.shape),
            low(*w_fc2.shape),
            low(seq, images, width),
            low(prompt_count, images, width),
            full(seq, images, width),
            full(seq, images, width),
            full(prompt_count, images, width),
            full(2, total, width),
            full(2, total, width),
            low(images, total, 2 * head_dim),
            full(images, total, 1),
            full(total, width),
            full(total, 1),
            low(total, width),
            low(total, width),
            low(total, width),
            low(total, width),
            low(total, width),
            low(total, width),
            low(width, total),
            low(width, total),
            low(HEADS, head_dim + 16, total),
            low(pairs, 2 * total, 2 * head_dim),
            low(pairs, 2 * total, 2 * head_dim),
            low(pairs, total, 2 * total),
            low(3, total, 2 * total),
            low(width, total),
            low(width, total),
            low(width, total),
            full(16, total),
            low(total, width),
            full(4, total, 256),
            low(images, total, hidden),
            low(total, hidden),
            full(images, total, width),
            full(images, total, width),
            full(2, total, width),
            low(images, total, 3 * width),
            full(tail, 3 * width),
            full(tail, width),
            full(group, share, width),
            full(group, share, width),
            full(line, share, width),
            full(group, share, width),
            pltpu.SemaphoreType.DMA((9,)),
            pltpu.SemaphoreType.DMA((12,)),
            pltpu.SemaphoreType.DMA((3, max(group, line))),
            pltpu.SemaphoreType.DMA((3, max(group, line))),
        ],
        compiler_params=pltpu.CompilerParams(
            vmem_limit_bytes=59 << 20, collective_id=0, has_side_effects=True
        ),
    )(
        prompts,
        keep_mask,
        counts,
        ln1_gain,
        ln1_bias,
        q_bias,
        v_bias,
        out_bias,
        ln2_gain,
        ln2_bias,
        fc1_bias,
        fc2_bias,
        turn(tokens),
        turn(cot_seq),
        turn(cot_prompt),
        w_qkv,
        w_out,
        w_fc1,
        w_fc2,
    )
    results = tuple(
        pltpu.with_memory_space_constraint(item, pltpu.VMEM)
        for item in (layer_out, prompt_out, input_grad, prompt_grad, penalty)
    )
    layer_out, prompt_out, input_grad, prompt_grad, penalty = pl.pallas_call(
        write_kernel,
        out_shape=tuple(jax.ShapeDtypeStruct(item.shape, item.dtype) for item in results),
        in_specs=[whole] * len(results),
        out_specs=(anywhere,) * len(results),
        scratch_shapes=[pltpu.SemaphoreType.DMA((len(results), 4))],
        compiler_params=pltpu.CompilerParams(vmem_limit_bytes=1 << 20),
    )(*results)
    return (
        turn(layer_out),
        turn(prompt_out),
        turn(input_grad),
        prompt_grad,
        penalty.reshape(()),
    )


def solution(mesh):
    rows = P(("batch", "stream"), None, None)
    in_specs = (
        (rows, P(), P(("batch", "stream"), None), P(("batch", "stream")))
        + (P(),) * 13
        + (rows, rows)
    )
    return jax.shard_map(
        run_layer,
        mesh=mesh,
        in_specs=in_specs,
        out_specs=(rows, rows, rows, P(), P()),
        check_vma=False,
    )
```

```python
import functools
import math

import jax
import jax.numpy as jnp
from jax import lax
from jax.experimental import pallas as pl
from jax.experimental.pallas import tpu as pltpu
from jax.sharding import PartitionSpec as P

HEADS = 12
EPSILON = 1e-06
F32 = jnp.float32
BF16 = jnp.bfloat16
MESH = pl.DeviceIdType.MESH
DEAD = -1e30

NN = (((1,), (0,)), ((), ()))
NT = (((1,), (1,)), ((), ()))


def dot(a, b, dims=NN):
    return lax.dot_general(a, b, dims, preferred_element_type=F32)


def round_up(value, step):
    return -(-value // step) * step


def norm_stats(rows_in):
    mean = jnp.mean(rows_in, axis=-1, keepdims=True)
    centered = rows_in - mean
    variance = jnp.mean(centered * centered, axis=-1, keepdims=True)
    scale = lax.rsqrt(variance + EPSILON)
    return centered * scale, scale


def norm_back(grad, gain, unit, scale):
    scaled = grad * gain
    mean = jnp.mean(scaled, axis=-1, keepdims=True)
    along = jnp.mean(scaled * unit, axis=-1, keepdims=True)
    return scale * (scaled - mean - unit * along)


class DeviceSum:
    def __init__(self, plane, line, streams, sums, came, line_sums, done, send_sems, recv_sems):
        self.group = plane * streams
        self.line = line
        batch = lax.axis_index("batch")
        stream = lax.axis_index("stream")
        self.level = batch // plane
        self.spot = lax.rem(batch, plane) * streams + stream
        self.sums, self.came, self.line_sums, self.done = sums, came, line_sums, done
        self.send_sems, self.recv_sems = send_sems, recv_sems
        self.in_plane = lambda other: (
            self.level * plane + other // streams,
            lax.rem(other, streams),
        )
        self.in_line = lambda other: (other * plane + lax.rem(batch, plane), stream)
        self.plane_peers = [lax.rem(self.spot + step, self.group) for step in range(1, self.group)]
        self.line_peers = [lax.rem(self.level + step, line) for step in range(1, line)]
        self.started = []

    def greet(self):
        barrier = pltpu.get_barrier_semaphore()
        for other in self.plane_peers:
            pl.semaphore_signal(
                barrier, inc=1, device_id=self.in_plane(other), device_id_type=MESH
            )
        for other in self.line_peers:
            pl.semaphore_signal(barrier, inc=1, device_id=self.in_line(other), device_id_type=MESH)

    def gather(self):
        pl.semaphore_wait(
            pltpu.get_barrier_semaphore(), len(self.plane_peers) + len(self.line_peers)
        )

    def copies(self, phase, peers, where, me, source, target):
        return [
            pltpu.make_async_remote_copy(
                src_ref=source(other),
                dst_ref=target(me),
                send_sem=self.send_sems.at[phase, step],
                recv_sem=self.recv_sems.at[phase, me],
                device_id=where(other),
                device_id_type=MESH,
            )
            for step, other in enumerate(peers)
        ]

    def send(self, phase, peers, where, me, source, target):
        started = self.copies(phase, peers, where, me, source, target)
        for copy in started:
            copy.start()
        self.started += started

    def receive(self, phase, peers, where, source, target):
        for step, other in enumerate(peers):
            pltpu.make_async_remote_copy(
                src_ref=source(other),
                dst_ref=target(other),
                send_sem=self.send_sems.at[phase, step],
                recv_sem=self.recv_sems.at[phase, other],
                device_id=where(other),
                device_id_type=MESH,
            ).wait_recv()

    def first(self):
        self.send(
            0,
            self.plane_peers,
            self.in_plane,
            self.spot,
            lambda other: self.sums.at[other],
            lambda me: self.came.at[me],
        )
        self.came[self.spot] = self.sums[self.spot]

    def second(self):
        self.receive(
            0,
            self.plane_peers,
            self.in_plane,
            lambda other: self.sums.at[other],
            lambda other: self.came.at[other],
        )
        part = self.came[0]
        for at in range(1, self.group):
            part = part + self.came[at]
        self.line_sums[self.level] = part
        self.send(
            1,
            self.line_peers,
            self.in_line,
            self.level,
            lambda other: self.line_sums.at[self.level],
            lambda me: self.line_sums.at[me],
        )

    def third(self):
        self.receive(
            1,
            self.line_peers,
            self.in_line,
            lambda other: self.line_sums.at[self.level],
            lambda other: self.line_sums.at[other],
        )
        whole = self.line_sums[0]
        for at in range(1, self.line):
            whole = whole + self.line_sums[at]
        self.done[self.spot] = whole
        self.send(
            2,
            self.plane_peers,
            self.in_plane,
            self.spot,
            lambda other: self.done.at[self.spot],
            lambda me: self.done.at[me],
        )

    def finish(self):
        self.receive(
            2,
            self.plane_peers,
            self.in_plane,
            lambda other: self.done.at[self.spot],
            lambda other: self.done.at[other],
        )
        for copy in self.started:
            copy.wait_send()


def layer_kernel(
    plane,
    line,
    streams,
    all_images,
    prompts_hbm,
    keep_hbm,
    counts_hbm,
    ln1_gain_hbm,
    ln1_bias_hbm,
    q_bias_hbm,
    v_bias_hbm,
    out_bias_hbm,
    ln2_gain_hbm,
    ln2_bias_hbm,
    fc1_bias_hbm,
    fc2_bias_hbm,
    tokens_hbm,
    cot_seq_hbm,
    cot_prompt_hbm,
    w_qkv_hbm,
    w_out_hbm,
    w_fc1_hbm,
    w_fc2_hbm,
    layer_out_ref,
    prompt_out_ref,
    input_grad_ref,
    prompt_grad_ref,
    penalty_ref,
    prompts_ref,
    keep_ref,
    counts_ref,
    ln1_gain_ref,
    ln1_bias_ref,
    q_bias_ref,
    v_bias_ref,
    out_bias_ref,
    ln2_gain_ref,
    ln2_bias_ref,
    fc1_bias_ref,
    fc2_bias_ref,
    w_qkv,
    w_out,
    w_fc1,
    w_fc2,
    cot_low,
    prompt_low,
    seq_turn,
    cot_turn,
    prompt_turn,
    rows_s,
    cot_s,
    mask_s,
    live_s,
    unit2_s,
    scale2_s,
    normed_s,
    second_s,
    q_s,
    k_s,
    v_s,
    v_next,
    kt_s,
    kt_next,
    vt_s,
    qm_s,
    gm_s,
    soft_s,
    ds_s,
    ctx_s,
    gmt_s,
    mixed_s,
    gq_s,
    recip_s,
    half_s,
    early_s,
    act_s,
    gh_s,
    mid_s,
    gmid_s,
    grad_s,
    dqkv_s,
    sum_s,
    gmid_sum_s,
    local_sums,
    came_sums,
    line_sums,
    done_sums,
    load_sems,
    small_sems,
    send_sems,
    recv_sems,
):
    image = pl.program_id(0)
    seq, images, width = layer_out_ref.shape
    whole_rows = seq // 8 * 8
    prompt_count = prompts_ref.shape[0]
    patches = keep_ref.shape[1]
    lead = seq - patches
    head_dim = width // HEADS
    pair_dim = 2 * head_dim
    pairs = HEADS // 2
    hidden = w_fc1.shape[1]
    total = rows_s.shape[1]
    first = round_up(seq, 8)
    tail = slice(first, total)
    tail_rows = total - first
    score_scale = head_dim ** (-0.5)
    block = 32
    blocks = [slice(at, at + block) for at in range(0, total, block)]
    wide = 256
    tiles = [slice(at, at + wide) for at in range(0, width, wide)]
    coming = jnp.minimum(image + 1, images - 1)
    now2 = lax.rem(image, 2)
    other2 = 1 - now2

    lane = lax.broadcasted_iota(jnp.int32, (total, pair_dim), 1)
    low_half = lane < head_dim
    one_column = jnp.where(lane == 0, 1.0, 0.0).astype(BF16)

    loads = [
        pltpu.make_async_copy(src, dst, load_sems.at[at])
        for at, (src, dst) in enumerate(
            (
                (tokens_hbm, layer_out_ref),
                (w_qkv_hbm.at[:, pl.ds(0, width)], w_qkv.at[:, pl.ds(0, width)]),
                (w_qkv_hbm.at[:, pl.ds(width, width)], w_qkv.at[:, pl.ds(width, width)]),
                (w_qkv_hbm.at[:, pl.ds(2 * width, width)], w_qkv.at[:, pl.ds(2 * width, width)]),
                (cot_seq_hbm, cot_low),
                (cot_prompt_hbm, prompt_low),
                (w_out_hbm, w_out),
                (w_fc2_hbm, w_fc2),
                (w_fc1_hbm, w_fc1),
            )
        )
    ]
    smalls = [
        pltpu.make_async_copy(src, dst, small_sems.at[at])
        for at, (src, dst) in enumerate(
            (
                (prompts_hbm, prompts_ref),
                (keep_hbm, keep_ref),
                (counts_hbm, counts_ref),
                (ln1_gain_hbm, ln1_gain_ref),
                (ln1_bias_hbm, ln1_bias_ref),
                (q_bias_hbm, q_bias_ref),
                (v_bias_hbm, v_bias_ref),
                (out_bias_hbm, out_bias_ref),
                (ln2_gain_hbm, ln2_gain_ref),
                (ln2_bias_hbm, ln2_bias_ref),
                (fc1_bias_hbm, fc1_bias_ref),
                (fc2_bias_hbm, fc2_bias_ref),
            )
        )
    ]
    def token_rows(source, at, target, part):
        stop = min(part.stop, seq)
        if stop > part.start:
            target[part.start : stop, :] = source[part.start : stop, at, :]
        return target[part, :]

    def first_norm(at, slot, part):
        unit, _ = norm_stats(token_rows(seq_turn, at, rows_s.at[slot], part))
        normed_s[part, :] = (unit * ln1_gain_ref[...][None, :] + ln1_bias_ref[...][None, :]).astype(BF16)

    def result_cotangent(at, slot, part):
        grad = token_rows(cot_turn, at, cot_s.at[slot], part)
        low_row, high_row = max(part.start, first), min(part.stop, first + prompt_count)
        if high_row > low_row:
            cot_s[slot, low_row:high_row, :] = prompt_turn[low_row - first : high_row - first, at, :]
            grad = cot_s[slot, part, :]
        grad = jnp.where(live_s[at, part, :] > 0.0, grad, 0.0)
        cot_s[slot, part, :] = grad
        half_s[part, :] = (grad * 0.5).astype(BF16)

    some_rows = round_up(seq, 16)

    def project_query(stop):
        q_s[:stop, :] = (
            dot(normed_s[:stop, :], w_qkv[:, :width]) + q_bias_ref[...][None, :]
        ).astype(BF16) * jnp.asarray(score_scale, BF16)

    def project_key(stop):
        k_s[:stop, :] = dot(normed_s[:stop, :], w_qkv[:, width : 2 * width]).astype(BF16)
        kt_next[...] = k_s[...].T

    def project_value(stop):
        v_next[:stop, :] = (
            dot(normed_s[:stop, :], w_qkv[:, 2 * width :]) + v_bias_ref[...][None, :]
        ).astype(BF16)
        value = v_next[...]
        for head in range(HEADS):
            vt_s[head, :head_dim, :] = value[:, head * head_dim : (head + 1) * head_dim].T

    over_devices = DeviceSum(
        plane, line, streams, local_sums, came_sums, line_sums, done_sums, send_sems, recv_sems
    )

    @pl.when(image == 0)
    def _():
        loads[0].start()
        for copy in smalls:
            copy.start()
        for copy in loads[1:6]:
            copy.start()
        over_devices.greet()
        sum_s[...] = jnp.zeros_like(sum_s)
        gmid_sum_s[...] = jnp.zeros_like(gmid_sum_s)
        recip_s[...] = jnp.zeros_like(recip_s)
        for copy in smalls:
            copy.wait()
        for at in range(2):
            rows_s[at, whole_rows:, :] = jnp.zeros((total - whole_rows, width), F32)
            rows_s[at, first : first + prompt_count, :] = prompts_ref[...]
            cot_s[at, whole_rows:, :] = jnp.zeros((total - whole_rows, width), F32)
        for head in range(HEADS):
            vt_s[head, head_dim:, :] = jnp.ones((vt_s.shape[1] - head_dim, total), BF16)
        at_row = lax.broadcasted_iota(jnp.int32, (total, patches), 0)
        at_col = lax.broadcasted_iota(jnp.int32, (total, patches), 1)
        row_at = lax.broadcasted_iota(jnp.int32, (total, 1), 0)
        always = (row_at < lead) | ((row_at >= first) & (row_at < first + prompt_count))
        for at in range(images):
            keep_row = keep_ref[at : at + 1, :].astype(F32)
            patch_kept = jnp.sum(
                jnp.where(at_row == at_col + lead, keep_row, 0.0), axis=1, keepdims=True
            )
            live = always | (patch_kept > 0.0)
            live_s[at] = jnp.where(live, 1.0, 0.0)
            mask_s[at] = jnp.where((lane == 0) & jnp.logical_not(live), DEAD, 0.0).astype(BF16)
        loads[0].wait()
        for copy in loads[6:]:
            copy.start()
        seq_turn[...] = layer_out_ref[...].astype(F32)
        for part in blocks:
            first_norm(0, 0, part)
        loads[1].wait()
        project_query(total)
        loads[2].wait()
        project_key(total)
        loads[3].wait()
        for copy in loads[4:6]:
            copy.wait()
        cot_turn[...] = cot_low[...].astype(F32)
        prompt_turn[...] = prompt_low[...].astype(F32)
        project_value(total)
        for part in blocks:
            result_cotangent(0, 0, part)

    v_s[...] = v_next[...]
    kt_s[...] = kt_next[...]
    mask = mask_s[image]

    def make_queries(pair):
        q_pair = q_s[:, pair * pair_dim : (pair + 1) * pair_dim]
        qm_s[pair, :total, :] = jnp.where(low_half, q_pair, jnp.zeros_like(q_pair))
        qm_s[pair, total:, :] = jnp.where(low_half, jnp.zeros_like(q_pair), q_pair)

    def head_scores(head):
        pair, half = divmod(head, 2)
        if half == 0:
            make_queries(pair)
        keys = jnp.concatenate([k_s[:, pair * pair_dim : (pair + 1) * pair_dim], mask], axis=1)
        queries = jnp.concatenate(
            [qm_s[pair, half * total : (half + 1) * total, :], one_column], axis=1
        )
        return dot(keys, queries, NT)

    @pl.when(image == 0)
    def _():
        loads[6].wait()

    heads_a_tile = wide // head_dim

    def soften(head, scores):
        pair, half = divmod(head, 2)
        for at in range(0, total, 128):
            part = scores[:, at : at + 128]
            top = jnp.max(part, axis=0, keepdims=True)
            soft_s[pair, :, half * total + at : half * total + at + 128] = jnp.exp(
                part - top
            ).astype(BF16)

    def mix(head):
        pair, half = divmod(head, 2)
        mixed = dot(vt_s[head], soft_s[pair, :, half * total : (half + 1) * total])
        recip = 1.0 / mixed[head_dim : head_dim + 8]
        recip_s[head : head + 1, :] = recip[:1]
        mixed_s[head * head_dim : (head + 1) * head_dim, :] = mixed[:head_dim]
        ctx_s[head * head_dim : (head + 1) * head_dim, :] = (
            mixed[:head_dim].reshape(head_dim // 8, 8, total) * recip[None]
        ).reshape(head_dim, total).astype(BF16)
        if (head + 1) % heads_a_tile == 0:
            tile = tiles[head // heads_a_tile]
            before = mid_s[image] if tile.start else rows_s[now2] + out_bias_ref[...][None, :]
            mid_s[image] = before + dot(ctx_s[tile, :].T, w_out[tile, :])

    before, after = 3, 3
    waiting = [head_scores(head) for head in range(before)]
    for head in range(HEADS + after):
        if head + before < HEADS:
            waiting.append(head_scores(head + before))
        if head < HEADS:
            soften(head, waiting.pop(0))
        if head >= after:
            mix(head - after)

    @pl.when(image == 0)
    def _():
        for copy in loads[7:]:
            copy.wait()

    ahead = early_s.shape[0]
    for count in range(ahead):
        early_s[count] = dot(half_s[...], w_fc2[count * wide : (count + 1) * wide, :], NT)
        share_of = -(-len(blocks) // ahead)
        for part in blocks[count * share_of : (count + 1) * share_of]:
            unit, scale = norm_stats(mid_s[image, part, :])
            unit2_s[part, :] = unit
            scale2_s[part, :] = scale
            second_s[part, :] = (
                unit * (0.5 * ln2_gain_ref[...][None, :]) + 0.5 * ln2_bias_ref[...][None, :]
            ).astype(BF16)

    second = second_s[...]
    root2 = 2.0**0.5
    for count, at in enumerate(range(0, hidden, wide)):
        cols = slice(at, at + wide)
        half_pre = dot(second, w_fc1[:, cols]) + 0.5 * fc1_bias_ref[cols][None, :]
        grad_act = early_s[count] if count < ahead else dot(half_s[...], w_fc2[cols, :], NT)
        scaled = half_pre * root2
        twice = 1.0 + lax.erf(scaled)
        act_s[image, :, cols] = (half_pre * twice).astype(BF16)
        bell = jnp.exp2(scaled * scaled * (-math.log2(math.e)))
        gh_s[:, cols] = (grad_act * (twice + scaled * bell * (2.0 / math.pi**0.5))).astype(BF16)

    per_tile = -(-len(blocks) // len(tiles))
    for count, tile in enumerate(tiles):
        grad_s[0, :, tile] = dot(gh_s[...], w_fc1[tile, :], NT)
        for part in blocks[count * per_tile : (count + 1) * per_tile]:
            if part.start < some_rows:
                first_norm(coming, other2, part)
            result_cotangent(coming, other2, part)
    def second_norm_back(part):
        gmid = cot_s[now2, part, :] + norm_back(
            grad_s[0, part, :], ln2_gain_ref[...][None, :], unit2_s[part, :], scale2_s[part, :]
        )
        gmid_s[image, part, :] = gmid
        second_s[part, :] = gmid.astype(BF16)

    for count, project in enumerate((project_query, project_key, project_value)):
        project(some_rows)
        for part in blocks[count * per_tile : (count + 1) * per_tile]:
            second_norm_back(part)
    gmid_sum_s[...] += gmid_s[image, tail, :]

    recip_t = recip_s[...].T

    def context_grads(tile):
        grad = dot(second_s[...], w_out[tile, :], NT)
        for at in range(0, wide, pair_dim):
            pair = (tile.start + at) // pair_dim
            by_total = jnp.where(
                low_half,
                recip_t[:, 2 * pair : 2 * pair + 1],
                recip_t[:, 2 * pair + 1 : 2 * pair + 2],
            )
            scaled = (grad[:, at : at + pair_dim] * by_total).astype(BF16)
            gmt_s[tile.start + at : tile.start + at + pair_dim, :] = scaled.T
            gm_s[pair, :total, :] = jnp.where(low_half, scaled, jnp.zeros_like(scaled))
            gm_s[pair, total:, :] = jnp.where(low_half, jnp.zeros_like(scaled), scaled)

    def head_grads(head):
        pair, half = divmod(head, 2)
        return dot(
            v_s[:, pair * pair_dim : (pair + 1) * pair_dim],
            gm_s[pair, half * total : (half + 1) * total, :],
            NT,
        )

    def score_grads(head, grads):
        pair, half = divmod(head, 2)
        rows = slice(head * head_dim, (head + 1) * head_dim)
        row_dot = jnp.sum(
            gmt_s[rows, :].astype(F32) * mixed_s[rows, :], axis=0, keepdims=True
        ) * recip_s[head : head + 1, :]
        for at in range(0, total, 128):
            cols = slice(half * total + at, half * total + at + 128)
            ds_s[pair % 3, :, cols] = soft_s[pair, :, cols] * (
                grads[:, at : at + 128] - row_dot[:, at : at + 128]
            ).astype(BF16)

    def head_products(head):
        pair, half = divmod(head, 2)
        rows = slice(head * head_dim, (head + 1) * head_dim)
        gq_s[rows, :] = (
            dot(kt_s[rows, :], ds_s[pair % 3, :, half * total : (half + 1) * total]) * score_scale
        ).astype(BF16)
        if half == 1:
            cols = slice(pair * pair_dim, (pair + 1) * pair_dim)
            kcols = slice(width + cols.start, width + cols.stop)
            vcols = slice(2 * width + cols.start, 2 * width + cols.stop)
            value_grad = dot(soft_s[pair], gm_s[pair])
            dqkv_s[image, :, vcols] = value_grad.astype(BF16)
            sum_s[:, vcols] += value_grad[first:]
            key_grad = dot(ds_s[pair % 3], qm_s[pair])
            dqkv_s[image, :, kcols] = key_grad.astype(BF16)
            sum_s[:, kcols] += key_grad[first:]

    context_grads(tiles[0])
    before, after = 2, 3
    waiting = [head_grads(head) for head in range(before)]
    for head in range(HEADS + after):
        if head % heads_a_tile == 0 and head // heads_a_tile + 1 < len(tiles):
            context_grads(tiles[head // heads_a_tile + 1])
        if head + before < HEADS:
            waiting.append(head_grads(head + before))
        if head < HEADS:
            score_grads(head, waiting.pop(0))
        if head >= after:
            head_products(head - after)
    query_grad = gq_s[...].T
    dqkv_s[image, :, :width] = query_grad
    sum_s[:, :width] += query_grad.astype(F32)[first:]

    @pl.when(image == images - 1)
    def _():
        last = images - 1
        sums = sum_s[...]
        high = sums.astype(BF16)
        rest = sums - high.astype(F32)
        middle = rest.astype(BF16)
        low = (rest - middle.astype(F32)).astype(BF16)
        size = sums.shape[0]
        stacked = dot(jnp.concatenate([high, middle, low], axis=0), w_qkv[...], NT)
        grad = stacked[:size] + (stacked[size : 2 * size] + stacked[2 * size :])
        unit, scale = norm_stats(rows_s[0, tail, :])
        local = gmid_sum_s[...] + norm_back(grad, ln1_gain_ref[...][None, :], unit, scale)
        kept = jnp.sum(counts_ref[...][None, :].astype(F32))
        at_row = lax.broadcasted_iota(jnp.int32, local.shape, 0)
        local = jnp.where(at_row < prompt_count, local, kept)
        share = local_sums.shape[1]
        for at in range(local_sums.shape[0]):
            low_row, high_row = min(at * share, tail_rows), min((at + 1) * share, tail_rows)
            if high_row > low_row:
                local_sums[at, : high_row - low_row, :] = local[low_row:high_row]
            if high_row - low_row < share:
                local_sums[at, high_row - low_row :, :] = jnp.zeros(
                    (share - (high_row - low_row), width), F32
                )
        over_devices.gather()
        over_devices.first()

        token_blocks = [slice(at, min(at + block, seq)) for at in range(0, seq, block)]

        def forward_out(group, tile):
            count = len(group)
            products = dot(
                act_s[group[0] : group[0] + count].reshape(count * total, hidden), w_fc2[:, tile]
            )
            for order, at in enumerate(group):
                result = products[order * total : (order + 1) * total]
                result = result + fc2_bias_ref[tile][None, :] + mid_s[at, :, tile]
                seq_turn[:, at, tile] = jnp.where(
                    live_s[at, :seq, :] > 0.0, result[:seq], seq_turn[:, at, tile]
                )
                prompt_turn[:, at, tile] = result[first : first + prompt_count]

        def normed_grads(group):
            count = len(group)
            grads = dqkv_s[group[0] : group[0] + count, :some_rows, :]
            for tile in tiles:
                grad_s[:count, :some_rows, tile] = dot(
                    grads.reshape(count * some_rows, 3 * width), w_qkv[tile, :], NT
                ).reshape(count, some_rows, wide)

        def first_norm_back(at, order, part):
            unit, scale = norm_stats(layer_out_ref[part, at, :].astype(F32))
            grad = gmid_s[at, part, :] + norm_back(
                grad_s[order, part, :], ln1_gain_ref[...][None, :], unit, scale
            )
            input_grad_ref[part, at, :] = jnp.where(
                live_s[at, part, :] > 0.0, grad, cot_turn[part, at, :]
            )

        squares = jnp.sum(prompts_ref[...] * prompts_ref[...])
        groups = [list(range(at, min(at + 2, images))) for at in range(0, images, 2)]
        spots = len(groups) * len(tiles)
        passes = {spots * 2 // 6: over_devices.second, spots * 4 // 6: over_devices.third}
        for turn_at, group in enumerate(groups):
            todo = [
                (at, order, part) for order, at in enumerate(group) for part in token_blocks
            ]
            each = -(-len(todo) // len(tiles))
            for count, tile in enumerate(tiles):
                if turn_at * len(tiles) + count in passes:
                    passes[turn_at * len(tiles) + count]()
                if count == 0:
                    normed_grads(group)
                forward_out(group, tile)
                for item in todo[count * each : (count + 1) * each]:
                    first_norm_back(*item)
        layer_out_ref[...] = seq_turn[...].astype(BF16)
        prompt_out_ref[...] = prompt_turn[...].astype(BF16)
        over_devices.finish()
        kept_row = done_sums[
            prompt_count // share, prompt_count % share : prompt_count % share + 1, :
        ]
        weight = kept_row * (1.0 / (patches * math.sqrt(all_images)))
        for at in range(done_sums.shape[0]):
            low_row, high_row = min(at * share, prompt_count), min((at + 1) * share, prompt_count)
            if high_row > low_row:
                prompt_grad_ref[low_row:high_row, :] = (
                    done_sums[at, : high_row - low_row, :]
                    + 2.0 * weight * prompts_ref[low_row:high_row, :]
                )
        penalty_ref[...] = weight[:, :1] * (squares * (1.0 / (prompt_count * width)))


def write_kernel(*refs):
    sems = refs[-1]
    count = len(refs) // 2
    copies = []
    for at in range(count):
        size = refs[at].shape[0]
        cuts = 4 if size > 100 else 1
        for cut in range(cuts):
            part = pl.ds(cut * size // cuts, (cut + 1) * size // cuts - cut * size // cuts)
            copies.append(
                pltpu.make_async_copy(
                    refs[at].at[part], refs[count + at].at[part], sems.at[at, cut]
                )
            )
    for copy in copies:
        copy.start()
    for copy in copies:
        copy.wait()


def run_layer(
    tokens,
    prompts,
    keep_mask,
    counts,
    ln1_gain,
    ln1_bias,
    w_qkv,
    q_bias,
    v_bias,
    w_out,
    out_bias,
    ln2_gain,
    ln2_bias,
    w_fc1,
    fc1_bias,
    w_fc2,
    fc2_bias,
    cot_seq,
    cot_prompt,
):
    images, seq, width = tokens.shape
    prompt_count = prompts.shape[0]
    hidden = w_fc1.shape[1]
    first = round_up(seq, 8)
    total = round_up(first + prompt_count, 128)
    tail = total - first
    head_dim = width // HEADS
    pairs = HEADS // 2
    turn = lambda array: jnp.transpose(array, (1, 0, 2))
    whole = pl.BlockSpec(memory_space=pltpu.VMEM)
    anywhere = pl.BlockSpec(memory_space=pl.ANY)
    low = lambda *shape: pltpu.VMEM(shape, BF16)
    full = lambda *shape: pltpu.VMEM(shape, F32)
    devices = lax.axis_size("batch")
    streams = lax.axis_size("stream")
    plane = 2 ** math.ceil(math.log2(devices) / 2)
    line = devices // plane
    group = plane * streams
    share = -(-tail // group)
    if share > 4:
        share = round_up(share, 8)
    layer_out, prompt_out, input_grad, prompt_grad, penalty = pl.pallas_call(
        functools.partial(layer_kernel, plane, line, streams, images * devices * streams),
        grid=(images,),
        out_shape=(
            low(seq, images, width),
            low(prompt_count, images, width),
            full(seq, images, width),
            full(prompt_count, width),
            full(1, 1),
        ),
        in_specs=[anywhere] * 19,
        out_specs=(whole,) * 5,
        scratch_shapes=[
            full(*prompts.shape),
            pltpu.VMEM(keep_mask.shape, jnp.int32),
            pltpu.VMEM(counts.shape, jnp.int32),
        ]
        + [
            full(*vector.shape)
            for vector in (
                ln1_gain,
                ln1_bias,
                q_bias,
                v_bias,
                out_bias,
                ln2_gain,
                ln2_bias,
                fc1_bias,
                fc2_bias,
            )
        ]
        + [
            low(*w_qkv.shape),
            low(*w_out.shape),
            low(*w_fc1.shape),
            low(*w_fc2.shape),
            low(seq, images, width),
            low(prompt_count, images, width),
            full(seq, images, width),
            full(seq, images, width),
            full(prompt_count, images, width),
            full(2, total, width),
            full(2, total, width),
            low(images, total, 2 * head_dim),
            full(images, total, 1),
            full(total, width),
            full(total, 1),
            low(total, width),
            low(total, width),
            low(total, width),
            low(total, width),
            low(total, width),
            low(total, width),
            low(width, total),
            low(width, total),
            low(HEADS, head_dim + 16, total),
            low(pairs, 2 * total, 2 * head_dim),
            low(pairs, 2 * total, 2 * head_dim),
            low(pairs, total, 2 * total),
            low(3, total, 2 * total),
            low(width, total),
            low(width, total),
            full(width, total),
            low(width, total),
            full(16, total),
            low(total, width),
            full(4, total, 256),
            low(images, total, hidden),
            low(total, hidden),
            full(images, total, width),
            full(images, total, width),
            full(2, total, width),
            low(images, total, 3 * width),
            full(tail, 3 * width),
            full(tail, width),
            full(group, share, width),
            full(group, share, width),
            full(line, share, width),
            full(group, share, width),
            pltpu.SemaphoreType.DMA((9,)),
            pltpu.SemaphoreType.DMA((12,)),
            pltpu.SemaphoreType.DMA((3, max(group, line))),
            pltpu.SemaphoreType.DMA((3, max(group, line))),
        ],
        compiler_params=pltpu.CompilerParams(
            vmem_limit_bytes=59 << 20, collective_id=0, has_side_effects=True
        ),
    )(
        prompts,
        keep_mask,
        counts,
        ln1_gain,
        ln1_bias,
        q_bias,
        v_bias,
        out_bias,
        ln2_gain,
        ln2_bias,
        fc1_bias,
        fc2_bias,
        turn(tokens),
        turn(cot_seq),
        turn(cot_prompt),
        w_qkv,
        w_out,
        w_fc1,
        w_fc2,
    )
    results = tuple(
        pltpu.with_memory_space_constraint(item, pltpu.VMEM)
        for item in (layer_out, prompt_out, input_grad, prompt_grad, penalty)
    )
    layer_out, prompt_out, input_grad, prompt_grad, penalty = pl.pallas_call(
        write_kernel,
        out_shape=tuple(jax.ShapeDtypeStruct(item.shape, item.dtype) for item in results),
        in_specs=[whole] * len(results),
        out_specs=(anywhere,) * len(results),
        scratch_shapes=[pltpu.SemaphoreType.DMA((len(results), 4))],
        compiler_params=pltpu.CompilerParams(vmem_limit_bytes=1 << 20),
    )(*results)
    return (
        turn(layer_out),
        turn(prompt_out),
        turn(input_grad),
        prompt_grad,
        penalty.reshape(()),
    )


def solution(mesh):
    rows = P(("batch", "stream"), None, None)
    in_specs = (
        (rows, P(), P(("batch", "stream"), None), P(("batch", "stream")))
        + (P(),) * 13
        + (rows, rows)
    )
    return jax.shard_map(
        run_layer,
        mesh=mesh,
        in_specs=in_specs,
        out_specs=(rows, rows, rows, P(), P()),
        check_vma=False,
    )
```

```python
import functools
import math

import jax
import jax.numpy as jnp
from jax import lax
from jax.experimental import pallas as pl
from jax.experimental.pallas import tpu as pltpu
from jax.sharding import PartitionSpec as P

HEADS = 12
EPSILON = 1e-06
F32 = jnp.float32
BF16 = jnp.bfloat16
MESH = pl.DeviceIdType.MESH
DEAD = -1e30

NN = (((1,), (0,)), ((), ()))
NT = (((1,), (1,)), ((), ()))


def dot(a, b, dims=NN):
    return lax.dot_general(a, b, dims, preferred_element_type=F32)


def round_up(value, step):
    return -(-value // step) * step


def norm_stats(rows_in):
    mean = jnp.mean(rows_in, axis=-1, keepdims=True)
    centered = rows_in - mean
    variance = jnp.mean(centered * centered, axis=-1, keepdims=True)
    scale = lax.rsqrt(variance + EPSILON)
    return centered * scale, scale


def norm_back(grad, gain, unit, scale):
    scaled = grad * gain
    mean = jnp.mean(scaled, axis=-1, keepdims=True)
    along = jnp.mean(scaled * unit, axis=-1, keepdims=True)
    return scale * (scaled - mean - unit * along)


class DeviceSum:
    def __init__(self, plane, line, streams, sums, came, line_sums, done, send_sems, recv_sems):
        self.group = plane * streams
        self.line = line
        batch = lax.axis_index("batch")
        stream = lax.axis_index("stream")
        self.level = batch // plane
        self.spot = lax.rem(batch, plane) * streams + stream
        self.sums, self.came, self.line_sums, self.done = sums, came, line_sums, done
        self.send_sems, self.recv_sems = send_sems, recv_sems
        self.in_plane = lambda other: (
            self.level * plane + other // streams,
            lax.rem(other, streams),
        )
        self.in_line = lambda other: (other * plane + lax.rem(batch, plane), stream)
        self.plane_peers = [lax.rem(self.spot + step, self.group) for step in range(1, self.group)]
        self.line_peers = [lax.rem(self.level + step, line) for step in range(1, line)]
        self.started = []

    def greet(self):
        barrier = pltpu.get_barrier_semaphore()
        for other in self.plane_peers:
            pl.semaphore_signal(
                barrier, inc=1, device_id=self.in_plane(other), device_id_type=MESH
            )
        for other in self.line_peers:
            pl.semaphore_signal(barrier, inc=1, device_id=self.in_line(other), device_id_type=MESH)

    def gather(self):
        pl.semaphore_wait(
            pltpu.get_barrier_semaphore(), len(self.plane_peers) + len(self.line_peers)
        )

    def copies(self, phase, peers, where, me, source, target):
        return [
            pltpu.make_async_remote_copy(
                src_ref=source(other),
                dst_ref=target(me),
                send_sem=self.send_sems.at[phase, step],
                recv_sem=self.recv_sems.at[phase, me],
                device_id=where(other),
                device_id_type=MESH,
            )
            for step, other in enumerate(peers)
        ]

    def send(self, phase, peers, where, me, source, target):
        started = self.copies(phase, peers, where, me, source, target)
        for copy in started:
            copy.start()
        self.started += started

    def receive(self, phase, peers, where, source, target):
        for step, other in enumerate(peers):
            pltpu.make_async_remote_copy(
                src_ref=source(other),
                dst_ref=target(other),
                send_sem=self.send_sems.at[phase, step],
                recv_sem=self.recv_sems.at[phase, other],
                device_id=where(other),
                device_id_type=MESH,
            ).wait_recv()

    def first(self):
        self.send(
            0,
            self.plane_peers,
            self.in_plane,
            self.spot,
            lambda other: self.sums.at[other],
            lambda me: self.came.at[me],
        )
        self.came[self.spot] = self.sums[self.spot]

    def second(self):
        self.receive(
            0,
            self.plane_peers,
            self.in_plane,
            lambda other: self.sums.at[other],
            lambda other: self.came.at[other],
        )
        part = self.came[0]
        for at in range(1, self.group):
            part = part + self.came[at]
        self.line_sums[self.level] = part
        self.send(
            1,
            self.line_peers,
            self.in_line,
            self.level,
            lambda other: self.line_sums.at[self.level],
            lambda me: self.line_sums.at[me],
        )

    def third(self):
        self.receive(
            1,
            self.line_peers,
            self.in_line,
            lambda other: self.line_sums.at[self.level],
            lambda other: self.line_sums.at[other],
        )
        whole = self.line_sums[0]
        for at in range(1, self.line):
            whole = whole + self.line_sums[at]
        self.done[self.spot] = whole
        self.send(
            2,
            self.plane_peers,
            self.in_plane,
            self.spot,
            lambda other: self.done.at[self.spot],
            lambda me: self.done.at[me],
        )

    def finish(self):
        self.receive(
            2,
            self.plane_peers,
            self.in_plane,
            lambda other: self.done.at[self.spot],
            lambda other: self.done.at[other],
        )
        for copy in self.started:
            copy.wait_send()


def layer_kernel(
    plane,
    line,
    streams,
    all_images,
    prompts_hbm,
    keep_hbm,
    counts_hbm,
    ln1_gain_hbm,
    ln1_bias_hbm,
    q_bias_hbm,
    v_bias_hbm,
    out_bias_hbm,
    ln2_gain_hbm,
    ln2_bias_hbm,
    fc1_bias_hbm,
    fc2_bias_hbm,
    tokens_hbm,
    cot_seq_hbm,
    cot_prompt_hbm,
    w_qkv_hbm,
    w_out_hbm,
    w_fc1_hbm,
    w_fc2_hbm,
    layer_out_ref,
    prompt_out_ref,
    input_grad_ref,
    prompt_grad_ref,
    penalty_ref,
    prompts_ref,
    keep_ref,
    counts_ref,
    ln1_gain_ref,
    ln1_bias_ref,
    q_bias_ref,
    v_bias_ref,
    out_bias_ref,
    ln2_gain_ref,
    ln2_bias_ref,
    fc1_bias_ref,
    fc2_bias_ref,
    w_qkv,
    w_out,
    w_fc1,
    w_fc2,
    cot_low,
    prompt_low,
    seq_turn,
    cot_turn,
    prompt_turn,
    rows_s,
    cot_s,
    mask_s,
    live_s,
    unit2_s,
    scale2_s,
    normed_s,
    second_s,
    q_s,
    k_s,
    v_s,
    v_next,
    kt_s,
    kt_next,
    vt_s,
    qm_s,
    gm_s,
    soft_s,
    ds_s,
    ctx_s,
    gmt_s,
    mixed_s,
    gq_s,
    recip_s,
    half_s,
    early_s,
    act_s,
    gh_s,
    mid_s,
    gmid_s,
    grad_s,
    dqkv_s,
    sum_s,
    gmid_sum_s,
    local_sums,
    came_sums,
    line_sums,
    done_sums,
    load_sems,
    small_sems,
    send_sems,
    recv_sems,
):
    image = pl.program_id(0)
    seq, images, width = layer_out_ref.shape
    whole_rows = seq // 8 * 8
    prompt_count = prompts_ref.shape[0]
    patches = keep_ref.shape[1]
    lead = seq - patches
    head_dim = width // HEADS
    pair_dim = 2 * head_dim
    pairs = HEADS // 2
    hidden = w_fc1.shape[1]
    total = rows_s.shape[1]
    first = round_up(seq, 8)
    tail = slice(first, total)
    tail_rows = total - first
    score_scale = head_dim ** (-0.5)
    block = 32
    blocks = [slice(at, at + block) for at in range(0, total, block)]
    wide = 256
    tiles = [slice(at, at + wide) for at in range(0, width, wide)]
    coming = jnp.minimum(image + 1, images - 1)
    now2 = lax.rem(image, 2)
    other2 = 1 - now2

    lane = lax.broadcasted_iota(jnp.int32, (total, pair_dim), 1)
    low_half = lane < head_dim
    one_column = jnp.where(lane == 0, 1.0, 0.0).astype(BF16)

    loads = [
        pltpu.make_async_copy(src, dst, load_sems.at[at])
        for at, (src, dst) in enumerate(
            (
                (tokens_hbm, layer_out_ref),
                (w_qkv_hbm.at[:, pl.ds(0, width)], w_qkv.at[:, pl.ds(0, width)]),
                (w_qkv_hbm.at[:, pl.ds(width, width)], w_qkv.at[:, pl.ds(width, width)]),
                (w_qkv_hbm.at[:, pl.ds(2 * width, width)], w_qkv.at[:, pl.ds(2 * width, width)]),
                (cot_seq_hbm, cot_low),
                (cot_prompt_hbm, prompt_low),
                (w_out_hbm, w_out),
                (w_fc2_hbm, w_fc2),
                (w_fc1_hbm, w_fc1),
            )
        )
    ]
    smalls = [
        pltpu.make_async_copy(src, dst, small_sems.at[at])
        for at, (src, dst) in enumerate(
            (
                (prompts_hbm, prompts_ref),
                (keep_hbm, keep_ref),
                (counts_hbm, counts_ref),
                (ln1_gain_hbm, ln1_gain_ref),
                (ln1_bias_hbm, ln1_bias_ref),
                (q_bias_hbm, q_bias_ref),
                (v_bias_hbm, v_bias_ref),
                (out_bias_hbm, out_bias_ref),
                (ln2_gain_hbm, ln2_gain_ref),
                (ln2_bias_hbm, ln2_bias_ref),
                (fc1_bias_hbm, fc1_bias_ref),
                (fc2_bias_hbm, fc2_bias_ref),
            )
        )
    ]
    def token_rows(source, at, target, part):
        stop = min(part.stop, seq)
        if stop > part.start:
            target[part.start : stop, :] = source[part.start : stop, at, :]
        return target[part, :]

    def first_norm(at, slot, part):
        unit, _ = norm_stats(token_rows(seq_turn, at, rows_s.at[slot], part))
        normed_s[part, :] = (unit * ln1_gain_ref[...][None, :] + ln1_bias_ref[...][None, :]).astype(BF16)

    def result_cotangent(at, slot, part):
        grad = token_rows(cot_turn, at, cot_s.at[slot], part)
        low_row, high_row = max(part.start, first), min(part.stop, first + prompt_count)
        if high_row > low_row:
            cot_s[slot, low_row:high_row, :] = prompt_turn[low_row - first : high_row - first, at, :]
            grad = cot_s[slot, part, :]
        grad = jnp.where(live_s[at, part, :] > 0.0, grad, 0.0)
        cot_s[slot, part, :] = grad
        half_s[part, :] = (grad * 0.5).astype(BF16)

    some_rows = round_up(seq, 16)

    def project_query(stop):
        q_s[:stop, :] = (
            dot(normed_s[:stop, :], w_qkv[:, :width]) + q_bias_ref[...][None, :]
        ).astype(BF16) * jnp.asarray(score_scale, BF16)

    def project_key(stop):
        k_s[:stop, :] = dot(normed_s[:stop, :], w_qkv[:, width : 2 * width]).astype(BF16)
        kt_next[...] = k_s[...].T

    def project_value(stop):
        v_next[:stop, :] = (
            dot(normed_s[:stop, :], w_qkv[:, 2 * width :]) + v_bias_ref[...][None, :]
        ).astype(BF16)
        value = v_next[...]
        for head in range(HEADS):
            vt_s[head, :head_dim, :] = value[:, head * head_dim : (head + 1) * head_dim].T

    over_devices = DeviceSum(
        plane, line, streams, local_sums, came_sums, line_sums, done_sums, send_sems, recv_sems
    )

    @pl.when(image == 0)
    def _():
        loads[0].start()
        for copy in smalls:
            copy.start()
        for copy in loads[1:6]:
            copy.start()
        over_devices.greet()
        sum_s[...] = jnp.zeros_like(sum_s)
        gmid_sum_s[...] = jnp.zeros_like(gmid_sum_s)
        recip_s[...] = jnp.zeros_like(recip_s)
        for copy in smalls:
            copy.wait()
        for at in range(2):
            rows_s[at, whole_rows:, :] = jnp.zeros((total - whole_rows, width), F32)
            rows_s[at, first : first + prompt_count, :] = prompts_ref[...]
            cot_s[at, whole_rows:, :] = jnp.zeros((total - whole_rows, width), F32)
        for head in range(HEADS):
            vt_s[head, head_dim:, :] = jnp.ones((vt_s.shape[1] - head_dim, total), BF16)
        at_row = lax.broadcasted_iota(jnp.int32, (total, patches), 0)
        at_col = lax.broadcasted_iota(jnp.int32, (total, patches), 1)
        row_at = lax.broadcasted_iota(jnp.int32, (total, 1), 0)
        always = (row_at < lead) | ((row_at >= first) & (row_at < first + prompt_count))
        for at in range(images):
            keep_row = keep_ref[at : at + 1, :].astype(F32)
            patch_kept = jnp.sum(
                jnp.where(at_row == at_col + lead, keep_row, 0.0), axis=1, keepdims=True
            )
            live = always | (patch_kept > 0.0)
            live_s[at] = jnp.where(live, 1.0, 0.0)
            mask_s[at] = jnp.where((lane == 0) & jnp.logical_not(live), DEAD, 0.0).astype(BF16)
        loads[0].wait()
        for copy in loads[6:]:
            copy.start()
        seq_turn[...] = layer_out_ref[...].astype(F32)
        for part in blocks:
            first_norm(0, 0, part)
        loads[1].wait()
        project_query(total)
        loads[2].wait()
        project_key(total)
        loads[3].wait()
        for copy in loads[4:6]:
            copy.wait()
        cot_turn[...] = cot_low[...].astype(F32)
        prompt_turn[...] = prompt_low[...].astype(F32)
        project_value(total)
        for part in blocks:
            result_cotangent(0, 0, part)

    v_s[...] = v_next[...]
    kt_s[...] = kt_next[...]
    mask = mask_s[image]

    def make_queries(pair):
        q_pair = q_s[:, pair * pair_dim : (pair + 1) * pair_dim]
        qm_s[pair, :total, :] = jnp.where(low_half, q_pair, jnp.zeros_like(q_pair))
        qm_s[pair, total:, :] = jnp.where(low_half, jnp.zeros_like(q_pair), q_pair)

    def head_scores(head):
        pair, half = divmod(head, 2)
        if half == 0:
            make_queries(pair)
        keys = jnp.concatenate([k_s[:, pair * pair_dim : (pair + 1) * pair_dim], mask], axis=1)
        queries = jnp.concatenate(
            [qm_s[pair, half * total : (half + 1) * total, :], one_column], axis=1
        )
        return dot(keys, queries, NT)

    @pl.when(image == 0)
    def _():
        loads[6].wait()

    heads_a_tile = wide // head_dim

    def soften(head, scores):
        pair, half = divmod(head, 2)
        for at in range(0, total, 128):
            part = scores[:, at : at + 128]
            top = jnp.max(part, axis=0, keepdims=True)
            soft_s[pair, :, half * total + at : half * total + at + 128] = jnp.exp(
                part - top
            ).astype(BF16)

    def mix(head):
        pair, half = divmod(head, 2)
        mixed = dot(vt_s[head], soft_s[pair, :, half * total : (half + 1) * total])
        recip = 1.0 / mixed[head_dim : head_dim + 8]
        recip_s[head : head + 1, :] = recip[:1]
        mixed_s[head * head_dim : (head + 1) * head_dim, :] = mixed[:head_dim]
        ctx_s[head * head_dim : (head + 1) * head_dim, :] = (
            mixed[:head_dim].reshape(head_dim // 8, 8, total) * recip[None]
        ).reshape(head_dim, total).astype(BF16)
        if (head + 1) % heads_a_tile == 0:
            tile = tiles[head // heads_a_tile]
            before = mid_s[image] if tile.start else rows_s[now2] + out_bias_ref[...][None, :]
            mid_s[image] = before + dot(ctx_s[tile, :].T, w_out[tile, :])

    before, after = 3, 4
    waiting = [head_scores(head) for head in range(before)]
    for head in range(HEADS + after):
        if head + before < HEADS:
            waiting.append(head_scores(head + before))
        if head < HEADS:
            soften(head, waiting.pop(0))
        if head >= after:
            mix(head - after)

    @pl.when(image == 0)
    def _():
        for copy in loads[7:]:
            copy.wait()

    ahead = early_s.shape[0]
    for count in range(ahead):
        early_s[count] = dot(half_s[...], w_fc2[count * wide : (count + 1) * wide, :], NT)
        share_of = -(-len(blocks) // ahead)
        for part in blocks[count * share_of : (count + 1) * share_of]:
            unit, scale = norm_stats(mid_s[image, part, :])
            unit2_s[part, :] = unit
            scale2_s[part, :] = scale
            second_s[part, :] = (
                unit * (0.5 * ln2_gain_ref[...][None, :]) + 0.5 * ln2_bias_ref[...][None, :]
            ).astype(BF16)

    second = second_s[...]
    root2 = 2.0**0.5
    for count, at in enumerate(range(0, hidden, wide)):
        cols = slice(at, at + wide)
        half_pre = dot(second, w_fc1[:, cols]) + 0.5 * fc1_bias_ref[cols][None, :]
        grad_act = early_s[count] if count < ahead else dot(half_s[...], w_fc2[cols, :], NT)
        scaled = half_pre * root2
        twice = 1.0 + lax.erf(scaled)
        act_s[image, :, cols] = (half_pre * twice).astype(BF16)
        bell = jnp.exp2(scaled * scaled * (-math.log2(math.e)))
        gh_s[:, cols] = (grad_act * (twice + scaled * bell * (2.0 / math.pi**0.5))).astype(BF16)

    per_tile = -(-len(blocks) // len(tiles))
    for count, tile in enumerate(tiles):
        grad_s[0, :, tile] = dot(gh_s[...], w_fc1[tile, :], NT)
        for part in blocks[count * per_tile : (count + 1) * per_tile]:
            if part.start < some_rows:
                first_norm(coming, other2, part)
            result_cotangent(coming, other2, part)
    def second_norm_back(part):
        gmid = cot_s[now2, part, :] + norm_back(
            grad_s[0, part, :], ln2_gain_ref[...][None, :], unit2_s[part, :], scale2_s[part, :]
        )
        gmid_s[image, part, :] = gmid
        second_s[part, :] = gmid.astype(BF16)

    for count, project in enumerate((project_query, project_key, project_value)):
        project(some_rows)
        for part in blocks[count * per_tile : (count + 1) * per_tile]:
            second_norm_back(part)
    gmid_sum_s[...] += gmid_s[image, tail, :]

    recip_t = recip_s[...].T

    def context_grads(tile):
        grad = dot(second_s[...], w_out[tile, :], NT)
        for at in range(0, wide, pair_dim):
            pair = (tile.start + at) // pair_dim
            by_total = jnp.where(
                low_half,
                recip_t[:, 2 * pair : 2 * pair + 1],
                recip_t[:, 2 * pair + 1 : 2 * pair + 2],
            )
            scaled = (grad[:, at : at + pair_dim] * by_total).astype(BF16)
            gmt_s[tile.start + at : tile.start + at + pair_dim, :] = scaled.T
            gm_s[pair, :total, :] = jnp.where(low_half, scaled, jnp.zeros_like(scaled))
            gm_s[pair, total:, :] = jnp.where(low_half, jnp.zeros_like(scaled), scaled)

    def head_grads(head):
        pair, half = divmod(head, 2)
        return dot(
            v_s[:, pair * pair_dim : (pair + 1) * pair_dim],
            gm_s[pair, half * total : (half + 1) * total, :],
            NT,
        )

    def score_grads(head, grads):
        pair, half = divmod(head, 2)
        rows = slice(head * head_dim, (head + 1) * head_dim)
        row_dot = jnp.sum(
            gmt_s[rows, :].astype(F32) * mixed_s[rows, :], axis=0, keepdims=True
        ) * recip_s[head : head + 1, :]
        for at in range(0, total, 128):
            cols = slice(half * total + at, half * total + at + 128)
            ds_s[pair % 3, :, cols] = soft_s[pair, :, cols] * (
                grads[:, at : at + 128] - row_dot[:, at : at + 128]
            ).astype(BF16)

    def head_products(head):
        pair, half = divmod(head, 2)
        rows = slice(head * head_dim, (head + 1) * head_dim)
        gq_s[rows, :] = (
            dot(kt_s[rows, :], ds_s[pair % 3, :, half * total : (half + 1) * total]) * score_scale
        ).astype(BF16)
        if half == 1:
            cols = slice(pair * pair_dim, (pair + 1) * pair_dim)
            kcols = slice(width + cols.start, width + cols.stop)
            vcols = slice(2 * width + cols.start, 2 * width + cols.stop)
            value_grad = dot(soft_s[pair], gm_s[pair])
            dqkv_s[image, :, vcols] = value_grad.astype(BF16)
            sum_s[:, vcols] += value_grad[first:]
            key_grad = dot(ds_s[pair % 3], qm_s[pair])
            dqkv_s[image, :, kcols] = key_grad.astype(BF16)
            sum_s[:, kcols] += key_grad[first:]

    context_grads(tiles[0])
    before, after = 2, 3
    waiting = [head_grads(head) for head in range(before)]
    for head in range(HEADS + after):
        if head % heads_a_tile == 0 and head // heads_a_tile + 1 < len(tiles):
            context_grads(tiles[head // heads_a_tile + 1])
        if head + before < HEADS:
            waiting.append(head_grads(head + before))
        if head < HEADS:
            score_grads(head, waiting.pop(0))
        if head >= after:
            head_products(head - after)
    query_grad = gq_s[...].T
    dqkv_s[image, :, :width] = query_grad
    sum_s[:, :width] += query_grad.astype(F32)[first:]

    @pl.when(image == images - 1)
    def _():
        last = images - 1
        sums = sum_s[...]
        high = sums.astype(BF16)
        rest = sums - high.astype(F32)
        middle = rest.astype(BF16)
        low = (rest - middle.astype(F32)).astype(BF16)
        size = sums.shape[0]
        stacked = dot(jnp.concatenate([high, middle, low], axis=0), w_qkv[...], NT)
        grad = stacked[:size] + (stacked[size : 2 * size] + stacked[2 * size :])
        unit, scale = norm_stats(rows_s[0, tail, :])
        local = gmid_sum_s[...] + norm_back(grad, ln1_gain_ref[...][None, :], unit, scale)
        kept = jnp.sum(counts_ref[...][None, :].astype(F32))
        at_row = lax.broadcasted_iota(jnp.int32, local.shape, 0)
        local = jnp.where(at_row < prompt_count, local, kept)
        share = local_sums.shape[1]
        for at in range(local_sums.shape[0]):
            low_row, high_row = min(at * share, tail_rows), min((at + 1) * share, tail_rows)
            if high_row > low_row:
                local_sums[at, : high_row - low_row, :] = local[low_row:high_row]
            if high_row - low_row < share:
                local_sums[at, high_row - low_row :, :] = jnp.zeros(
                    (share - (high_row - low_row), width), F32
                )
        over_devices.gather()
        over_devices.first()

        token_blocks = [slice(at, min(at + block, seq)) for at in range(0, seq, block)]

        def forward_out(group, tile):
            count = len(group)
            products = dot(
                act_s[group[0] : group[0] + count].reshape(count * total, hidden), w_fc2[:, tile]
            )
            for order, at in enumerate(group):
                result = products[order * total : (order + 1) * total]
                result = result + fc2_bias_ref[tile][None, :] + mid_s[at, :, tile]
                seq_turn[:, at, tile] = jnp.where(
                    live_s[at, :seq, :] > 0.0, result[:seq], seq_turn[:, at, tile]
                )
                prompt_turn[:, at, tile] = result[first : first + prompt_count]

        def normed_grads(group):
            count = len(group)
            grads = dqkv_s[group[0] : group[0] + count, :some_rows, :]
            for tile in tiles:
                grad_s[:count, :some_rows, tile] = dot(
                    grads.reshape(count * some_rows, 3 * width), w_qkv[tile, :], NT
                ).reshape(count, some_rows, wide)

        def first_norm_back(at, order, part):
            unit, scale = norm_stats(layer_out_ref[part, at, :].astype(F32))
            grad = gmid_s[at, part, :] + norm_back(
                grad_s[order, part, :], ln1_gain_ref[...][None, :], unit, scale
            )
            input_grad_ref[part, at, :] = jnp.where(
                live_s[at, part, :] > 0.0, grad, cot_turn[part, at, :]
            )

        squares = jnp.sum(prompts_ref[...] * prompts_ref[...])
        groups = [list(range(at, min(at + 2, images))) for at in range(0, images, 2)]
        spots = len(groups) * len(tiles)
        passes = {spots * 2 // 6: over_devices.second, spots * 4 // 6: over_devices.third}
        for turn_at, group in enumerate(groups):
            todo = [
                (at, order, part) for order, at in enumerate(group) for part in token_blocks
            ]
            each = -(-len(todo) // len(tiles))
            for count, tile in enumerate(tiles):
                if turn_at * len(tiles) + count in passes:
                    passes[turn_at * len(tiles) + count]()
                if count == 0:
                    normed_grads(group)
                forward_out(group, tile)
                for item in todo[count * each : (count + 1) * each]:
                    first_norm_back(*item)
        layer_out_ref[...] = seq_turn[...].astype(BF16)
        prompt_out_ref[...] = prompt_turn[...].astype(BF16)
        over_devices.finish()
        kept_row = done_sums[
            prompt_count // share, prompt_count % share : prompt_count % share + 1, :
        ]
        weight = kept_row * (1.0 / (patches * math.sqrt(all_images)))
        for at in range(done_sums.shape[0]):
            low_row, high_row = min(at * share, prompt_count), min((at + 1) * share, prompt_count)
            if high_row > low_row:
                prompt_grad_ref[low_row:high_row, :] = (
                    done_sums[at, : high_row - low_row, :]
                    + 2.0 * weight * prompts_ref[low_row:high_row, :]
                )
        penalty_ref[...] = weight[:, :1] * (squares * (1.0 / (prompt_count * width)))


def write_kernel(*refs):
    sems = refs[-1]
    count = len(refs) // 2
    copies = []
    for at in range(count):
        size = refs[at].shape[0]
        cuts = 4 if size > 100 else 1
        for cut in range(cuts):
            part = pl.ds(cut * size // cuts, (cut + 1) * size // cuts - cut * size // cuts)
            copies.append(
                pltpu.make_async_copy(
                    refs[at].at[part], refs[count + at].at[part], sems.at[at, cut]
                )
            )
    for copy in copies:
        copy.start()
    for copy in copies:
        copy.wait()


def run_layer(
    tokens,
    prompts,
    keep_mask,
    counts,
    ln1_gain,
    ln1_bias,
    w_qkv,
    q_bias,
    v_bias,
    w_out,
    out_bias,
    ln2_gain,
    ln2_bias,
    w_fc1,
    fc1_bias,
    w_fc2,
    fc2_bias,
    cot_seq,
    cot_prompt,
):
    images, seq, width = tokens.shape
    prompt_count = prompts.shape[0]
    hidden = w_fc1.shape[1]
    first = round_up(seq, 8)
    total = round_up(first + prompt_count, 128)
    tail = total - first
    head_dim = width // HEADS
    pairs = HEADS // 2
    turn = lambda array: jnp.transpose(array, (1, 0, 2))
    whole = pl.BlockSpec(memory_space=pltpu.VMEM)
    anywhere = pl.BlockSpec(memory_space=pl.ANY)
    low = lambda *shape: pltpu.VMEM(shape, BF16)
    full = lambda *shape: pltpu.VMEM(shape, F32)
    devices = lax.axis_size("batch")
    streams = lax.axis_size("stream")
    plane = 2 ** math.ceil(math.log2(devices) / 2)
    line = devices // plane
    group = plane * streams
    share = -(-tail // group)
    if share > 4:
        share = round_up(share, 8)
    layer_out, prompt_out, input_grad, prompt_grad, penalty = pl.pallas_call(
        functools.partial(layer_kernel, plane, line, streams, images * devices * streams),
        grid=(images,),
        out_shape=(
            low(seq, images, width),
            low(prompt_count, images, width),
            full(seq, images, width),
            full(prompt_count, width),
            full(1, 1),
        ),
        in_specs=[anywhere] * 19,
        out_specs=(whole,) * 5,
        scratch_shapes=[
            full(*prompts.shape),
            pltpu.VMEM(keep_mask.shape, jnp.int32),
            pltpu.VMEM(counts.shape, jnp.int32),
        ]
        + [
            full(*vector.shape)
            for vector in (
                ln1_gain,
                ln1_bias,
                q_bias,
                v_bias,
                out_bias,
                ln2_gain,
                ln2_bias,
                fc1_bias,
                fc2_bias,
            )
        ]
        + [
            low(*w_qkv.shape),
            low(*w_out.shape),
            low(*w_fc1.shape),
            low(*w_fc2.shape),
            low(seq, images, width),
            low(prompt_count, images, width),
            full(seq, images, width),
            full(seq, images, width),
            full(prompt_count, images, width),
            full(2, total, width),
            full(2, total, width),
            low(images, total, 2 * head_dim),
            full(images, total, 1),
            full(total, width),
            full(total, 1),
            low(total, width),
            low(total, width),
            low(total, width),
            low(total, width),
            low(total, width),
            low(total, width),
            low(width, total),
            low(width, total),
            low(HEADS, head_dim + 16, total),
            low(pairs, 2 * total, 2 * head_dim),
            low(pairs, 2 * total, 2 * head_dim),
            low(pairs, total, 2 * total),
            low(3, total, 2 * total),
            low(width, total),
            low(width, total),
            full(width, total),
            low(width, total),
            full(16, total),
            low(total, width),
            full(6, total, 256),
            low(images, total, hidden),
            low(total, hidden),
            full(images, total, width),
            full(images, total, width),
            full(2, total, width),
            low(images, total, 3 * width),
            full(tail, 3 * width),
            full(tail, width),
            full(group, share, width),
            full(group, share, width),
            full(line, share, width),
            full(group, share, width),
            pltpu.SemaphoreType.DMA((9,)),
            pltpu.SemaphoreType.DMA((12,)),
            pltpu.SemaphoreType.DMA((3, max(group, line))),
            pltpu.SemaphoreType.DMA((3, max(group, line))),
        ],
        compiler_params=pltpu.CompilerParams(
            vmem_limit_bytes=59 << 20, collective_id=0, has_side_effects=True
        ),
    )(
        prompts,
        keep_mask,
        counts,
        ln1_gain,
        ln1_bias,
        q_bias,
        v_bias,
        out_bias,
        ln2_gain,
        ln2_bias,
        fc1_bias,
        fc2_bias,
        turn(tokens),
        turn(cot_seq),
        turn(cot_prompt),
        w_qkv,
        w_out,
        w_fc1,
        w_fc2,
    )
    results = tuple(
        pltpu.with_memory_space_constraint(item, pltpu.VMEM)
        for item in (layer_out, prompt_out, input_grad, prompt_grad, penalty)
    )
    layer_out, prompt_out, input_grad, prompt_grad, penalty = pl.pallas_call(
        write_kernel,
        out_shape=tuple(jax.ShapeDtypeStruct(item.shape, item.dtype) for item in results),
        in_specs=[whole] * len(results),
        out_specs=(anywhere,) * len(results),
        scratch_shapes=[pltpu.SemaphoreType.DMA((len(results), 4))],
        compiler_params=pltpu.CompilerParams(vmem_limit_bytes=1 << 20),
    )(*results)
    return (
        turn(layer_out),
        turn(prompt_out),
        turn(input_grad),
        prompt_grad,
        penalty.reshape(()),
    )


def solution(mesh):
    rows = P(("batch", "stream"), None, None)
    in_specs = (
        (rows, P(), P(("batch", "stream"), None), P(("batch", "stream")))
        + (P(),) * 13
        + (rows, rows)
    )
    return jax.shard_map(
        run_layer,
        mesh=mesh,
        in_specs=in_specs,
        out_specs=(rows, rows, rows, P(), P()),
        check_vma=False,
    )
```
